256 devices in a mesh: blk: 64 (over z, y, core), par: 4 (over x).
Axes of the slice: x: 4, y: 4, z: 8, core: 2. Of those that a mesh axis runs over, the one named last changes fastest.
Arguments:
- potential: float32 [2048, 32, 1024], P('blk', 'par'), may hold values from 0 to 1
- fiber_angle: bfloat16 [2048, 32, 1024], P('blk', 'par'), may hold values from -3.140625 to 3.140625
- tissue: int32 [2048, 32, 1024], P('blk', 'par'), may hold values 0 or 1
- sensitivity: bfloat16 [2048, 32, 1024], P('blk', 'par'), may hold values from -6 to 6
- conductance: float32 [512], P(('blk', 'par')), may hold values from 0.5 to 1
- brick_slot: int32 [2048], replicated, may hold values from 0 to 2047, as said below
- neighbours: int32 [2048, 4], P('blk'), may hold values from 0 to 2047, as said below
- brick_cell: int32 [2048], P('blk'), may hold values from 0 to 511, as said below
Outputs:
- final_potential: float32 [2048, 32, 1024], P('blk', 'par')
- potential_gradient: float32 [2048, 32, 1024], P('blk', 'par')
- cell_gradient: float32 [512], P(('blk', 'par'))
The draws below stay inside these ranges and needn't reach their ends.
Inputs may be any that keep to these rules, and one draw needn't show every extreme that they name: brick_slot is a permutation: slot s lies on blk index s // 32. The relation is symmetric: if brick c is beside brick a across x high, a is beside c across x low, and likewise for y. A brick's neighbours always lie on other blk indices. For any two blk indices, exactly 0 or exactly 4 faces of the bricks of the first have their neighbour on the second. `brick_cell`: every parameter cell holds exactly 4 bricks.
All inputs are finite; a program needn't handle non-finite values. No bound on the sum of `tissue` on one device may be relied on, other than what follows from the above.
Results may differ from the reference program's by a relative error of at most 0.0003.
Values sent between devices are 32-bit elements; how exact they have to be, the bound alone decides.
A program may use at most 128 MiB of HBM per device.

```python
import math
import jax
import jax.numpy as jnp

BX = 32
BD = 32
STEPS = 1
CELL_BRICKS = 4
BRICKS = 2048
PCELLS = 512
N_BLK = 64


def brick_graph(key):
    graph_key = jax.random.fold_in(key, 1234)
    key_order_x, key_order_y, key_start_x, key_start_y, key_relabel, key_offset = jax.random.split(graph_key, 6)
    halfway = N_BLK // 2
    positions_in = jnp.arange(BD, dtype=jnp.int32)
    pair_index = positions_in // 2 % (halfway // 2)
    member = positions_in % 2
    step_index = jnp.where(member == 0, pair_index, halfway - 1 - pair_index)
    odd_steps = 2 * step_index + 1
    steps_x = odd_steps[jax.random.permutation(key_order_x, BD)]
    steps_y = odd_steps[jax.random.permutation(key_order_y, BD)]
    start_x = jax.random.randint(key_start_x, (), 0, N_BLK)
    start_y = jax.random.randint(key_start_y, (), 0, N_BLK)
    relabel = jax.random.permutation(key_relabel, N_BLK).astype(jnp.int32)
    offset_y = jax.random.randint(key_offset, (N_BLK,), 0, BD)
    visits = jnp.arange(N_BLK, dtype=jnp.int32)
    blocks_in = jnp.arange(BD, dtype=jnp.int32)
    device_x = relabel[(start_x + visits[None, :] * steps_x[:, None]) % N_BLK]
    slot_x = (device_x * BD + blocks_in[:, None]).reshape(-1)
    device_y = relabel[(start_y + visits[None, :] * steps_y[:, None]) % N_BLK]
    slot_y = (device_y * BD + (blocks_in[:, None] + offset_y[device_y]) % BD).reshape(-1)
    positions = jnp.arange(BRICKS, dtype=jnp.int32)
    global_id = jnp.zeros((BRICKS,), jnp.int32).at[slot_x].set(positions)
    lower_x = (global_id - 1) % BRICKS
    upper_x = (global_id + 1) % BRICKS
    lower_y = jnp.zeros((BRICKS,), jnp.int32).at[slot_y].set(global_id[jnp.roll(slot_y, 1)])
    upper_y = jnp.zeros((BRICKS,), jnp.int32).at[slot_y].set(global_id[jnp.roll(slot_y, -1)])
    linked = jnp.stack([lower_x, upper_x, lower_y, upper_y], axis=1)
    return (slot_x, linked, global_id)


def draw_brick_slot(key, part):
    return brick_graph(key)[0]


def draw_neighbours(key, part):
    return brick_graph(key)[1]


def draw_brick_cell(key, part):
    return brick_graph(key)[2] // CELL_BRICKS


def with_ends(result, own_key, least, largest):
    longest = result.shape.index(max(result.shape))
    spots = []
    for shift in (0, 1):
        where = [jax.random.randint(jax.random.fold_in(own_key, axis), (), 0, length) for axis, length in enumerate(result.shape)]
        where[longest] = (where[longest] + shift) % result.shape[longest]
        spots.append(tuple(where))
    return result.at[spots[0]].set(least).at[spots[1]].set(largest)


def steps_of(own_key, dims, cuts, low, top_value):
    level = 1.0
    for dim, blocks in cuts:
        steps = jax.random.uniform(jax.random.fold_in(jax.random.fold_in(own_key, 6), dim), (blocks,), jnp.float32, low / len(cuts), top_value / len(cuts))
        level = level * jnp.repeat(jnp.exp(steps), dims[dim] // blocks).reshape((-1,) + (1,) * (len(dims) - 1 - dim))
    return level


def centred(stream_key, shape, deviation, reach, cuts=(), kind=jnp.bfloat16):
    gain = steps_of(stream_key, shape, cuts, -0.22, 0.18) if cuts else 1.0
    values = jax.random.normal(stream_key, shape, jnp.float32) * deviation * gain
    return jnp.minimum(jnp.maximum(values, -reach), reach).astype(kind)


def setup_inputs(seed: int = 0) -> dict:
    streams_of = jax.random.split(jax.random.key(seed), 9)
    potential = jnp.clip(1.0 * jax.random.uniform(streams_of[0], (BRICKS, BX, BX * BX), jnp.float32) ** steps_of(streams_of[0], (BRICKS, BX, BX * BX), ((0, 64), (1, 4)), -0.2, 0.2), 0.0, 1.0)
    fiber_angle = jnp.clip(jax.random.uniform(streams_of[1], (BRICKS, BX, BX * BX), jnp.float32, -3.140625, 3.140625), -3.140625, 3.140625).astype(jnp.bfloat16)
    tissue = with_ends((jax.random.randint(streams_of[2], (BRICKS, BX, BX * BX), 0, 8) < 7).astype(jnp.int32), jax.random.fold_in(streams_of[2], 1), 0, 1)
    sensitivity = centred(streams_of[3], (BRICKS, BX, BX * BX), 1.0, 6.0, ((0, 64), (1, 4)))
    conductance = jnp.clip(jnp.exp(math.log(1.0) - 0.6931472 * jax.random.uniform(streams_of[4], (PCELLS,), jnp.float32) ** steps_of(streams_of[4], (PCELLS,), ((0, 256),), -0.2, 0.2)), 0.5, 1.0)
    brick_slot = draw_brick_slot(jax.random.fold_in(streams_of[8], 71), 0)
    neighbours = draw_neighbours(jax.random.fold_in(streams_of[8], 71), 0)
    brick_cell = draw_brick_cell(jax.random.fold_in(streams_of[8], 71), 0)
    return {"potential": potential, "fiber_angle": fiber_angle, "tissue": tissue, "sensitivity": sensitivity, "conductance": conductance, "brick_slot": brick_slot, "neighbours": neighbours, "brick_cell": brick_cell}


TIMESTEP = 0.12
THRESHOLD = 0.2
ACROSS = 0.3
ALONG = 1.0
VERTICAL = 0.6


def layers(values, brick_edge):
    return jnp.stack([values[..., :brick_edge], values[..., -brick_edge:], values[..., 0::brick_edge], values[..., brick_edge - 1::brick_edge]], axis=1)


def along_x(values, lower_face, upper_face, brick_edge):
    return (jnp.concatenate([lower_face, values[..., :-brick_edge]], -1), jnp.concatenate([values[..., brick_edge:], upper_face], -1))


def along_y(values, lower_face, upper_face, brick_edge):
    y_index = jnp.arange(values.shape[-1]) % brick_edge
    zero_pad = jnp.zeros(values.shape[:-1] + (1,), values.dtype)
    shifted_down = jnp.concatenate([zero_pad, values[..., :-1]], -1)
    shifted_up = jnp.concatenate([values[..., 1:], zero_pad], -1)
    return (jnp.where(y_index == 0, jnp.repeat(lower_face, brick_edge, axis=-1), shifted_down),
            jnp.where(y_index == brick_edge - 1, jnp.repeat(upper_face, brick_edge, axis=-1), shifted_up))


def near_values(values, layer_set, padded, brick_edge):
    x_low, x_high = along_x(values, layer_set[:, 0], layer_set[:, 1], brick_edge)
    y_low, y_high = along_y(values, layer_set[:, 2], layer_set[:, 3], brick_edge)
    return (x_low, x_high, y_low, y_high, padded[:, :-2], padded[:, 2:])


def laplace(conduct, values, beside):
    summed = conduct[0] * (beside[0] - values)
    for facet in range(1, 6):
        summed = summed + conduct[facet] * (beside[facet] - values)
    return summed


def brick_terms(conduct, adjoint, beside_adjoint, earlier, beside_state):
    summed = -conduct[0] * (adjoint - beside_adjoint[0]) * (earlier - beside_state[0])
    for facet in range(1, 6):
        summed = summed - conduct[facet] * (adjoint - beside_adjoint[facet]) * (earlier - beside_state[facet])
    return jnp.sum(summed, axis=(1, 2))


def weights(tissue, fiber_angle, brick_scale):
    present = tissue.astype(jnp.float32)
    cos_square = jnp.cos(fiber_angle.astype(jnp.float32)) ** 2
    weight_x = present * brick_scale * (ACROSS + (ALONG - ACROSS) * cos_square)
    weight_y = present * brick_scale * (ACROSS + (ALONG - ACROSS) * (1.0 - cos_square))
    weight_z = present * brick_scale * VERTICAL
    return weight_x, weight_y, weight_z


def conductances(weight_x, weight_y, weight_z, weight_near, padded_z, brick_edge):
    x_low, x_high = along_x(weight_x, weight_near[:, 0], weight_near[:, 1], brick_edge)
    y_low, y_high = along_y(weight_y, weight_near[:, 2], weight_near[:, 3], brick_edge)
    return (weight_x * x_low, weight_x * x_high, weight_y * y_low, weight_y * y_high,
            weight_z * padded_z[:, :-2], weight_z * padded_z[:, 2:])


def reference(potential, fiber_angle, tissue, sensitivity, conductance, brick_slot, neighbours, brick_cell):
    brick_edge = BX
    opposite = jnp.array([1, 0, 3, 2], jnp.int32)
    near_slot = brick_slot[neighbours]

    def remote(values):
        return layers(values, brick_edge)[near_slot, opposite[None, :]]

    def pad_z(values):
        return jnp.pad(values, ((0, 0), (1, 1), (0, 0)))

    brick_scale = conductance[brick_cell][:, None, None]
    weight_x, weight_y, weight_z = weights(tissue, fiber_angle, brick_scale)
    weight_layers = jnp.concatenate([layers(weight_x, brick_edge)[:, :2], layers(weight_y, brick_edge)[:, 2:]], axis=1)
    conduct = conductances(weight_x, weight_y, weight_z, weight_layers[near_slot, opposite[None, :]], pad_z(weight_z), brick_edge)
    current = potential
    stored = []
    for section in range(STEPS):
        stored.append(current)
        beside = near_values(current, remote(current), pad_z(current), brick_edge)
        ionic_term = current * (1.0 - current) * (current - THRESHOLD)
        current = current + TIMESTEP * (laplace(conduct, current, beside) + ionic_term)
    adjoint = sensitivity.astype(jnp.float32)
    brick_total = jnp.zeros((potential.shape[0],), jnp.float32)
    for section in reversed(range(STEPS)):
        earlier = stored[section]
        beside_state = near_values(earlier, remote(earlier), pad_z(earlier), brick_edge)
        beside_adjoint = near_values(adjoint, remote(adjoint), pad_z(adjoint), brick_edge)
        brick_total = brick_total + brick_terms(conduct, adjoint, beside_adjoint, earlier, beside_state)
        ionic_slope = -3.0 * earlier * earlier + 2.0 * (1.0 + THRESHOLD) * earlier - THRESHOLD
        adjoint = adjoint + TIMESTEP * (laplace(conduct, adjoint, beside_adjoint) + ionic_slope * adjoint)
    cell_total = jax.ops.segment_sum(brick_total, brick_cell, num_segments=PCELLS)
    cell_gradient = TIMESTEP * cell_total / (conductance * float(BX) ** 1.5)
    return current, adjoint, cell_gradient
```

```python
import jax
import jax.numpy as jnp
from jax import lax
from jax.sharding import PartitionSpec as P

BX = 32
STEPS = 1


TIMESTEP = 0.12
THRESHOLD = 0.2
ACROSS = 0.3
ALONG = 1.0
VERTICAL = 0.6


def extended(x, sides, width):
    for axis, dim in sides:
        size, length = (lax.axis_size(axis), x.shape[dim])
        up = [(i, (i + 1) % size) for i in range(size - 1)]
        down = [(j, i) for i, j in up]
        last = lax.slice_in_dim(x, length - width, length, axis=dim)
        initial = lax.slice_in_dim(x, 0, width, axis=dim)
        before = lax.ppermute(last, axis, up)
        after = lax.ppermute(initial, axis, down)
        x = jnp.concatenate([before, x, after], axis=dim)
    return x


def layers(values, brick_edge):
    return jnp.stack(
        [
            values[..., :brick_edge],
            values[..., -brick_edge:],
            values[..., 0::brick_edge],
            values[..., brick_edge - 1 :: brick_edge],
        ],
        axis=1,
    )


def along_x(values, lower_face, upper_face, brick_edge):
    return (
        jnp.concatenate([lower_face, values[..., :-brick_edge]], -1),
        jnp.concatenate([values[..., brick_edge:], upper_face], -1),
    )


def along_y(values, lower_face, upper_face, brick_edge):
    y_index = jnp.arange(values.shape[-1]) % brick_edge
    zero_pad = jnp.zeros(values.shape[:-1] + (1,), values.dtype)
    shifted_down = jnp.concatenate([zero_pad, values[..., :-1]], -1)
    shifted_up = jnp.concatenate([values[..., 1:], zero_pad], -1)
    return (
        jnp.where(y_index == 0, jnp.repeat(lower_face, brick_edge, axis=-1), shifted_down),
        jnp.where(
            y_index == brick_edge - 1, jnp.repeat(upper_face, brick_edge, axis=-1), shifted_up
        ),
    )


def near_values(values, layer_set, padded, brick_edge):
    x_low, x_high = along_x(values, layer_set[:, 0], layer_set[:, 1], brick_edge)
    y_low, y_high = along_y(values, layer_set[:, 2], layer_set[:, 3], brick_edge)
    return (x_low, x_high, y_low, y_high, padded[:, :-2], padded[:, 2:])


def laplace(conduct, values, beside):
    summed = conduct[0] * (beside[0] - values)
    for facet in range(1, 6):
        summed = summed + conduct[facet] * (beside[facet] - values)
    return summed


def brick_terms(conduct, adjoint, beside_adjoint, earlier, beside_state):
    summed = -conduct[0] * (adjoint - beside_adjoint[0]) * (earlier - beside_state[0])
    for facet in range(1, 6):
        summed = summed - conduct[facet] * (adjoint - beside_adjoint[facet]) * (
            earlier - beside_state[facet]
        )
    return jnp.sum(summed, axis=(1, 2))


def weights(tissue, fiber_angle, brick_scale):
    present = tissue.astype(jnp.float32)
    cos_square = jnp.cos(fiber_angle.astype(jnp.float32)) ** 2
    weight_x = present * brick_scale * (ACROSS + (ALONG - ACROSS) * cos_square)
    weight_y = present * brick_scale * (ACROSS + (ALONG - ACROSS) * (1.0 - cos_square))
    weight_z = present * brick_scale * VERTICAL
    return (weight_x, weight_y, weight_z)


def conductances(weight_x, weight_y, weight_z, weight_near, padded_z, brick_edge):
    x_low, x_high = along_x(weight_x, weight_near[:, 0], weight_near[:, 1], brick_edge)
    y_low, y_high = along_y(weight_y, weight_near[:, 2], weight_near[:, 3], brick_edge)
    return (
        weight_x * x_low,
        weight_x * x_high,
        weight_y * y_low,
        weight_y * y_high,
        weight_z * padded_z[:, :-2],
        weight_z * padded_z[:, 2:],
    )


def z_extended(fields, axis):
    size = lax.axis_size(axis)
    up = [(i, (i + 1) % size) for i in range(size - 1)]
    down = [(j, i) for i, j in up]
    last = jnp.stack([f[:, -1:] for f in fields])
    initial = jnp.stack([f[:, :1] for f in fields])
    before = lax.ppermute(last, axis, up)
    after = lax.ppermute(initial, axis, down)
    return [jnp.concatenate([before[k], f, after[k]], axis=1) for k, f in enumerate(fields)]


def body(
    potential, fiber_angle, tissue, sensitivity, conductance, brick_slot, neighbours, brick_cell
):
    bricks, z_layers, plane_cells = potential.shape
    brick_edge = BX
    blocks = lax.axis_size("blk")
    parts = lax.axis_size("par")
    devices = blocks * parts
    capacity = max(4, 8 * bricks // blocks)
    face_count = 4 * bricks
    face_cells = z_layers * brick_edge
    own_cells = conductance.shape[0]
    cell_count = own_cells * devices
    opposite = jnp.array([1, 0, 3, 2], jnp.int32)

    row = jnp.concatenate([conductance, brick_cell.astype(jnp.float32)])
    table = lax.all_to_all(
        jnp.broadcast_to(row[None], (devices, row.shape[0])),
        ("blk", "par"),
        split_axis=0,
        concat_axis=0,
        tiled=True,
    )
    cond_all = table[:, :own_cells].reshape(-1)
    cell_all = table[::parts, own_cells:].reshape(-1).astype(jnp.int32)

    near_slot = brick_slot[neighbours]
    near_blk = (near_slot // bricks).reshape(-1)
    far_key = (near_slot % bricks * 4 + opposite[None, :]).reshape(-1)
    own_key = jnp.arange(face_count, dtype=jnp.int32)
    matches = near_blk[:, None] == near_blk[None, :]
    send_rank = jnp.sum((matches & (own_key[None, :] < own_key[:, None])).astype(jnp.int32), axis=1)
    recv_rank = jnp.sum((matches & (far_key[None, :] < far_key[:, None])).astype(jnp.int32), axis=1)
    send_slot = near_blk * capacity + send_rank
    recv_slot = near_blk * capacity + recv_rank

    present = tissue.astype(jnp.float32)
    cos_square = jnp.cos(fiber_angle.astype(jnp.float32)) ** 2
    factor_x = ACROSS + (ALONG - ACROSS) * cos_square
    factor_y = ACROSS + (ALONG - ACROSS) * (1.0 - cos_square)
    current = potential
    adjoint = sensitivity.astype(jnp.float32)

    face_weight = jnp.concatenate(
        [layers(present * factor_x, brick_edge)[:, :2], layers(present * factor_y, brick_edge)[:, 2:]],
        axis=1,
    )
    fields = jnp.stack([face_weight, layers(current, brick_edge), layers(adjoint, brick_edge)], axis=2)
    flattened = fields.reshape(face_count, 3 * face_cells)
    outgoing = jnp.zeros((blocks * capacity, 3 * face_cells), jnp.float32).at[send_slot].set(flattened)
    received = lax.all_to_all(
        outgoing.reshape(blocks, capacity, 3 * face_cells), "blk", split_axis=0, concat_axis=0, tiled=True
    )
    near = received.reshape(blocks * capacity, 3, z_layers, brick_edge)[recv_slot].reshape(
        bricks, 4, 3, z_layers, brick_edge
    )
    present_padded, state_padded, adjoint_padded = z_extended([present, current, adjoint], "par")

    theta = cond_all[brick_cell]
    theta_near = cond_all[cell_all[near_slot]]
    brick_scale = theta[:, None, None]
    scaled = present * brick_scale
    weight_x = scaled * factor_x
    weight_y = scaled * factor_y
    weight_z = scaled * VERTICAL
    weight_near = theta_near[:, :, None, None] * near[:, :, 0]
    padded_weight = present_padded * brick_scale * VERTICAL
    conduct = conductances(weight_x, weight_y, weight_z, weight_near, padded_weight, brick_edge)

    state_near = near[:, :, 1]
    adjoint_near = near[:, :, 2]
    beside_state = near_values(current, state_near, state_padded, brick_edge)
    beside_adjoint = near_values(adjoint, adjoint_near, adjoint_padded, brick_edge)
    brick_part = brick_terms(conduct, adjoint, beside_adjoint, current, beside_state)
    onehot_cells = brick_cell[:, None] == jnp.arange(cell_count, dtype=jnp.int32)[None, :]
    shares = jnp.sum(jnp.where(onehot_cells, brick_part[:, None], 0.0), axis=0)
    grad_share = jnp.sum(
        lax.all_to_all(
            shares.reshape(devices, own_cells), ("blk", "par"), split_axis=0, concat_axis=0, tiled=True
        ),
        axis=0,
    )
    ionic_term = current * (1.0 - current) * (current - THRESHOLD)
    final = current + TIMESTEP * (laplace(conduct, current, beside_state) + ionic_term)
    ionic_slope = -3.0 * current * current + 2.0 * (1.0 + THRESHOLD) * current - THRESHOLD
    adjoint = adjoint + TIMESTEP * (laplace(conduct, adjoint, beside_adjoint) + ionic_slope * adjoint)
    cell_gradient = TIMESTEP * grad_share / (conductance * float(BX) ** 1.5)
    return (final, adjoint, cell_gradient)


def solution(mesh):
    placed = (
        P("blk", "par", None),
        P("blk", "par", None),
        P("blk", "par", None),
        P("blk", "par", None),
        P(("blk", "par")),
        P(),
        P("blk", None),
        P("blk"),
    )
    return jax.shard_map(
        body,
        mesh=mesh,
        in_specs=placed,
        out_specs=(P("blk", "par", None), P("blk", "par", None), P(("blk", "par"))),
        check_vma=False,
    )
```

```python
import jax
import jax.numpy as jnp
from jax import lax
from jax.sharding import PartitionSpec as P
from jax.experimental import pallas as pl
from jax.experimental.pallas import tpu as pltpu

BX = 32
STEPS = 1


TIMESTEP = 0.12
THRESHOLD = 0.2
ACROSS = 0.3
ALONG = 1.0
VERTICAL = 0.6


def extended(x, sides, width):
    for axis, dim in sides:
        size, length = (lax.axis_size(axis), x.shape[dim])
        up = [(i, (i + 1) % size) for i in range(size - 1)]
        down = [(j, i) for i, j in up]
        last = lax.slice_in_dim(x, length - width, length, axis=dim)
        initial = lax.slice_in_dim(x, 0, width, axis=dim)
        before = lax.ppermute(last, axis, up)
        after = lax.ppermute(initial, axis, down)
        x = jnp.concatenate([before, x, after], axis=dim)
    return x


def layers(values, brick_edge):
    return jnp.stack(
        [
            values[..., :brick_edge],
            values[..., -brick_edge:],
            values[..., 0::brick_edge],
            values[..., brick_edge - 1 :: brick_edge],
        ],
        axis=1,
    )


def along_x(values, lower_face, upper_face, brick_edge):
    return (
        jnp.concatenate([lower_face, values[..., :-brick_edge]], -1),
        jnp.concatenate([values[..., brick_edge:], upper_face], -1),
    )


def along_y(values, lower_face, upper_face, brick_edge):
    y_index = jnp.arange(values.shape[-1]) % brick_edge
    zero_pad = jnp.zeros(values.shape[:-1] + (1,), values.dtype)
    shifted_down = jnp.concatenate([zero_pad, values[..., :-1]], -1)
    shifted_up = jnp.concatenate([values[..., 1:], zero_pad], -1)
    return (
        jnp.where(y_index == 0, jnp.repeat(lower_face, brick_edge, axis=-1), shifted_down),
        jnp.where(
            y_index == brick_edge - 1, jnp.repeat(upper_face, brick_edge, axis=-1), shifted_up
        ),
    )


def near_values(values, layer_set, padded, brick_edge):
    x_low, x_high = along_x(values, layer_set[:, 0], layer_set[:, 1], brick_edge)
    y_low, y_high = along_y(values, layer_set[:, 2], layer_set[:, 3], brick_edge)
    return (x_low, x_high, y_low, y_high, padded[:, :-2], padded[:, 2:])


def laplace(conduct, values, beside):
    summed = conduct[0] * (beside[0] - values)
    for facet in range(1, 6):
        summed = summed + conduct[facet] * (beside[facet] - values)
    return summed


def brick_terms(conduct, adjoint, beside_adjoint, earlier, beside_state):
    summed = -conduct[0] * (adjoint - beside_adjoint[0]) * (earlier - beside_state[0])
    for facet in range(1, 6):
        summed = summed - conduct[facet] * (adjoint - beside_adjoint[facet]) * (
            earlier - beside_state[facet]
        )
    return jnp.sum(summed, axis=(1, 2))


def weights(tissue, fiber_angle, brick_scale):
    present = tissue.astype(jnp.float32)
    cos_square = jnp.cos(fiber_angle.astype(jnp.float32)) ** 2
    weight_x = present * brick_scale * (ACROSS + (ALONG - ACROSS) * cos_square)
    weight_y = present * brick_scale * (ACROSS + (ALONG - ACROSS) * (1.0 - cos_square))
    weight_z = present * brick_scale * VERTICAL
    return (weight_x, weight_y, weight_z)


def conductances(weight_x, weight_y, weight_z, weight_near, padded_z, brick_edge):
    x_low, x_high = along_x(weight_x, weight_near[:, 0], weight_near[:, 1], brick_edge)
    y_low, y_high = along_y(weight_y, weight_near[:, 2], weight_near[:, 3], brick_edge)
    return (
        weight_x * x_low,
        weight_x * x_high,
        weight_y * y_low,
        weight_y * y_high,
        weight_z * padded_z[:, :-2],
        weight_z * padded_z[:, 2:],
    )


GROUP = 8


def expanders(edge, cells):
    lane = jnp.arange(cells, dtype=jnp.int32)[None, :]
    k = jnp.arange(edge, dtype=jnp.int32)[:, None]
    return jnp.stack(
        [lane == k, lane == cells - edge + k, lane == edge * k, lane == edge * k + edge - 1]
    ).astype(jnp.float32)


def cell_kernel(scale_ref, expand_ref, tissue_ref, angle_ref, u_ref, l_ref, face_ref, halo_ref,
                u_out, l_out, part_out):
    g = pl.program_id(0)
    nz, cells = u_ref.shape[1], u_ref.shape[2]
    edge = face_ref.shape[-1]
    lane = lax.broadcasted_iota(jnp.int32, (nz, cells), 1)
    row = lax.broadcasted_iota(jnp.int32, (nz, cells), 0)
    ycoord = lane % edge
    masks = (lane < edge, lane >= cells - edge, ycoord == 0, ycoord == edge - 1)
    shifts = (edge, cells - edge, 1, cells - 1)
    zlo = row == 0
    zhi = row == nz - 1

    def one(i, carry):
        b = g * GROUP + i
        th = scale_ref[b, 0]
        present = tissue_ref[i].astype(jnp.float32)
        c = jnp.cos(angle_ref[i].astype(jnp.float32))
        c2 = c * c
        scaled = present * th
        wx = scaled * (ACROSS + (ALONG - ACROSS) * c2)
        wy = scaled * (ACROSS + (ALONG - ACROSS) * (1.0 - c2))
        wz = scaled * VERTICAL
        u = u_ref[i]
        l = l_ref[i].astype(jnp.float32)
        halo = halo_ref[i]
        conds, ub, lb = [], [], []
        for f in range(4):
            ext = jnp.dot(face_ref[i, f], expand_ref[f], precision=lax.Precision.HIGHEST,
                          preferred_element_type=jnp.float32)
            w_self = wx if f < 2 else wy
            w_near = jnp.where(masks[f], scale_ref[b, 1 + f] * ext[:nz], pltpu.roll(w_self, shifts[f], 1))
            conds.append(w_self * w_near)
            ub.append(jnp.where(masks[f], ext[nz:2 * nz], pltpu.roll(u, shifts[f], 1)))
            lb.append(jnp.where(masks[f], ext[2 * nz:], pltpu.roll(l, shifts[f], 1)))
        wz_lo = jnp.where(zlo, (halo[0:1] * th) * VERTICAL, pltpu.roll(wz, 1, 0))
        wz_hi = jnp.where(zhi, (halo[3:4] * th) * VERTICAL, pltpu.roll(wz, nz - 1, 0))
        conds += [wz * wz_lo, wz * wz_hi]
        ub += [jnp.where(zlo, halo[1:2], pltpu.roll(u, 1, 0)), jnp.where(zhi, halo[4:5], pltpu.roll(u, nz - 1, 0))]
        lb += [jnp.where(zlo, halo[2:3], pltpu.roll(l, 1, 0)), jnp.where(zhi, halo[5:6], pltpu.roll(l, nz - 1, 0))]
        lap_u = conds[0] * (ub[0] - u)
        lap_l = conds[0] * (lb[0] - l)
        terms = -conds[0] * (l - lb[0]) * (u - ub[0])
        for k in range(1, 6):
            lap_u = lap_u + conds[k] * (ub[k] - u)
            lap_l = lap_l + conds[k] * (lb[k] - l)
            terms = terms - conds[k] * (l - lb[k]) * (u - ub[k])
        ionic = u * (1.0 - u) * (u - THRESHOLD)
        slope = -3.0 * u * u + 2.0 * (1.0 + THRESHOLD) * u - THRESHOLD
        u_out[i] = u + TIMESTEP * (lap_u + ionic)
        l_out[i] = l + TIMESTEP * (lap_l + slope * l)
        col = jnp.sum(terms, axis=0, keepdims=True)
        acc = col[:, 0:128]
        for t in range(1, cells // 128):
            acc = acc + col[:, t * 128:(t + 1) * 128]
        part_out[i] = acc
        return carry

    lax.fori_loop(0, GROUP, one, 0)


def cell_step(scales, tissue, angle, potential, sensitivity, faces, halos, interpret=False):
    bricks, nz, cells = potential.shape
    edge = faces.shape[-1]
    expand = expanders(edge, cells)
    blk3 = lambda: pl.BlockSpec((GROUP, nz, cells), lambda g: (g, 0, 0))
    return pl.pallas_call(
        cell_kernel,
        grid=(bricks // GROUP,),
        in_specs=[
            pl.BlockSpec(memory_space=pltpu.SMEM),
            pl.BlockSpec((4, edge, cells), lambda g: (0, 0, 0)),
            blk3(), blk3(), blk3(), blk3(),
            pl.BlockSpec((GROUP, 4, 3 * nz, edge), lambda g: (g, 0, 0, 0)),
            pl.BlockSpec((GROUP, 6, cells), lambda g: (g, 0, 0)),
        ],
        out_specs=[blk3(), blk3(), pl.BlockSpec((GROUP, 1, 128), lambda g: (g, 0, 0))],
        out_shape=[
            jax.ShapeDtypeStruct((bricks, nz, cells), jnp.float32),
            jax.ShapeDtypeStruct((bricks, nz, cells), jnp.float32),
            jax.ShapeDtypeStruct((bricks, 1, 128), jnp.float32),
        ],
        compiler_params=pltpu.CompilerParams(dimension_semantics=("parallel",)),
        interpret=interpret,
    )(scales, expand, tissue, angle, potential, sensitivity, faces, halos)


def body(
    potential, fiber_angle, tissue, sensitivity, conductance, brick_slot, neighbours, brick_cell
):
    bricks, z_layers, plane_cells = potential.shape
    brick_edge = BX
    blocks = lax.axis_size("blk")
    parts = lax.axis_size("par")
    devices = blocks * parts
    capacity = max(4, 8 * bricks // blocks)
    face_count = 4 * bricks
    face_cells = z_layers * brick_edge
    own_cells = conductance.shape[0]
    cell_count = own_cells * devices
    opposite = jnp.array([1, 0, 3, 2], jnp.int32)

    row = jnp.concatenate([conductance, brick_cell.astype(jnp.float32)])
    table = lax.all_to_all(
        jnp.broadcast_to(row[None], (devices, row.shape[0])),
        ("blk", "par"),
        split_axis=0,
        concat_axis=0,
        tiled=True,
    )
    cond_all = table[:, :own_cells].reshape(-1)
    cell_all = table[::parts, own_cells:].reshape(-1).astype(jnp.int32)

    near_slot = brick_slot[neighbours]
    near_blk = (near_slot // bricks).reshape(-1)
    far_key = (near_slot % bricks * 4 + opposite[None, :]).reshape(-1)
    own_key = jnp.arange(face_count, dtype=jnp.int32)
    matches = near_blk[:, None] == near_blk[None, :]
    send_rank = jnp.sum((matches & (own_key[None, :] < own_key[:, None])).astype(jnp.int32), axis=1)
    recv_rank = jnp.sum((matches & (far_key[None, :] < far_key[:, None])).astype(jnp.int32), axis=1)
    send_slot = near_blk * capacity + send_rank
    recv_slot = near_blk * capacity + recv_rank

    adjoint = sensitivity.astype(jnp.float32)
    tissue_faces = layers(tissue, brick_edge).astype(jnp.float32)
    cos_faces = jnp.cos(layers(fiber_angle, brick_edge).astype(jnp.float32)) ** 2
    factor_faces = jnp.concatenate(
        [
            ACROSS + (ALONG - ACROSS) * cos_faces[:, :2],
            ACROSS + (ALONG - ACROSS) * (1.0 - cos_faces[:, 2:]),
        ],
        axis=1,
    )
    fields = jnp.stack(
        [tissue_faces * factor_faces, layers(potential, brick_edge), layers(adjoint, brick_edge)], axis=2
    )
    flattened = fields.reshape(face_count, 3 * face_cells)
    outgoing = jnp.zeros((blocks * capacity, 3 * face_cells), jnp.float32).at[send_slot].set(flattened)
    received = lax.all_to_all(
        outgoing.reshape(blocks, capacity, 3 * face_cells), "blk", split_axis=0, concat_axis=0, tiled=True
    )
    faces = received.reshape(blocks * capacity, 3 * face_cells)[recv_slot].reshape(
        bricks, 4, 3 * z_layers, brick_edge
    )

    size = lax.axis_size("par")
    up = [(i, i + 1) for i in range(size - 1)]
    down = [(j, i) for i, j in up]
    last = jnp.stack([tissue[:, -1].astype(jnp.float32), potential[:, -1], adjoint[:, -1]], axis=1)
    initial = jnp.stack([tissue[:, 0].astype(jnp.float32), potential[:, 0], adjoint[:, 0]], axis=1)
    halos = jnp.concatenate([lax.ppermute(last, "par", up), lax.ppermute(initial, "par", down)], axis=1)

    theta = cond_all[brick_cell]
    theta_near = cond_all[cell_all[near_slot]]
    scales = jnp.concatenate(
        [theta[:, None], theta_near, jnp.zeros((bricks, 3), jnp.float32)], axis=1
    )
    final, adjoint, parts_out = cell_step(
        scales, tissue, fiber_angle, potential, sensitivity, faces, halos
    )
    brick_part = jnp.sum(parts_out, axis=(1, 2))
    onehot_cells = brick_cell[:, None] == jnp.arange(cell_count, dtype=jnp.int32)[None, :]
    shares = jnp.sum(jnp.where(onehot_cells, brick_part[:, None], 0.0), axis=0)
    grad_share = jnp.sum(
        lax.all_to_all(
            shares.reshape(devices, own_cells), ("blk", "par"), split_axis=0, concat_axis=0, tiled=True
        ),
        axis=0,
    )
    cell_gradient = TIMESTEP * grad_share / (conductance * float(BX) ** 1.5)
    return (final, adjoint, cell_gradient)


def solution(mesh):
    placed = (
        P("blk", "par", None),
        P("blk", "par", None),
        P("blk", "par", None),
        P("blk", "par", None),
        P(("blk", "par")),
        P(),
        P("blk", None),
        P("blk"),
    )
    return jax.shard_map(
        body,
        mesh=mesh,
        in_specs=placed,
        out_specs=(P("blk", "par", None), P("blk", "par", None), P(("blk", "par"))),
        check_vma=False,
    )
```

```python
import jax
import jax.numpy as jnp
from jax import lax
from jax.sharding import PartitionSpec as P
from jax.experimental import pallas as pl
from jax.experimental.pallas import tpu as pltpu

BX = 32
STEPS = 1


TIMESTEP = 0.12
THRESHOLD = 0.2
ACROSS = 0.3
ALONG = 1.0
VERTICAL = 0.6


def extended(x, sides, width):
    for axis, dim in sides:
        size, length = (lax.axis_size(axis), x.shape[dim])
        up = [(i, (i + 1) % size) for i in range(size - 1)]
        down = [(j, i) for i, j in up]
        last = lax.slice_in_dim(x, length - width, length, axis=dim)
        initial = lax.slice_in_dim(x, 0, width, axis=dim)
        before = lax.ppermute(last, axis, up)
        after = lax.ppermute(initial, axis, down)
        x = jnp.concatenate([before, x, after], axis=dim)
    return x


def layers(values, brick_edge):
    return jnp.stack(
        [
            values[..., :brick_edge],
            values[..., -brick_edge:],
            values[..., 0::brick_edge],
            values[..., brick_edge - 1 :: brick_edge],
        ],
        axis=1,
    )


def along_x(values, lower_face, upper_face, brick_edge):
    return (
        jnp.concatenate([lower_face, values[..., :-brick_edge]], -1),
        jnp.concatenate([values[..., brick_edge:], upper_face], -1),
    )


def along_y(values, lower_face, upper_face, brick_edge):
    y_index = jnp.arange(values.shape[-1]) % brick_edge
    zero_pad = jnp.zeros(values.shape[:-1] + (1,), values.dtype)
    shifted_down = jnp.concatenate([zero_pad, values[..., :-1]], -1)
    shifted_up = jnp.concatenate([values[..., 1:], zero_pad], -1)
    return (
        jnp.where(y_index == 0, jnp.repeat(lower_face, brick_edge, axis=-1), shifted_down),
        jnp.where(
            y_index == brick_edge - 1, jnp.repeat(upper_face, brick_edge, axis=-1), shifted_up
        ),
    )


def near_values(values, layer_set, padded, brick_edge):
    x_low, x_high = along_x(values, layer_set[:, 0], layer_set[:, 1], brick_edge)
    y_low, y_high = along_y(values, layer_set[:, 2], layer_set[:, 3], brick_edge)
    return (x_low, x_high, y_low, y_high, padded[:, :-2], padded[:, 2:])


def laplace(conduct, values, beside):
    summed = conduct[0] * (beside[0] - values)
    for facet in range(1, 6):
        summed = summed + conduct[facet] * (beside[facet] - values)
    return summed


def brick_terms(conduct, adjoint, beside_adjoint, earlier, beside_state):
    summed = -conduct[0] * (adjoint - beside_adjoint[0]) * (earlier - beside_state[0])
    for facet in range(1, 6):
        summed = summed - conduct[facet] * (adjoint - beside_adjoint[facet]) * (
            earlier - beside_state[facet]
        )
    return jnp.sum(summed, axis=(1, 2))


def weights(tissue, fiber_angle, brick_scale):
    present = tissue.astype(jnp.float32)
    cos_square = jnp.cos(fiber_angle.astype(jnp.float32)) ** 2
    weight_x = present * brick_scale * (ACROSS + (ALONG - ACROSS) * cos_square)
    weight_y = present * brick_scale * (ACROSS + (ALONG - ACROSS) * (1.0 - cos_square))
    weight_z = present * brick_scale * VERTICAL
    return (weight_x, weight_y, weight_z)


def conductances(weight_x, weight_y, weight_z, weight_near, padded_z, brick_edge):
    x_low, x_high = along_x(weight_x, weight_near[:, 0], weight_near[:, 1], brick_edge)
    y_low, y_high = along_y(weight_y, weight_near[:, 2], weight_near[:, 3], brick_edge)
    return (
        weight_x * x_low,
        weight_x * x_high,
        weight_y * y_low,
        weight_y * y_high,
        weight_z * padded_z[:, :-2],
        weight_z * padded_z[:, 2:],
    )


GROUP = 8


def expanders(edge, cells):
    lane = jnp.arange(cells, dtype=jnp.int32)[None, :]
    k = jnp.arange(edge, dtype=jnp.int32)[:, None]
    return jnp.stack(
        [lane == k, lane == cells - edge + k, lane == edge * k, lane == edge * k + edge - 1]
    )


def cell_kernel(scale_ref, expand_ref, tissue_ref, angle_ref, u_ref, l_ref, face_ref, halo_ref,
                u_out, l_out, part_out):
    g = pl.program_id(0)
    nz, cells = u_ref.shape[1], u_ref.shape[2]
    edge = face_ref.shape[-1]
    lane = lax.broadcasted_iota(jnp.int32, (nz, cells), 1)
    row = lax.broadcasted_iota(jnp.int32, (nz, cells), 0)
    ycoord = lane % edge
    masks = (lane < edge, lane >= cells - edge, ycoord == 0, ycoord == edge - 1)
    shifts = (edge, cells - edge, 1, cells - 1)
    zlo = row == 0
    zhi = row == nz - 1

    def one(i, carry):
        b = g * GROUP + i
        th = scale_ref[b, 0]
        present = tissue_ref[i].astype(jnp.float32)
        c = jnp.cos(angle_ref[i].astype(jnp.float32))
        c2 = c * c
        scaled = present * th
        wx = scaled * (ACROSS + (ALONG - ACROSS) * c2)
        wy = scaled * (ACROSS + (ALONG - ACROSS) * (1.0 - c2))
        wz = scaled * VERTICAL
        u = u_ref[i]
        l = l_ref[i].astype(jnp.float32)
        halo = halo_ref[i]
        conds, ub, lb = [], [], []
        for f in range(4):
            face = face_ref[i, f]
            high = face.astype(jnp.bfloat16)
            rest = face - high.astype(jnp.float32)
            middle = rest.astype(jnp.bfloat16)
            low = (rest - middle.astype(jnp.float32)).astype(jnp.bfloat16)
            ext = jnp.dot(high, expand_ref[f], preferred_element_type=jnp.float32)
            ext = ext + jnp.dot(middle, expand_ref[f], preferred_element_type=jnp.float32)
            ext = ext + jnp.dot(low, expand_ref[f], preferred_element_type=jnp.float32)
            w_self = wx if f < 2 else wy
            w_near = jnp.where(masks[f], scale_ref[b, 1 + f] * ext[:nz], pltpu.roll(w_self, shifts[f], 1))
            conds.append(w_self * w_near)
            ub.append(jnp.where(masks[f], ext[nz:2 * nz], pltpu.roll(u, shifts[f], 1)))
            lb.append(jnp.where(masks[f], ext[2 * nz:3 * nz], pltpu.roll(l, shifts[f], 1)))
        wz_lo = jnp.where(zlo, (halo[0:1] * th) * VERTICAL, pltpu.roll(wz, 1, 0))
        wz_hi = jnp.where(zhi, (halo[3:4] * th) * VERTICAL, pltpu.roll(wz, nz - 1, 0))
        conds += [wz * wz_lo, wz * wz_hi]
        ub += [jnp.where(zlo, halo[1:2], pltpu.roll(u, 1, 0)), jnp.where(zhi, halo[4:5], pltpu.roll(u, nz - 1, 0))]
        lb += [jnp.where(zlo, halo[2:3], pltpu.roll(l, 1, 0)), jnp.where(zhi, halo[5:6], pltpu.roll(l, nz - 1, 0))]
        lap_u = conds[0] * (ub[0] - u)
        lap_l = conds[0] * (lb[0] - l)
        terms = lap_l * (ub[0] - u)
        for k in range(1, 6):
            step_u = ub[k] - u
            step_l = conds[k] * (lb[k] - l)
            lap_u = lap_u + conds[k] * step_u
            lap_l = lap_l + step_l
            terms = terms + step_l * step_u
        ionic = u * (1.0 - u) * (u - THRESHOLD)
        slope = -3.0 * u * u + 2.0 * (1.0 + THRESHOLD) * u - THRESHOLD
        u_out[i] = u + TIMESTEP * (lap_u + ionic)
        l_out[i] = l + TIMESTEP * (lap_l + slope * l)
        col = -jnp.sum(terms, axis=0, keepdims=True)
        acc = col[:, 0:128]
        for t in range(1, cells // 128):
            acc = acc + col[:, t * 128:(t + 1) * 128]
        part_out[i] = acc
        return carry

    lax.fori_loop(0, GROUP, one, 0)


def cell_step(scales, tissue, angle, potential, sensitivity, faces, halos, interpret=False):
    bricks, nz, cells = potential.shape
    edge = faces.shape[-1]
    expand = expanders(edge, cells).astype(jnp.bfloat16)
    blk3 = lambda: pl.BlockSpec((GROUP, nz, cells), lambda g: (g, 0, 0))
    return pl.pallas_call(
        cell_kernel,
        grid=(bricks // GROUP,),
        in_specs=[
            pl.BlockSpec(memory_space=pltpu.SMEM),
            pl.BlockSpec((4, edge, cells), lambda g: (0, 0, 0)),
            blk3(), blk3(), blk3(), blk3(),
            pl.BlockSpec((GROUP, 4, faces.shape[2], edge), lambda g: (g, 0, 0, 0)),
            pl.BlockSpec((GROUP, 6, cells), lambda g: (g, 0, 0)),
        ],
        out_specs=[blk3(), blk3(), pl.BlockSpec((GROUP, 1, 128), lambda g: (g, 0, 0))],
        out_shape=[
            jax.ShapeDtypeStruct((bricks, nz, cells), jnp.float32),
            jax.ShapeDtypeStruct((bricks, nz, cells), jnp.float32),
            jax.ShapeDtypeStruct((bricks, 1, 128), jnp.float32),
        ],
        compiler_params=pltpu.CompilerParams(dimension_semantics=("parallel",)),
        interpret=interpret,
    )(scales, expand, tissue, angle, potential, sensitivity, faces, halos)


def body(
    potential, fiber_angle, tissue, sensitivity, conductance, brick_slot, neighbours, brick_cell
):
    bricks, z_layers, plane_cells = potential.shape
    brick_edge = BX
    blocks = lax.axis_size("blk")
    parts = lax.axis_size("par")
    devices = blocks * parts
    capacity = max(4, 8 * bricks // blocks)
    face_count = 4 * bricks
    face_cells = z_layers * brick_edge
    own_cells = conductance.shape[0]
    cell_count = own_cells * devices
    opposite = jnp.array([1, 0, 3, 2], jnp.int32)

    near_slot = brick_slot[neighbours]
    near_blk = (near_slot // bricks).reshape(-1)
    far_key = (near_slot % bricks * 4 + opposite[None, :]).reshape(-1)
    own_key = jnp.arange(face_count, dtype=jnp.int32)
    matches = near_blk[:, None] == near_blk[None, :]
    send_rank = jnp.sum((matches & (own_key[None, :] < own_key[:, None])).astype(jnp.int32), axis=1)
    recv_rank = jnp.sum((matches & (far_key[None, :] < far_key[:, None])).astype(jnp.int32), axis=1)
    send_slot = near_blk * capacity + send_rank
    recv_slot = near_blk * capacity + recv_rank

    adjoint = sensitivity.astype(jnp.float32)
    picker = expanders(brick_edge, plane_cells).reshape(4 * brick_edge, plane_cells).T.astype(jnp.float32)

    def boundary(values):
        picked = jnp.dot(
            values.astype(jnp.float32).reshape(bricks * z_layers, plane_cells),
            picker,
            precision=lax.Precision.HIGHEST,
        )
        return picked.reshape(bricks, z_layers, 4, brick_edge).transpose(0, 2, 1, 3)

    tissue_faces = boundary(tissue)
    cos_faces = jnp.cos(boundary(fiber_angle)) ** 2
    factor_faces = jnp.concatenate(
        [
            ACROSS + (ALONG - ACROSS) * cos_faces[:, :2],
            ACROSS + (ALONG - ACROSS) * (1.0 - cos_faces[:, 2:]),
        ],
        axis=1,
    )
    fields = jnp.stack(
        [tissue_faces * factor_faces, boundary(potential), boundary(sensitivity)], axis=2
    )
    flattened = fields.reshape(face_count, 3 * face_cells)
    outgoing = jnp.zeros((blocks * capacity, 3 * face_cells), jnp.float32).at[send_slot].set(flattened)
    shifted = [conductance] + [
        lax.ppermute(conductance, "par", [(i, (i + s) % parts) for i in range(parts)])
        for s in range(1, parts)
    ]
    source = (lax.axis_index("par") - jnp.arange(parts, dtype=jnp.int32)) % parts
    extra = jnp.concatenate([jnp.stack(shifted)[source].reshape(-1), brick_cell.astype(jnp.float32)])
    width = capacity * 3 * face_cells
    extra_width = -(-extra.shape[0] // 128) * 128
    extra = jnp.pad(extra, (0, extra_width - extra.shape[0]))
    sending = jnp.concatenate(
        [outgoing.reshape(blocks, width), jnp.broadcast_to(extra[None], (blocks, extra_width))], axis=1
    )
    arrived = lax.all_to_all(sending, "blk", split_axis=0, concat_axis=0, tiled=True)
    received = arrived[:, :width]
    par_cells = own_cells * parts
    cond_all = arrived[:, width : width + par_cells].reshape(-1)
    cell_all = arrived[:, width + par_cells : width + par_cells + bricks].reshape(-1).astype(jnp.int32)
    faces = received.reshape(blocks * capacity, 3 * face_cells)[recv_slot].reshape(
        bricks, 4, 3 * z_layers, brick_edge
    )
    faces = jnp.pad(faces, ((0, 0), (0, 0), (0, 32 - 3 * z_layers % 32), (0, 0)))

    size = lax.axis_size("par")
    up = [(i, i + 1) for i in range(size - 1)]
    down = [(j, i) for i, j in up]
    last = jnp.stack([tissue[:, -1].astype(jnp.float32), potential[:, -1], adjoint[:, -1]], axis=1)
    initial = jnp.stack([tissue[:, 0].astype(jnp.float32), potential[:, 0], adjoint[:, 0]], axis=1)
    halos = jnp.concatenate([lax.ppermute(last, "par", up), lax.ppermute(initial, "par", down)], axis=1)

    theta = cond_all[brick_cell]
    theta_near = cond_all[cell_all[near_slot]]
    scales = jnp.concatenate(
        [theta[:, None], theta_near, jnp.zeros((bricks, 3), jnp.float32)], axis=1
    )
    final, adjoint, parts_out = cell_step(
        scales, tissue, fiber_angle, potential, sensitivity, faces, halos
    )
    brick_part = jnp.sum(parts_out, axis=(1, 2))
    onehot_cells = brick_cell[:, None] == jnp.arange(cell_count, dtype=jnp.int32)[None, :]
    shares = jnp.sum(jnp.where(onehot_cells, brick_part[:, None], 0.0), axis=0)
    grad_share = jnp.sum(
        lax.all_to_all(
            shares.reshape(devices, own_cells), ("blk", "par"), split_axis=0, concat_axis=0, tiled=True
        ),
        axis=0,
    )
    cell_gradient = TIMESTEP * grad_share / (conductance * float(BX) ** 1.5)
    return (final, adjoint, cell_gradient)


def solution(mesh):
    placed = (
        P("blk", "par", None),
        P("blk", "par", None),
        P("blk", "par", None),
        P("blk", "par", None),
        P(("blk", "par")),
        P(),
        P("blk", None),
        P("blk"),
    )
    return jax.shard_map(
        body,
        mesh=mesh,
        in_specs=placed,
        out_specs=(P("blk", "par", None), P("blk", "par", None), P(("blk", "par"))),
        check_vma=False,
    )
```

```python
import jax
import jax.numpy as jnp
from jax import lax
from jax.sharding import PartitionSpec as P
from jax.experimental import pallas as pl
from jax.experimental.pallas import tpu as pltpu

BX = 32
STEPS = 1


TIMESTEP = 0.12
THRESHOLD = 0.2
ACROSS = 0.3
ALONG = 1.0
VERTICAL = 0.6


def extended(x, sides, width):
    for axis, dim in sides:
        size, length = (lax.axis_size(axis), x.shape[dim])
        up = [(i, (i + 1) % size) for i in range(size - 1)]
        down = [(j, i) for i, j in up]
        last = lax.slice_in_dim(x, length - width, length, axis=dim)
        initial = lax.slice_in_dim(x, 0, width, axis=dim)
        before = lax.ppermute(last, axis, up)
        after = lax.ppermute(initial, axis, down)
        x = jnp.concatenate([before, x, after], axis=dim)
    return x


def layers(values, brick_edge):
    return jnp.stack(
        [
            values[..., :brick_edge],
            values[..., -brick_edge:],
            values[..., 0::brick_edge],
            values[..., brick_edge - 1 :: brick_edge],
        ],
        axis=1,
    )


def along_x(values, lower_face, upper_face, brick_edge):
    return (
        jnp.concatenate([lower_face, values[..., :-brick_edge]], -1),
        jnp.concatenate([values[..., brick_edge:], upper_face], -1),
    )


def along_y(values, lower_face, upper_face, brick_edge):
    y_index = jnp.arange(values.shape[-1]) % brick_edge
    zero_pad = jnp.zeros(values.shape[:-1] + (1,), values.dtype)
    shifted_down = jnp.concatenate([zero_pad, values[..., :-1]], -1)
    shifted_up = jnp.concatenate([values[..., 1:], zero_pad], -1)
    return (
        jnp.where(y_index == 0, jnp.repeat(lower_face, brick_edge, axis=-1), shifted_down),
        jnp.where(
            y_index == brick_edge - 1, jnp.repeat(upper_face, brick_edge, axis=-1), shifted_up
        ),
    )


def near_values(values, layer_set, padded, brick_edge):
    x_low, x_high = along_x(values, layer_set[:, 0], layer_set[:, 1], brick_edge)
    y_low, y_high = along_y(values, layer_set[:, 2], layer_set[:, 3], brick_edge)
    return (x_low, x_high, y_low, y_high, padded[:, :-2], padded[:, 2:])


def laplace(conduct, values, beside):
    summed = conduct[0] * (beside[0] - values)
    for facet in range(1, 6):
        summed = summed + conduct[facet] * (beside[facet] - values)
    return summed


def brick_terms(conduct, adjoint, beside_adjoint, earlier, beside_state):
    summed = -conduct[0] * (adjoint - beside_adjoint[0]) * (earlier - beside_state[0])
    for facet in range(1, 6):
        summed = summed - conduct[facet] * (adjoint - beside_adjoint[facet]) * (
            earlier - beside_state[facet]
        )
    return jnp.sum(summed, axis=(1, 2))


def weights(tissue, fiber_angle, brick_scale):
    present = tissue.astype(jnp.float32)
    cos_square = jnp.cos(fiber_angle.astype(jnp.float32)) ** 2
    weight_x = present * brick_scale * (ACROSS + (ALONG - ACROSS) * cos_square)
    weight_y = present * brick_scale * (ACROSS + (ALONG - ACROSS) * (1.0 - cos_square))
    weight_z = present * brick_scale * VERTICAL
    return (weight_x, weight_y, weight_z)


def conductances(weight_x, weight_y, weight_z, weight_near, padded_z, brick_edge):
    x_low, x_high = along_x(weight_x, weight_near[:, 0], weight_near[:, 1], brick_edge)
    y_low, y_high = along_y(weight_y, weight_near[:, 2], weight_near[:, 3], brick_edge)
    return (
        weight_x * x_low,
        weight_x * x_high,
        weight_y * y_low,
        weight_y * y_high,
        weight_z * padded_z[:, :-2],
        weight_z * padded_z[:, 2:],
    )


GROUP = 8


def expanders(edge, cells):
    lane = jnp.arange(cells, dtype=jnp.int32)[None, :]
    k = jnp.arange(edge, dtype=jnp.int32)[:, None]
    return jnp.stack(
        [lane == k, lane == cells - edge + k, lane == edge * k, lane == edge * k + edge - 1]
    )


def cell_kernel(scale_ref, expand_ref, tissue_ref, angle_ref, u_ref, l_ref, face_ref, halo_ref,
                u_out, l_out, part_out):
    g = pl.program_id(0)
    nz, cells = u_ref.shape[1], u_ref.shape[2]
    edge = face_ref.shape[-1]
    lane = lax.broadcasted_iota(jnp.int32, (nz, cells), 1)
    row = lax.broadcasted_iota(jnp.int32, (nz, cells), 0)
    ycoord = lane % edge
    masks = (lane < edge, lane >= cells - edge, ycoord == 0, ycoord == edge - 1)
    shifts = (edge, cells - edge, 1, cells - 1)
    zlo = row == 0
    zhi = row == nz - 1

    def one(i, carry):
        b = g * GROUP + i
        th = scale_ref[b, 0]
        present = tissue_ref[i].astype(jnp.float32)
        c = jnp.cos(angle_ref[i].astype(jnp.float32))
        c2 = c * c
        scaled = present * th
        wx = scaled * (ACROSS + (ALONG - ACROSS) * c2)
        wy = scaled * (ACROSS + (ALONG - ACROSS) * (1.0 - c2))
        wz = scaled * VERTICAL
        u = u_ref[i]
        l = l_ref[i].astype(jnp.float32)
        halo = halo_ref[i]
        conds, ub, lb = [], [], []
        for f in range(4):
            face = face_ref[i, f]
            high = face.astype(jnp.bfloat16)
            rest = face - high.astype(jnp.float32)
            middle = rest.astype(jnp.bfloat16)
            low = (rest - middle.astype(jnp.float32)).astype(jnp.bfloat16)
            ext = jnp.dot(high, expand_ref[f], preferred_element_type=jnp.float32)
            ext = ext + jnp.dot(middle, expand_ref[f], preferred_element_type=jnp.float32)
            ext = ext + jnp.dot(low, expand_ref[f], preferred_element_type=jnp.float32)
            w_self = wx if f < 2 else wy
            w_near = jnp.where(masks[f], scale_ref[b, 1 + f] * ext[:nz], pltpu.roll(w_self, shifts[f], 1))
            conds.append(w_self * w_near)
            ub.append(jnp.where(masks[f], ext[nz:2 * nz], pltpu.roll(u, shifts[f], 1)))
            lb.append(jnp.where(masks[f], ext[2 * nz:3 * nz], pltpu.roll(l, shifts[f], 1)))
        wz_lo = jnp.where(zlo, (halo[0:1] * th) * VERTICAL, pltpu.roll(wz, 1, 0))
        wz_hi = jnp.where(zhi, (halo[3:4] * th) * VERTICAL, pltpu.roll(wz, nz - 1, 0))
        conds += [wz * wz_lo, wz * wz_hi]
        ub += [jnp.where(zlo, halo[1:2], pltpu.roll(u, 1, 0)), jnp.where(zhi, halo[4:5], pltpu.roll(u, nz - 1, 0))]
        lb += [jnp.where(zlo, halo[2:3], pltpu.roll(l, 1, 0)), jnp.where(zhi, halo[5:6], pltpu.roll(l, nz - 1, 0))]
        lap_u = conds[0] * (ub[0] - u)
        lap_l = conds[0] * (lb[0] - l)
        terms = lap_l * (ub[0] - u)
        for k in range(1, 6):
            step_u = ub[k] - u
            step_l = conds[k] * (lb[k] - l)
            lap_u = lap_u + conds[k] * step_u
            lap_l = lap_l + step_l
            terms = terms + step_l * step_u
        ionic = u * (1.0 - u) * (u - THRESHOLD)
        slope = -3.0 * u * u + 2.0 * (1.0 + THRESHOLD) * u - THRESHOLD
        u_out[i] = u + TIMESTEP * (lap_u + ionic)
        l_out[i] = l + TIMESTEP * (lap_l + slope * l)
        col = -jnp.sum(terms, axis=0, keepdims=True)
        acc = col[:, 0:128]
        for t in range(1, cells // 128):
            acc = acc + col[:, t * 128:(t + 1) * 128]
        part_out[i] = acc
        return carry

    lax.fori_loop(0, GROUP, one, 0)


def cell_step(scales, tissue, angle, potential, sensitivity, faces, halos, interpret=False):
    bricks, nz, cells = potential.shape
    edge = faces.shape[-1]
    expand = expanders(edge, cells).astype(jnp.bfloat16)
    blk3 = lambda: pl.BlockSpec((GROUP, nz, cells), lambda g: (g, 0, 0))
    return pl.pallas_call(
        cell_kernel,
        grid=(bricks // GROUP,),
        in_specs=[
            pl.BlockSpec(memory_space=pltpu.SMEM),
            pl.BlockSpec((4, edge, cells), lambda g: (0, 0, 0)),
            blk3(), blk3(), blk3(), blk3(),
            pl.BlockSpec((GROUP, 4, faces.shape[2], edge), lambda g: (g, 0, 0, 0)),
            pl.BlockSpec((GROUP, 6, cells), lambda g: (g, 0, 0)),
        ],
        out_specs=[blk3(), blk3(), pl.BlockSpec((GROUP, 1, 128), lambda g: (g, 0, 0))],
        out_shape=[
            jax.ShapeDtypeStruct((bricks, nz, cells), jnp.float32),
            jax.ShapeDtypeStruct((bricks, nz, cells), jnp.float32),
            jax.ShapeDtypeStruct((bricks, 1, 128), jnp.float32),
        ],
        compiler_params=pltpu.CompilerParams(dimension_semantics=("parallel",)),
        interpret=interpret,
    )(scales, expand, tissue, angle, potential, sensitivity, faces, halos)


def group_sum(values):
    col = jnp.sum(values, axis=0, keepdims=True)
    acc = col[:, 0:128]
    for t in range(1, values.shape[1] // 128):
        acc = acc + col[:, t * 128:(t + 1) * 128]
    return acc


def inner_kernel(tissue_ref, angle_ref, u_ref, l_ref, lu_out, ll_out, gx_out, gy_out, part_out):
    nz, cells = u_ref.shape[1], u_ref.shape[2]
    edge = BX
    lane = lax.broadcasted_iota(jnp.int32, (nz, cells), 1)
    row = lax.broadcasted_iota(jnp.int32, (nz, cells), 0)
    ycoord = lane % edge
    inside = (lane >= edge, lane < cells - edge, ycoord != 0, ycoord != edge - 1, row != 0, row != nz - 1)
    shifts = ((edge, 1), (cells - edge, 1), (1, 1), (cells - 1, 1), (1, 0), (nz - 1, 0))

    def one(i, carry):
        present = tissue_ref[i].astype(jnp.float32)
        c = jnp.cos(angle_ref[i].astype(jnp.float32))
        c2 = c * c
        gx = present * (ACROSS + (ALONG - ACROSS) * c2)
        gy = present * (ACROSS + (ALONG - ACROSS) * (1.0 - c2))
        gz = present * VERTICAL
        u = u_ref[i]
        l = l_ref[i].astype(jnp.float32)
        lap_u = jnp.zeros_like(u)
        lap_l = jnp.zeros_like(u)
        terms = jnp.zeros_like(u)
        for k in range(6):
            g = gx if k < 2 else (gy if k < 4 else gz)
            shift, axis = shifts[k]
            conduct = jnp.where(inside[k], g * pltpu.roll(g, shift, axis), 0.0)
            step_u = pltpu.roll(u, shift, axis) - u
            step_l = conduct * (pltpu.roll(l, shift, axis) - l)
            lap_u = lap_u + conduct * step_u
            lap_l = lap_l + step_l
            terms = terms + step_l * step_u
        lu_out[i] = lap_u
        ll_out[i] = lap_l
        gx_out[i] = gx
        gy_out[i] = gy
        part_out[i] = group_sum(terms)
        return carry

    lax.fori_loop(0, GROUP, one, 0)


def outer_kernel(scale_ref, expand_ref, u_ref, l_ref, lu_ref, ll_ref, gx_ref, gy_ref, inner_ref, face_ref,
                 halo_ref, u_out, l_out, part_out):
    g = pl.program_id(0)
    nz, cells = u_ref.shape[1], u_ref.shape[2]
    edge = BX
    lane = lax.broadcasted_iota(jnp.int32, (nz, cells), 1)
    row = lax.broadcasted_iota(jnp.int32, (nz, cells), 0)
    ycoord = lane % edge
    masks = (lane < edge, lane >= cells - edge, ycoord == 0, ycoord == edge - 1)

    def one(i, carry):
        b = g * GROUP + i
        th = scale_ref[b, 0]
        u = u_ref[i]
        l = l_ref[i].astype(jnp.float32)
        gx = gx_ref[i]
        gy = gy_ref[i]
        halo = halo_ref[i]
        edge_u, edge_l, edge_t = [], [], []
        for side, r in ((0, 0), (1, nz - 1)):
            own_z = (gx[r:r + 1] != 0.0).astype(jnp.float32) * VERTICAL
            conduct = own_z * (halo[3 * side:3 * side + 1] * VERTICAL)
            step_u = halo[3 * side + 1:3 * side + 2] - u[r:r + 1]
            step_l = conduct * (halo[3 * side + 2:3 * side + 3] - l[r:r + 1])
            edge_u.append(conduct * step_u)
            edge_l.append(step_l)
            edge_t.append(step_l * step_u)
        lap_u = lu_ref[i] + jnp.where(row == 0, edge_u[0], 0.0) + jnp.where(row == nz - 1, edge_u[1], 0.0)
        lap_l = ll_ref[i] + jnp.where(row == 0, edge_l[0], 0.0) + jnp.where(row == nz - 1, edge_l[1], 0.0)
        inner = inner_ref[i] + group_sum(edge_t[0]) + group_sum(edge_t[1])
        face_u = jnp.zeros_like(u)
        face_l = jnp.zeros_like(u)
        face_t = jnp.zeros_like(u)
        for f in range(4):
            face = face_ref[i, f]
            high = face.astype(jnp.bfloat16)
            rest = face - high.astype(jnp.float32)
            middle = rest.astype(jnp.bfloat16)
            low = (rest - middle.astype(jnp.float32)).astype(jnp.bfloat16)
            ext = jnp.dot(high, expand_ref[f], preferred_element_type=jnp.float32)
            ext = ext + jnp.dot(middle, expand_ref[f], preferred_element_type=jnp.float32)
            ext = ext + jnp.dot(low, expand_ref[f], preferred_element_type=jnp.float32)
            g_self = gx if f < 2 else gy
            conduct = jnp.where(masks[f], scale_ref[b, 1 + f] * (g_self * ext[:nz]), 0.0)
            step_u = ext[nz:2 * nz] - u
            step_l = conduct * (ext[2 * nz:3 * nz] - l)
            face_u = face_u + conduct * step_u
            face_l = face_l + step_l
            face_t = face_t + step_l * step_u
        square = th * th
        ionic = u * (1.0 - u) * (u - THRESHOLD)
        slope = -3.0 * u * u + 2.0 * (1.0 + THRESHOLD) * u - THRESHOLD
        u_out[i] = u + TIMESTEP * ((square * lap_u + th * face_u) + ionic)
        l_out[i] = l + TIMESTEP * ((square * lap_l + th * face_l) + slope * l)
        part_out[i] = -(square * inner + th * group_sum(face_t))
        return carry

    lax.fori_loop(0, GROUP, one, 0)


def inner_step(tissue, angle, potential, sensitivity, interpret=False):
    bricks, nz, cells = potential.shape
    blk3 = lambda: pl.BlockSpec((GROUP, nz, cells), lambda g: (g, 0, 0))
    full = jax.ShapeDtypeStruct((bricks, nz, cells), jnp.float32)
    return pl.pallas_call(
        inner_kernel,
        grid=(bricks // GROUP,),
        in_specs=[blk3(), blk3(), blk3(), blk3()],
        out_specs=[blk3(), blk3(), blk3(), blk3(), pl.BlockSpec((GROUP, 1, 128), lambda g: (g, 0, 0))],
        out_shape=[full, full, full, full, jax.ShapeDtypeStruct((bricks, 1, 128), jnp.float32)],
        compiler_params=pltpu.CompilerParams(dimension_semantics=("parallel",)),
        interpret=interpret,
    )(tissue, angle, potential, sensitivity)


def outer_step(scales, potential, sensitivity, inner, faces, halos, interpret=False):
    bricks, nz, cells = potential.shape
    edge = faces.shape[-1]
    expand = expanders(edge, cells).astype(jnp.bfloat16)
    blk3 = lambda: pl.BlockSpec((GROUP, nz, cells), lambda g: (g, 0, 0))
    lap_u, lap_l, gx, gy, inner_part = inner
    return pl.pallas_call(
        outer_kernel,
        grid=(bricks // GROUP,),
        in_specs=[
            pl.BlockSpec(memory_space=pltpu.SMEM),
            pl.BlockSpec((4, edge, cells), lambda g: (0, 0, 0)),
            blk3(), blk3(), blk3(), blk3(), blk3(), blk3(),
            pl.BlockSpec((GROUP, 1, 128), lambda g: (g, 0, 0)),
            pl.BlockSpec((GROUP, 4, faces.shape[2], edge), lambda g: (g, 0, 0, 0)),
            pl.BlockSpec((GROUP, 6, cells), lambda g: (g, 0, 0)),
        ],
        out_specs=[blk3(), blk3(), pl.BlockSpec((GROUP, 1, 128), lambda g: (g, 0, 0))],
        out_shape=[
            jax.ShapeDtypeStruct((bricks, nz, cells), jnp.float32),
            jax.ShapeDtypeStruct((bricks, nz, cells), jnp.float32),
            jax.ShapeDtypeStruct((bricks, 1, 128), jnp.float32),
        ],
        compiler_params=pltpu.CompilerParams(dimension_semantics=("parallel",)),
        interpret=interpret,
    )(scales, expand, potential, sensitivity, lap_u, lap_l, gx, gy, inner_part, faces, halos)


def body(
    potential, fiber_angle, tissue, sensitivity, conductance, brick_slot, neighbours, brick_cell
):
    bricks, z_layers, plane_cells = potential.shape
    brick_edge = BX
    blocks = lax.axis_size("blk")
    parts = lax.axis_size("par")
    devices = blocks * parts
    capacity = max(4, 8 * bricks // blocks)
    face_count = 4 * bricks
    face_cells = z_layers * brick_edge
    own_cells = conductance.shape[0]
    cell_count = own_cells * devices
    opposite = jnp.array([1, 0, 3, 2], jnp.int32)

    near_slot = brick_slot[neighbours]
    near_blk = (near_slot // bricks).reshape(-1)
    far_key = (near_slot % bricks * 4 + opposite[None, :]).reshape(-1)
    own_key = jnp.arange(face_count, dtype=jnp.int32)
    matches = near_blk[:, None] == near_blk[None, :]
    send_rank = jnp.sum((matches & (own_key[None, :] < own_key[:, None])).astype(jnp.int32), axis=1)
    recv_rank = jnp.sum((matches & (far_key[None, :] < far_key[:, None])).astype(jnp.int32), axis=1)
    send_slot = near_blk * capacity + send_rank
    recv_slot = near_blk * capacity + recv_rank

    adjoint = sensitivity.astype(jnp.float32)
    inner = inner_step(tissue, fiber_angle, potential, sensitivity)
    picker = expanders(brick_edge, plane_cells).reshape(4 * brick_edge, plane_cells).T.astype(jnp.float32)

    def boundary(values):
        picked = jnp.dot(
            values.astype(jnp.float32).reshape(bricks * z_layers, plane_cells),
            picker,
            precision=lax.Precision.HIGHEST,
        )
        return picked.reshape(bricks, z_layers, 4, brick_edge).transpose(0, 2, 1, 3)

    tissue_faces = boundary(tissue)
    cos_faces = jnp.cos(boundary(fiber_angle)) ** 2
    factor_faces = jnp.concatenate(
        [
            ACROSS + (ALONG - ACROSS) * cos_faces[:, :2],
            ACROSS + (ALONG - ACROSS) * (1.0 - cos_faces[:, 2:]),
        ],
        axis=1,
    )
    fields = jnp.stack(
        [tissue_faces * factor_faces, boundary(potential), boundary(sensitivity)], axis=2
    )
    flattened = fields.reshape(face_count, 3 * face_cells)
    outgoing = jnp.zeros((blocks * capacity, 3 * face_cells), jnp.float32).at[send_slot].set(flattened)
    shifted = [conductance] + [
        lax.ppermute(conductance, "par", [(i, (i + s) % parts) for i in range(parts)])
        for s in range(1, parts)
    ]
    source = (lax.axis_index("par") - jnp.arange(parts, dtype=jnp.int32)) % parts
    extra = jnp.concatenate([jnp.stack(shifted)[source].reshape(-1), brick_cell.astype(jnp.float32)])
    width = capacity * 3 * face_cells
    extra_width = -(-extra.shape[0] // 128) * 128
    extra = jnp.pad(extra, (0, extra_width - extra.shape[0]))
    sending = jnp.concatenate(
        [outgoing.reshape(blocks, width), jnp.broadcast_to(extra[None], (blocks, extra_width))], axis=1
    )
    arrived = lax.all_to_all(sending, "blk", split_axis=0, concat_axis=0, tiled=True)
    received = arrived[:, :width]
    par_cells = own_cells * parts
    cond_all = arrived[:, width : width + par_cells].reshape(-1)
    cell_all = arrived[:, width + par_cells : width + par_cells + bricks].reshape(-1).astype(jnp.int32)
    faces = received.reshape(blocks * capacity, 3 * face_cells)[recv_slot].reshape(
        bricks, 4, 3 * z_layers, brick_edge
    )
    faces = jnp.pad(faces, ((0, 0), (0, 0), (0, 32 - 3 * z_layers % 32), (0, 0)))

    size = lax.axis_size("par")
    up = [(i, i + 1) for i in range(size - 1)]
    down = [(j, i) for i, j in up]
    last = jnp.stack([tissue[:, -1].astype(jnp.float32), potential[:, -1], adjoint[:, -1]], axis=1)
    initial = jnp.stack([tissue[:, 0].astype(jnp.float32), potential[:, 0], adjoint[:, 0]], axis=1)
    halos = jnp.concatenate([lax.ppermute(last, "par", up), lax.ppermute(initial, "par", down)], axis=1)

    theta = cond_all[brick_cell]
    theta_near = cond_all[cell_all[near_slot]]
    scales = jnp.concatenate(
        [theta[:, None], theta_near, jnp.zeros((bricks, 3), jnp.float32)], axis=1
    )
    final, adjoint, parts_out = outer_step(scales, potential, sensitivity, inner, faces, halos)
    brick_part = jnp.sum(parts_out, axis=(1, 2))
    onehot_cells = brick_cell[:, None] == jnp.arange(cell_count, dtype=jnp.int32)[None, :]
    shares = jnp.sum(jnp.where(onehot_cells, brick_part[:, None], 0.0), axis=0)
    grad_share = jnp.sum(
        lax.all_to_all(
            shares.reshape(devices, own_cells), ("blk", "par"), split_axis=0, concat_axis=0, tiled=True
        ),
        axis=0,
    )
    cell_gradient = TIMESTEP * grad_share / (conductance * float(BX) ** 1.5)
    return (final, adjoint, cell_gradient)


def solution(mesh):
    placed = (
        P("blk", "par", None),
        P("blk", "par", None),
        P("blk", "par", None),
        P("blk", "par", None),
        P(("blk", "par")),
        P(),
        P("blk", None),
        P("blk"),
    )
    return jax.shard_map(
        body,
        mesh=mesh,
        in_specs=placed,
        out_specs=(P("blk", "par", None), P("blk", "par", None), P(("blk", "par"))),
        check_vma=False,
    )
```

```python
import jax
import jax.numpy as jnp
from jax import lax
from jax.sharding import PartitionSpec as P
from jax.experimental import pallas as pl
from jax.experimental.pallas import tpu as pltpu

BX = 32
STEPS = 1


TIMESTEP = 0.12
THRESHOLD = 0.2
ACROSS = 0.3
ALONG = 1.0
VERTICAL = 0.6


def extended(x, sides, width):
    for axis, dim in sides:
        size, length = (lax.axis_size(axis), x.shape[dim])
        up = [(i, (i + 1) % size) for i in range(size - 1)]
        down = [(j, i) for i, j in up]
        last = lax.slice_in_dim(x, length - width, length, axis=dim)
        initial = lax.slice_in_dim(x, 0, width, axis=dim)
        before = lax.ppermute(last, axis, up)
        after = lax.ppermute(initial, axis, down)
        x = jnp.concatenate([before, x, after], axis=dim)
    return x


def layers(values, brick_edge):
    return jnp.stack(
        [
            values[..., :brick_edge],
            values[..., -brick_edge:],
            values[..., 0::brick_edge],
            values[..., brick_edge - 1 :: brick_edge],
        ],
        axis=1,
    )


def along_x(values, lower_face, upper_face, brick_edge):
    return (
        jnp.concatenate([lower_face, values[..., :-brick_edge]], -1),
        jnp.concatenate([values[..., brick_edge:], upper_face], -1),
    )


def along_y(values, lower_face, upper_face, brick_edge):
    y_index = jnp.arange(values.shape[-1]) % brick_edge
    zero_pad = jnp.zeros(values.shape[:-1] + (1,), values.dtype)
    shifted_down = jnp.concatenate([zero_pad, values[..., :-1]], -1)
    shifted_up = jnp.concatenate([values[..., 1:], zero_pad], -1)
    return (
        jnp.where(y_index == 0, jnp.repeat(lower_face, brick_edge, axis=-1), shifted_down),
        jnp.where(
            y_index == brick_edge - 1, jnp.repeat(upper_face, brick_edge, axis=-1), shifted_up
        ),
    )


def near_values(values, layer_set, padded, brick_edge):
    x_low, x_high = along_x(values, layer_set[:, 0], layer_set[:, 1], brick_edge)
    y_low, y_high = along_y(values, layer_set[:, 2], layer_set[:, 3], brick_edge)
    return (x_low, x_high, y_low, y_high, padded[:, :-2], padded[:, 2:])


def laplace(conduct, values, beside):
    summed = conduct[0] * (beside[0] - values)
    for facet in range(1, 6):
        summed = summed + conduct[facet] * (beside[facet] - values)
    return summed


def brick_terms(conduct, adjoint, beside_adjoint, earlier, beside_state):
    summed = -conduct[0] * (adjoint - beside_adjoint[0]) * (earlier - beside_state[0])
    for facet in range(1, 6):
        summed = summed - conduct[facet] * (adjoint - beside_adjoint[facet]) * (
            earlier - beside_state[facet]
        )
    return jnp.sum(summed, axis=(1, 2))


def weights(tissue, fiber_angle, brick_scale):
    present = tissue.astype(jnp.float32)
    cos_square = jnp.cos(fiber_angle.astype(jnp.float32)) ** 2
    weight_x = present * brick_scale * (ACROSS + (ALONG - ACROSS) * cos_square)
    weight_y = present * brick_scale * (ACROSS + (ALONG - ACROSS) * (1.0 - cos_square))
    weight_z = present * brick_scale * VERTICAL
    return (weight_x, weight_y, weight_z)


def conductances(weight_x, weight_y, weight_z, weight_near, padded_z, brick_edge):
    x_low, x_high = along_x(weight_x, weight_near[:, 0], weight_near[:, 1], brick_edge)
    y_low, y_high = along_y(weight_y, weight_near[:, 2], weight_near[:, 3], brick_edge)
    return (
        weight_x * x_low,
        weight_x * x_high,
        weight_y * y_low,
        weight_y * y_high,
        weight_z * padded_z[:, :-2],
        weight_z * padded_z[:, 2:],
    )


GROUP = 8


def expanders(edge, cells):
    lane = jnp.arange(cells, dtype=jnp.int32)[None, :]
    k = jnp.arange(edge, dtype=jnp.int32)[:, None]
    return jnp.stack(
        [lane == k, lane == cells - edge + k, lane == edge * k, lane == edge * k + edge - 1]
    )


def cell_kernel(scale_ref, expand_ref, tissue_ref, angle_ref, u_ref, l_ref, face_ref, halo_ref,
                u_out, l_out, part_out):
    g = pl.program_id(0)
    nz, cells = u_ref.shape[1], u_ref.shape[2]
    edge = face_ref.shape[-1]
    lane = lax.broadcasted_iota(jnp.int32, (nz, cells), 1)
    row = lax.broadcasted_iota(jnp.int32, (nz, cells), 0)
    ycoord = lane % edge
    masks = (lane < edge, lane >= cells - edge, ycoord == 0, ycoord == edge - 1)
    shifts = (edge, cells - edge, 1, cells - 1)
    zlo = row == 0
    zhi = row == nz - 1

    def one(i, carry):
        b = g * GROUP + i
        th = scale_ref[b, 0]
        present = tissue_ref[i].astype(jnp.float32)
        c = jnp.cos(angle_ref[i].astype(jnp.float32))
        c2 = c * c
        scaled = present * th
        wx = scaled * (ACROSS + (ALONG - ACROSS) * c2)
        wy = scaled * (ACROSS + (ALONG - ACROSS) * (1.0 - c2))
        wz = scaled * VERTICAL
        u = u_ref[i]
        l = l_ref[i].astype(jnp.float32)
        halo = halo_ref[i]
        conds, ub, lb = [], [], []
        for f in range(4):
            face = face_ref[i, f]
            high = face.astype(jnp.bfloat16)
            rest = face - high.astype(jnp.float32)
            middle = rest.astype(jnp.bfloat16)
            low = (rest - middle.astype(jnp.float32)).astype(jnp.bfloat16)
            ext = jnp.dot(high, expand_ref[f], preferred_element_type=jnp.float32)
            ext = ext + jnp.dot(middle, expand_ref[f], preferred_element_type=jnp.float32)
            ext = ext + jnp.dot(low, expand_ref[f], preferred_element_type=jnp.float32)
            w_self = wx if f < 2 else wy
            w_near = jnp.where(masks[f], scale_ref[b, 1 + f] * ext[:nz], pltpu.roll(w_self, shifts[f], 1))
            conds.append(w_self * w_near)
            ub.append(jnp.where(masks[f], ext[nz:2 * nz], pltpu.roll(u, shifts[f], 1)))
            lb.append(jnp.where(masks[f], ext[2 * nz:3 * nz], pltpu.roll(l, shifts[f], 1)))
        wz_lo = jnp.where(zlo, (halo[0:1] * th) * VERTICAL, pltpu.roll(wz, 1, 0))
        wz_hi = jnp.where(zhi, (halo[3:4] * th) * VERTICAL, pltpu.roll(wz, nz - 1, 0))
        conds += [wz * wz_lo, wz * wz_hi]
        ub += [jnp.where(zlo, halo[1:2], pltpu.roll(u, 1, 0)), jnp.where(zhi, halo[4:5], pltpu.roll(u, nz - 1, 0))]
        lb += [jnp.where(zlo, halo[2:3], pltpu.roll(l, 1, 0)), jnp.where(zhi, halo[5:6], pltpu.roll(l, nz - 1, 0))]
        lap_u = conds[0] * (ub[0] - u)
        lap_l = conds[0] * (lb[0] - l)
        terms = lap_l * (ub[0] - u)
        for k in range(1, 6):
            step_u = ub[k] - u
            step_l = conds[k] * (lb[k] - l)
            lap_u = lap_u + conds[k] * step_u
            lap_l = lap_l + step_l
            terms = terms + step_l * step_u
        ionic = u * (1.0 - u) * (u - THRESHOLD)
        slope = -3.0 * u * u + 2.0 * (1.0 + THRESHOLD) * u - THRESHOLD
        u_out[i] = u + TIMESTEP * (lap_u + ionic)
        l_out[i] = l + TIMESTEP * (lap_l + slope * l)
        col = -jnp.sum(terms, axis=0, keepdims=True)
        acc = col[:, 0:128]
        for t in range(1, cells // 128):
            acc = acc + col[:, t * 128:(t + 1) * 128]
        part_out[i] = acc
        return carry

    lax.fori_loop(0, GROUP, one, 0)


def cell_step(scales, tissue, angle, potential, sensitivity, faces, halos, interpret=False):
    bricks, nz, cells = potential.shape
    edge = faces.shape[-1]
    expand = expanders(edge, cells).astype(jnp.bfloat16)
    blk3 = lambda: pl.BlockSpec((GROUP, nz, cells), lambda g: (g, 0, 0))
    return pl.pallas_call(
        cell_kernel,
        grid=(bricks // GROUP,),
        in_specs=[
            pl.BlockSpec(memory_space=pltpu.SMEM),
            pl.BlockSpec((4, edge, cells), lambda g: (0, 0, 0)),
            blk3(), blk3(), blk3(), blk3(),
            pl.BlockSpec((GROUP, 4, faces.shape[2], edge), lambda g: (g, 0, 0, 0)),
            pl.BlockSpec((GROUP, 6, cells), lambda g: (g, 0, 0)),
        ],
        out_specs=[blk3(), blk3(), pl.BlockSpec((GROUP, 1, 128), lambda g: (g, 0, 0))],
        out_shape=[
            jax.ShapeDtypeStruct((bricks, nz, cells), jnp.float32),
            jax.ShapeDtypeStruct((bricks, nz, cells), jnp.float32),
            jax.ShapeDtypeStruct((bricks, 1, 128), jnp.float32),
        ],
        compiler_params=pltpu.CompilerParams(dimension_semantics=("parallel",)),
        interpret=interpret,
    )(scales, expand, tissue, angle, potential, sensitivity, faces, halos)


def group_sum(values):
    col = jnp.sum(values, axis=0, keepdims=True)
    acc = col[:, 0:128]
    for t in range(1, values.shape[1] // 128):
        acc = acc + col[:, t * 128:(t + 1) * 128]
    return acc


def inner_kernel(tissue_ref, angle_ref, u_ref, l_ref, lu_out, ll_out, gx_out, gy_out, part_out):
    nz, cells = u_ref.shape[1], u_ref.shape[2]
    edge = BX
    lane = lax.broadcasted_iota(jnp.int32, (nz, cells), 1)
    row = lax.broadcasted_iota(jnp.int32, (nz, cells), 0)
    ycoord = lane % edge
    inside = (lane >= edge, lane < cells - edge, ycoord != 0, ycoord != edge - 1, row != 0, row != nz - 1)
    shifts = ((edge, 1), (cells - edge, 1), (1, 1), (cells - 1, 1), (1, 0), (nz - 1, 0))

    def one(i, carry):
        present = tissue_ref[i].astype(jnp.float32)
        c = jnp.cos(angle_ref[i].astype(jnp.float32))
        c2 = c * c
        gx = present * (ACROSS + (ALONG - ACROSS) * c2)
        gy = present * (ACROSS + (ALONG - ACROSS) * (1.0 - c2))
        gz = present * VERTICAL
        u = u_ref[i]
        l = l_ref[i].astype(jnp.float32)
        lap_u = jnp.zeros_like(u)
        lap_l = jnp.zeros_like(u)
        terms = jnp.zeros_like(u)
        for k in range(6):
            g = gx if k < 2 else (gy if k < 4 else gz)
            shift, axis = shifts[k]
            conduct = jnp.where(inside[k], g * pltpu.roll(g, shift, axis), 0.0)
            step_u = pltpu.roll(u, shift, axis) - u
            step_l = conduct * (pltpu.roll(l, shift, axis) - l)
            lap_u = lap_u + conduct * step_u
            lap_l = lap_l + step_l
            terms = terms + step_l * step_u
        lu_out[i] = lap_u
        ll_out[i] = lap_l
        gx_out[i] = gx
        gy_out[i] = gy
        part_out[i] = group_sum(terms)
        return carry

    lax.fori_loop(0, GROUP, one, 0)


def outer_kernel(scale_ref, expand_ref, u_ref, l_ref, lu_ref, ll_ref, gx_ref, gy_ref, inner_ref, face_ref,
                 halo_ref, u_out, l_out, part_out):
    g = pl.program_id(0)
    nz, cells = u_ref.shape[1], u_ref.shape[2]
    edge = BX
    lane = lax.broadcasted_iota(jnp.int32, (nz, cells), 1)
    row = lax.broadcasted_iota(jnp.int32, (nz, cells), 0)
    ycoord = lane % edge
    masks = (lane < edge, lane >= cells - edge, ycoord == 0, ycoord == edge - 1)

    def one(i, carry):
        b = g * GROUP + i
        th = scale_ref[b, 0]
        u = u_ref[i]
        l = l_ref[i].astype(jnp.float32)
        gx = gx_ref[i]
        gy = gy_ref[i]
        halo = halo_ref[i]
        edge_u, edge_l, edge_t = [], [], []
        for side, r in ((0, 0), (1, nz - 1)):
            own_z = (gx[r:r + 1] != 0.0).astype(jnp.float32) * VERTICAL
            conduct = own_z * (halo[3 * side:3 * side + 1] * VERTICAL)
            step_u = halo[3 * side + 1:3 * side + 2] - u[r:r + 1]
            step_l = conduct * (halo[3 * side + 2:3 * side + 3] - l[r:r + 1])
            edge_u.append(conduct * step_u)
            edge_l.append(step_l)
            edge_t.append(step_l * step_u)
        lap_u = lu_ref[i] + jnp.where(row == 0, edge_u[0], 0.0) + jnp.where(row == nz - 1, edge_u[1], 0.0)
        lap_l = ll_ref[i] + jnp.where(row == 0, edge_l[0], 0.0) + jnp.where(row == nz - 1, edge_l[1], 0.0)
        inner = inner_ref[i] + group_sum(edge_t[0]) + group_sum(edge_t[1])
        face_u = jnp.zeros_like(u)
        face_l = jnp.zeros_like(u)
        face_t = jnp.zeros_like(u)
        for f in range(4):
            face = face_ref[i, f]
            pieces = []
            for part in (face[:2 * nz],):
                high = part.astype(jnp.bfloat16).astype(jnp.float32)
                rest = part - high
                middle = rest.astype(jnp.bfloat16).astype(jnp.float32)
                low = (rest - middle).astype(jnp.bfloat16).astype(jnp.float32)
                pieces += [high, middle, low]
            pieces += [face[2 * nz:3 * nz], jnp.zeros_like(face[:nz])]
            stacked = jnp.concatenate(pieces, axis=0).astype(jnp.bfloat16)
            ext = jnp.dot(stacked, expand_ref[f], preferred_element_type=jnp.float32)
            near_w = (ext[0:nz] + ext[2 * nz:3 * nz]) + ext[4 * nz:5 * nz]
            near_u = (ext[nz:2 * nz] + ext[3 * nz:4 * nz]) + ext[5 * nz:6 * nz]
            near_l = ext[6 * nz:7 * nz]
            g_self = gx if f < 2 else gy
            conduct = jnp.where(masks[f], scale_ref[b, 1 + f] * (g_self * near_w), 0.0)
            step_u = near_u - u
            step_l = conduct * (near_l - l)
            face_u = face_u + conduct * step_u
            face_l = face_l + step_l
            face_t = face_t + step_l * step_u
        square = th * th
        ionic = u * (1.0 - u) * (u - THRESHOLD)
        slope = -3.0 * u * u + 2.0 * (1.0 + THRESHOLD) * u - THRESHOLD
        u_out[i] = u + TIMESTEP * ((square * lap_u + th * face_u) + ionic)
        l_out[i] = l + TIMESTEP * ((square * lap_l + th * face_l) + slope * l)
        part_out[i] = -(square * inner + th * group_sum(face_t))
        return carry

    lax.fori_loop(0, GROUP, one, 0)


def inner_step(tissue, angle, potential, sensitivity, interpret=False):
    bricks, nz, cells = potential.shape
    blk3 = lambda: pl.BlockSpec((GROUP, nz, cells), lambda g: (g, 0, 0))
    full = jax.ShapeDtypeStruct((bricks, nz, cells), jnp.float32)
    return pl.pallas_call(
        inner_kernel,
        grid=(bricks // GROUP,),
        in_specs=[blk3(), blk3(), blk3(), blk3()],
        out_specs=[blk3(), blk3(), blk3(), blk3(), pl.BlockSpec((GROUP, 1, 128), lambda g: (g, 0, 0))],
        out_shape=[full, full, full, full, jax.ShapeDtypeStruct((bricks, 1, 128), jnp.float32)],
        compiler_params=pltpu.CompilerParams(dimension_semantics=("parallel",)),
        interpret=interpret,
    )(tissue, angle, potential, sensitivity)


def outer_step(scales, potential, sensitivity, inner, faces, halos, interpret=False):
    bricks, nz, cells = potential.shape
    edge = faces.shape[-1]
    expand = expanders(edge, cells).astype(jnp.bfloat16)
    blk3 = lambda: pl.BlockSpec((GROUP, nz, cells), lambda g: (g, 0, 0))
    lap_u, lap_l, gx, gy, inner_part = inner
    return pl.pallas_call(
        outer_kernel,
        grid=(bricks // GROUP,),
        in_specs=[
            pl.BlockSpec(memory_space=pltpu.SMEM),
            pl.BlockSpec((4, edge, cells), lambda g: (0, 0, 0)),
            blk3(), blk3(), blk3(), blk3(), blk3(), blk3(),
            pl.BlockSpec((GROUP, 1, 128), lambda g: (g, 0, 0)),
            pl.BlockSpec((GROUP, 4, faces.shape[2], edge), lambda g: (g, 0, 0, 0)),
            pl.BlockSpec((GROUP, 6, cells), lambda g: (g, 0, 0)),
        ],
        out_specs=[blk3(), blk3(), pl.BlockSpec((GROUP, 1, 128), lambda g: (g, 0, 0))],
        out_shape=[
            jax.ShapeDtypeStruct((bricks, nz, cells), jnp.float32),
            jax.ShapeDtypeStruct((bricks, nz, cells), jnp.float32),
            jax.ShapeDtypeStruct((bricks, 1, 128), jnp.float32),
        ],
        compiler_params=pltpu.CompilerParams(dimension_semantics=("parallel",)),
        interpret=interpret,
    )(scales, expand, potential, sensitivity, lap_u, lap_l, gx, gy, inner_part, faces, halos)


def body(
    potential, fiber_angle, tissue, sensitivity, conductance, brick_slot, neighbours, brick_cell
):
    bricks, z_layers, plane_cells = potential.shape
    brick_edge = BX
    blocks = lax.axis_size("blk")
    parts = lax.axis_size("par")
    devices = blocks * parts
    capacity = max(4, 8 * bricks // blocks)
    face_count = 4 * bricks
    face_cells = z_layers * brick_edge
    own_cells = conductance.shape[0]
    cell_count = own_cells * devices
    opposite = jnp.array([1, 0, 3, 2], jnp.int32)

    near_slot = brick_slot[neighbours]
    near_blk = (near_slot // bricks).reshape(-1)
    far_key = (near_slot % bricks * 4 + opposite[None, :]).reshape(-1)
    own_key = jnp.arange(face_count, dtype=jnp.int32)
    matches = near_blk[:, None] == near_blk[None, :]
    send_rank = jnp.sum((matches & (own_key[None, :] < own_key[:, None])).astype(jnp.int32), axis=1)
    recv_rank = jnp.sum((matches & (far_key[None, :] < far_key[:, None])).astype(jnp.int32), axis=1)
    send_slot = near_blk * capacity + send_rank
    recv_slot = near_blk * capacity + recv_rank

    adjoint = sensitivity.astype(jnp.float32)
    inner = inner_step(tissue, fiber_angle, potential, sensitivity)
    picker = expanders(brick_edge, plane_cells).reshape(4 * brick_edge, plane_cells).T.astype(jnp.float32)

    def boundary(values):
        picked = jnp.dot(
            values.astype(jnp.float32).reshape(bricks * z_layers, plane_cells),
            picker,
            precision=lax.Precision.HIGHEST,
        )
        return picked.reshape(bricks, z_layers, 4, brick_edge).transpose(0, 2, 1, 3)

    tissue_faces = boundary(tissue)
    cos_faces = jnp.cos(boundary(fiber_angle)) ** 2
    factor_faces = jnp.concatenate(
        [
            ACROSS + (ALONG - ACROSS) * cos_faces[:, :2],
            ACROSS + (ALONG - ACROSS) * (1.0 - cos_faces[:, 2:]),
        ],
        axis=1,
    )
    fields = jnp.stack(
        [tissue_faces * factor_faces, boundary(potential), boundary(sensitivity)], axis=2
    )
    flattened = fields.reshape(face_count, 3 * face_cells)
    outgoing = jnp.zeros((blocks * capacity, 3 * face_cells), jnp.float32).at[send_slot].set(flattened)
    shifted = [conductance] + [
        lax.ppermute(conductance, "par", [(i, (i + s) % parts) for i in range(parts)])
        for s in range(1, parts)
    ]
    source = (lax.axis_index("par") - jnp.arange(parts, dtype=jnp.int32)) % parts
    extra = jnp.concatenate([jnp.stack(shifted)[source].reshape(-1), brick_cell.astype(jnp.float32)])
    width = capacity * 3 * face_cells
    extra_width = -(-extra.shape[0] // 128) * 128
    extra = jnp.pad(extra, (0, extra_width - extra.shape[0]))
    sending = jnp.concatenate(
        [outgoing.reshape(blocks, width), jnp.broadcast_to(extra[None], (blocks, extra_width))], axis=1
    )
    arrived = lax.all_to_all(sending, "blk", split_axis=0, concat_axis=0, tiled=True)
    received = arrived[:, :width]
    par_cells = own_cells * parts
    cond_all = arrived[:, width : width + par_cells].reshape(-1)
    cell_all = arrived[:, width + par_cells : width + par_cells + bricks].reshape(-1).astype(jnp.int32)
    faces = received.reshape(blocks * capacity, 3 * face_cells)[recv_slot].reshape(
        bricks, 4, 3 * z_layers, brick_edge
    )

    size = lax.axis_size("par")
    up = [(i, i + 1) for i in range(size - 1)]
    down = [(j, i) for i, j in up]
    last = jnp.stack([tissue[:, -1].astype(jnp.float32), potential[:, -1], adjoint[:, -1]], axis=1)
    initial = jnp.stack([tissue[:, 0].astype(jnp.float32), potential[:, 0], adjoint[:, 0]], axis=1)
    halos = jnp.concatenate([lax.ppermute(last, "par", up), lax.ppermute(initial, "par", down)], axis=1)

    theta = cond_all[brick_cell]
    theta_near = cond_all[cell_all[near_slot]]
    scales = jnp.concatenate(
        [theta[:, None], theta_near, jnp.zeros((bricks, 3), jnp.float32)], axis=1
    )
    final, adjoint, parts_out = outer_step(scales, potential, sensitivity, inner, faces, halos)
    brick_part = jnp.sum(parts_out, axis=(1, 2))
    onehot_cells = brick_cell[:, None] == jnp.arange(cell_count, dtype=jnp.int32)[None, :]
    shares = jnp.sum(jnp.where(onehot_cells, brick_part[:, None], 0.0), axis=0)
    grad_share = jnp.sum(
        lax.all_to_all(
            shares.reshape(devices, own_cells), ("blk", "par"), split_axis=0, concat_axis=0, tiled=True
        ),
        axis=0,
    )
    cell_gradient = TIMESTEP * grad_share / (conductance * float(BX) ** 1.5)
    return (final, adjoint, cell_gradient)


def solution(mesh):
    placed = (
        P("blk", "par", None),
        P("blk", "par", None),
        P("blk", "par", None),
        P("blk", "par", None),
        P(("blk", "par")),
        P(),
        P("blk", None),
        P("blk"),
    )
    return jax.shard_map(
        body,
        mesh=mesh,
        in_specs=placed,
        out_specs=(P("blk", "par", None), P("blk", "par", None), P(("blk", "par"))),
        check_vma=False,
    )
```

```python
import jax
import jax.numpy as jnp
from jax import lax
from jax.sharding import PartitionSpec as P
from jax.experimental import pallas as pl
from jax.experimental.pallas import tpu as pltpu

BX = 32
STEPS = 1


TIMESTEP = 0.12
THRESHOLD = 0.2
ACROSS = 0.3
ALONG = 1.0
VERTICAL = 0.6


def extended(x, sides, width):
    for axis, dim in sides:
        size, length = (lax.axis_size(axis), x.shape[dim])
        up = [(i, (i + 1) % size) for i in range(size - 1)]
        down = [(j, i) for i, j in up]
        last = lax.slice_in_dim(x, length - width, length, axis=dim)
        initial = lax.slice_in_dim(x, 0, width, axis=dim)
        before = lax.ppermute(last, axis, up)
        after = lax.ppermute(initial, axis, down)
        x = jnp.concatenate([before, x, after], axis=dim)
    return x


def layers(values, brick_edge):
    return jnp.stack(
        [
            values[..., :brick_edge],
            values[..., -brick_edge:],
            values[..., 0::brick_edge],
            values[..., brick_edge - 1 :: brick_edge],
        ],
        axis=1,
    )


def along_x(values, lower_face, upper_face, brick_edge):
    return (
        jnp.concatenate([lower_face, values[..., :-brick_edge]], -1),
        jnp.concatenate([values[..., brick_edge:], upper_face], -1),
    )


def along_y(values, lower_face, upper_face, brick_edge):
    y_index = jnp.arange(values.shape[-1]) % brick_edge
    zero_pad = jnp.zeros(values.shape[:-1] + (1,), values.dtype)
    shifted_down = jnp.concatenate([zero_pad, values[..., :-1]], -1)
    shifted_up = jnp.concatenate([values[..., 1:], zero_pad], -1)
    return (
        jnp.where(y_index == 0, jnp.repeat(lower_face, brick_edge, axis=-1), shifted_down),
        jnp.where(
            y_index == brick_edge - 1, jnp.repeat(upper_face, brick_edge, axis=-1), shifted_up
        ),
    )


def near_values(values, layer_set, padded, brick_edge):
    x_low, x_high = along_x(values, layer_set[:, 0], layer_set[:, 1], brick_edge)
    y_low, y_high = along_y(values, layer_set[:, 2], layer_set[:, 3], brick_edge)
    return (x_low, x_high, y_low, y_high, padded[:, :-2], padded[:, 2:])


def laplace(conduct, values, beside):
    summed = conduct[0] * (beside[0] - values)
    for facet in range(1, 6):
        summed = summed + conduct[facet] * (beside[facet] - values)
    return summed


def brick_terms(conduct, adjoint, beside_adjoint, earlier, beside_state):
    summed = -conduct[0] * (adjoint - beside_adjoint[0]) * (earlier - beside_state[0])
    for facet in range(1, 6):
        summed = summed - conduct[facet] * (adjoint - beside_adjoint[facet]) * (
            earlier - beside_state[facet]
        )
    return jnp.sum(summed, axis=(1, 2))


def weights(tissue, fiber_angle, brick_scale):
    present = tissue.astype(jnp.float32)
    cos_square = jnp.cos(fiber_angle.astype(jnp.float32)) ** 2
    weight_x = present * brick_scale * (ACROSS + (ALONG - ACROSS) * cos_square)
    weight_y = present * brick_scale * (ACROSS + (ALONG - ACROSS) * (1.0 - cos_square))
    weight_z = present * brick_scale * VERTICAL
    return (weight_x, weight_y, weight_z)


def conductances(weight_x, weight_y, weight_z, weight_near, padded_z, brick_edge):
    x_low, x_high = along_x(weight_x, weight_near[:, 0], weight_near[:, 1], brick_edge)
    y_low, y_high = along_y(weight_y, weight_near[:, 2], weight_near[:, 3], brick_edge)
    return (
        weight_x * x_low,
        weight_x * x_high,
        weight_y * y_low,
        weight_y * y_high,
        weight_z * padded_z[:, :-2],
        weight_z * padded_z[:, 2:],
    )


GROUP = 8


def expanders(edge, cells):
    lane = jnp.arange(cells, dtype=jnp.int32)[None, :]
    k = jnp.arange(edge, dtype=jnp.int32)[:, None]
    return jnp.stack(
        [lane == k, lane == cells - edge + k, lane == edge * k, lane == edge * k + edge - 1]
    )


def cell_kernel(scale_ref, expand_ref, tissue_ref, angle_ref, u_ref, l_ref, face_ref, halo_ref,
                u_out, l_out, part_out):
    g = pl.program_id(0)
    nz, cells = u_ref.shape[1], u_ref.shape[2]
    edge = face_ref.shape[-1]
    lane = lax.broadcasted_iota(jnp.int32, (nz, cells), 1)
    row = lax.broadcasted_iota(jnp.int32, (nz, cells), 0)
    ycoord = lane % edge
    masks = (lane < edge, lane >= cells - edge, ycoord == 0, ycoord == edge - 1)
    shifts = (edge, cells - edge, 1, cells - 1)
    zlo = row == 0
    zhi = row == nz - 1

    def one(i, carry):
        b = g * GROUP + i
        th = scale_ref[b, 0]
        present = tissue_ref[i].astype(jnp.float32)
        c = jnp.cos(angle_ref[i].astype(jnp.float32))
        c2 = c * c
        scaled = present * th
        wx = scaled * (ACROSS + (ALONG - ACROSS) * c2)
        wy = scaled * (ACROSS + (ALONG - ACROSS) * (1.0 - c2))
        wz = scaled * VERTICAL
        u = u_ref[i]
        l = l_ref[i].astype(jnp.float32)
        halo = halo_ref[i]
        conds, ub, lb = [], [], []
        for f in range(4):
            face = face_ref[i, f]
            high = face.astype(jnp.bfloat16)
            rest = face - high.astype(jnp.float32)
            middle = rest.astype(jnp.bfloat16)
            low = (rest - middle.astype(jnp.float32)).astype(jnp.bfloat16)
            ext = jnp.dot(high, expand_ref[f], preferred_element_type=jnp.float32)
            ext = ext + jnp.dot(middle, expand_ref[f], preferred_element_type=jnp.float32)
            ext = ext + jnp.dot(low, expand_ref[f], preferred_element_type=jnp.float32)
            w_self = wx if f < 2 else wy
            w_near = jnp.where(masks[f], scale_ref[b, 1 + f] * ext[:nz], pltpu.roll(w_self, shifts[f], 1))
            conds.append(w_self * w_near)
            ub.append(jnp.where(masks[f], ext[nz:2 * nz], pltpu.roll(u, shifts[f], 1)))
            lb.append(jnp.where(masks[f], ext[2 * nz:3 * nz], pltpu.roll(l, shifts[f], 1)))
        wz_lo = jnp.where(zlo, (halo[0:1] * th) * VERTICAL, pltpu.roll(wz, 1, 0))
        wz_hi = jnp.where(zhi, (halo[3:4] * th) * VERTICAL, pltpu.roll(wz, nz - 1, 0))
        conds += [wz * wz_lo, wz * wz_hi]
        ub += [jnp.where(zlo, halo[1:2], pltpu.roll(u, 1, 0)), jnp.where(zhi, halo[4:5], pltpu.roll(u, nz - 1, 0))]
        lb += [jnp.where(zlo, halo[2:3], pltpu.roll(l, 1, 0)), jnp.where(zhi, halo[5:6], pltpu.roll(l, nz - 1, 0))]
        lap_u = conds[0] * (ub[0] - u)
        lap_l = conds[0] * (lb[0] - l)
        terms = lap_l * (ub[0] - u)
        for k in range(1, 6):
            step_u = ub[k] - u
            step_l = conds[k] * (lb[k] - l)
            lap_u = lap_u + conds[k] * step_u
            lap_l = lap_l + step_l
            terms = terms + step_l * step_u
        ionic = u * (1.0 - u) * (u - THRESHOLD)
        slope = -3.0 * u * u + 2.0 * (1.0 + THRESHOLD) * u - THRESHOLD
        u_out[i] = u + TIMESTEP * (lap_u + ionic)
        l_out[i] = l + TIMESTEP * (lap_l + slope * l)
        col = -jnp.sum(terms, axis=0, keepdims=True)
        acc = col[:, 0:128]
        for t in range(1, cells // 128):
            acc = acc + col[:, t * 128:(t + 1) * 128]
        part_out[i] = acc
        return carry

    lax.fori_loop(0, GROUP, one, 0)


def cell_step(scales, tissue, angle, potential, sensitivity, faces, halos, interpret=False):
    bricks, nz, cells = potential.shape
    edge = faces.shape[-1]
    expand = expanders(edge, cells).astype(jnp.bfloat16)
    blk3 = lambda: pl.BlockSpec((GROUP, nz, cells), lambda g: (g, 0, 0))
    return pl.pallas_call(
        cell_kernel,
        grid=(bricks // GROUP,),
        in_specs=[
            pl.BlockSpec(memory_space=pltpu.SMEM),
            pl.BlockSpec((4, edge, cells), lambda g: (0, 0, 0)),
            blk3(), blk3(), blk3(), blk3(),
            pl.BlockSpec((GROUP, 4, faces.shape[2], edge), lambda g: (g, 0, 0, 0)),
            pl.BlockSpec((GROUP, 6, cells), lambda g: (g, 0, 0)),
        ],
        out_specs=[blk3(), blk3(), pl.BlockSpec((GROUP, 1, 128), lambda g: (g, 0, 0))],
        out_shape=[
            jax.ShapeDtypeStruct((bricks, nz, cells), jnp.float32),
            jax.ShapeDtypeStruct((bricks, nz, cells), jnp.float32),
            jax.ShapeDtypeStruct((bricks, 1, 128), jnp.float32),
        ],
        compiler_params=pltpu.CompilerParams(dimension_semantics=("parallel",)),
        interpret=interpret,
    )(scales, expand, tissue, angle, potential, sensitivity, faces, halos)


def group_sum(values):
    col = jnp.sum(values, axis=0, keepdims=True)
    acc = col[:, 0:128]
    for t in range(1, values.shape[1] // 128):
        acc = acc + col[:, t * 128:(t + 1) * 128]
    return acc


def inner_kernel(tissue_ref, angle_ref, u_ref, l_ref, lu_out, ll_out, gx_out, gy_out, part_out):
    nz, cells = u_ref.shape[1], u_ref.shape[2]
    edge = BX
    lane = lax.broadcasted_iota(jnp.int32, (nz, cells), 1)
    row = lax.broadcasted_iota(jnp.int32, (nz, cells), 0)
    ycoord = lane % edge
    inside = (lane >= edge, lane < cells - edge, ycoord != 0, ycoord != edge - 1, row != 0, row != nz - 1)
    shifts = ((edge, 1), (cells - edge, 1), (1, 1), (cells - 1, 1), (1, 0), (nz - 1, 0))

    def one(i, carry):
        present = tissue_ref[i].astype(jnp.float32)
        c = jnp.cos(angle_ref[i].astype(jnp.float32))
        c2 = c * c
        gx = present * (ACROSS + (ALONG - ACROSS) * c2)
        gy = present * (ACROSS + (ALONG - ACROSS) * (1.0 - c2))
        gz = present * VERTICAL
        u = u_ref[i]
        l = l_ref[i].astype(jnp.float32)
        lap_u = jnp.zeros_like(u)
        lap_l = jnp.zeros_like(u)
        terms = jnp.zeros_like(u)
        for k in range(6):
            g = gx if k < 2 else (gy if k < 4 else gz)
            shift, axis = shifts[k]
            conduct = jnp.where(inside[k], g * pltpu.roll(g, shift, axis), 0.0)
            step_u = pltpu.roll(u, shift, axis) - u
            step_l = conduct * (pltpu.roll(l, shift, axis) - l)
            lap_u = lap_u + conduct * step_u
            lap_l = lap_l + step_l
            terms = terms + step_l * step_u
        lu_out[i] = lap_u
        ll_out[i] = lap_l
        gx_out[i] = gx
        gy_out[i] = gy
        part_out[i] = group_sum(terms)
        return carry

    lax.fori_loop(0, GROUP, one, 0)


def outer_kernel(scale_ref, expand_ref, u_ref, l_ref, lu_ref, ll_ref, gx_ref, gy_ref, inner_ref, face_ref,
                 halo_ref, u_out, l_out, part_out, ext_ref):
    g = pl.program_id(0)
    nz, cells = u_ref.shape[1], u_ref.shape[2]
    edge = BX
    rows = 8 * nz
    for f in range(4):
        face = face_ref[:, f]
        part = face[:, :2 * nz]
        high = part.astype(jnp.bfloat16).astype(jnp.float32)
        rest = part - high
        middle = rest.astype(jnp.bfloat16).astype(jnp.float32)
        low = (rest - middle).astype(jnp.bfloat16).astype(jnp.float32)
        stacked = jnp.concatenate(
            [high, middle, low, face[:, 2 * nz:3 * nz], jnp.zeros_like(face[:, :nz])], axis=1
        )
        ext_ref[f] = jnp.dot(
            stacked.reshape(GROUP * rows, edge).astype(jnp.bfloat16),
            expand_ref[f],
            preferred_element_type=jnp.float32,
        )
    lane = lax.broadcasted_iota(jnp.int32, (nz, cells), 1)
    row = lax.broadcasted_iota(jnp.int32, (nz, cells), 0)
    ycoord = lane % edge
    masks = (lane < edge, lane >= cells - edge, ycoord == 0, ycoord == edge - 1)

    def one(i, carry):
        b = g * GROUP + i
        th = scale_ref[b, 0]
        u = u_ref[i]
        l = l_ref[i].astype(jnp.float32)
        gx = gx_ref[i]
        gy = gy_ref[i]
        halo = halo_ref[i]
        edge_u, edge_l, edge_t = [], [], []
        for side, r in ((0, 0), (1, nz - 1)):
            own_z = (gx[r:r + 1] != 0.0).astype(jnp.float32) * VERTICAL
            conduct = own_z * (halo[3 * side:3 * side + 1] * VERTICAL)
            step_u = halo[3 * side + 1:3 * side + 2] - u[r:r + 1]
            step_l = conduct * (halo[3 * side + 2:3 * side + 3] - l[r:r + 1])
            edge_u.append(conduct * step_u)
            edge_l.append(step_l)
            edge_t.append(step_l * step_u)
        lap_u = lu_ref[i] + jnp.where(row == 0, edge_u[0], 0.0) + jnp.where(row == nz - 1, edge_u[1], 0.0)
        lap_l = ll_ref[i] + jnp.where(row == 0, edge_l[0], 0.0) + jnp.where(row == nz - 1, edge_l[1], 0.0)
        inner = inner_ref[i] + group_sum(edge_t[0]) + group_sum(edge_t[1])
        face_u = jnp.zeros_like(u)
        face_l = jnp.zeros_like(u)
        face_t = jnp.zeros_like(u)
        for f in range(4):
            ext = ext_ref[f, pl.ds(pl.multiple_of(i * rows, rows), rows), :]
            near_w = (ext[0:nz] + ext[2 * nz:3 * nz]) + ext[4 * nz:5 * nz]
            near_u = (ext[nz:2 * nz] + ext[3 * nz:4 * nz]) + ext[5 * nz:6 * nz]
            near_l = ext[6 * nz:7 * nz]
            g_self = gx if f < 2 else gy
            conduct = jnp.where(masks[f], scale_ref[b, 1 + f] * (g_self * near_w), 0.0)
            step_u = near_u - u
            step_l = conduct * (near_l - l)
            face_u = face_u + conduct * step_u
            face_l = face_l + step_l
            face_t = face_t + step_l * step_u
        square = th * th
        ionic = u * (1.0 - u) * (u - THRESHOLD)
        slope = -3.0 * u * u + 2.0 * (1.0 + THRESHOLD) * u - THRESHOLD
        u_out[i] = u + TIMESTEP * ((square * lap_u + th * face_u) + ionic)
        l_out[i] = l + TIMESTEP * ((square * lap_l + th * face_l) + slope * l)
        part_out[i] = -(square * inner + th * group_sum(face_t))
        return carry

    lax.fori_loop(0, GROUP, one, 0)


def inner_step(tissue, angle, potential, sensitivity, interpret=False):
    bricks, nz, cells = potential.shape
    blk3 = lambda: pl.BlockSpec((GROUP, nz, cells), lambda g: (g, 0, 0))
    full = jax.ShapeDtypeStruct((bricks, nz, cells), jnp.float32)
    return pl.pallas_call(
        inner_kernel,
        grid=(bricks // GROUP,),
        in_specs=[blk3(), blk3(), blk3(), blk3()],
        out_specs=[blk3(), blk3(), blk3(), blk3(), pl.BlockSpec((GROUP, 1, 128), lambda g: (g, 0, 0))],
        out_shape=[full, full, full, full, jax.ShapeDtypeStruct((bricks, 1, 128), jnp.float32)],
        compiler_params=pltpu.CompilerParams(dimension_semantics=("parallel",)),
        interpret=interpret,
    )(tissue, angle, potential, sensitivity)


def outer_step(scales, potential, sensitivity, inner, faces, halos, interpret=False):
    bricks, nz, cells = potential.shape
    edge = faces.shape[-1]
    expand = expanders(edge, cells).astype(jnp.bfloat16)
    blk3 = lambda: pl.BlockSpec((GROUP, nz, cells), lambda g: (g, 0, 0))
    lap_u, lap_l, gx, gy, inner_part = inner
    return pl.pallas_call(
        outer_kernel,
        grid=(bricks // GROUP,),
        in_specs=[
            pl.BlockSpec(memory_space=pltpu.SMEM),
            pl.BlockSpec((4, edge, cells), lambda g: (0, 0, 0)),
            blk3(), blk3(), blk3(), blk3(), blk3(), blk3(),
            pl.BlockSpec((GROUP, 1, 128), lambda g: (g, 0, 0)),
            pl.BlockSpec((GROUP, 4, faces.shape[2], edge), lambda g: (g, 0, 0, 0)),
            pl.BlockSpec((GROUP, 6, cells), lambda g: (g, 0, 0)),
        ],
        out_specs=[blk3(), blk3(), pl.BlockSpec((GROUP, 1, 128), lambda g: (g, 0, 0))],
        out_shape=[
            jax.ShapeDtypeStruct((bricks, nz, cells), jnp.float32),
            jax.ShapeDtypeStruct((bricks, nz, cells), jnp.float32),
            jax.ShapeDtypeStruct((bricks, 1, 128), jnp.float32),
        ],
        scratch_shapes=[pltpu.VMEM((4, GROUP * 8 * nz, cells), jnp.float32)],
        compiler_params=pltpu.CompilerParams(dimension_semantics=("parallel",)),
        interpret=interpret,
    )(scales, expand, potential, sensitivity, lap_u, lap_l, gx, gy, inner_part, faces, halos)


def body(
    potential, fiber_angle, tissue, sensitivity, conductance, brick_slot, neighbours, brick_cell
):
    bricks, z_layers, plane_cells = potential.shape
    brick_edge = BX
    blocks = lax.axis_size("blk")
    parts = lax.axis_size("par")
    devices = blocks * parts
    capacity = max(4, 8 * bricks // blocks)
    face_count = 4 * bricks
    face_cells = z_layers * brick_edge
    own_cells = conductance.shape[0]
    cell_count = own_cells * devices
    opposite = jnp.array([1, 0, 3, 2], jnp.int32)

    near_slot = brick_slot[neighbours]
    near_blk = (near_slot // bricks).reshape(-1)
    far_key = (near_slot % bricks * 4 + opposite[None, :]).reshape(-1)
    own_key = jnp.arange(face_count, dtype=jnp.int32)
    matches = near_blk[:, None] == near_blk[None, :]
    send_rank = jnp.sum((matches & (own_key[None, :] < own_key[:, None])).astype(jnp.int32), axis=1)
    recv_rank = jnp.sum((matches & (far_key[None, :] < far_key[:, None])).astype(jnp.int32), axis=1)
    send_slot = near_blk * capacity + send_rank
    recv_slot = near_blk * capacity + recv_rank

    adjoint = sensitivity.astype(jnp.float32)
    inner = inner_step(tissue, fiber_angle, potential, sensitivity)
    picker = expanders(brick_edge, plane_cells).reshape(4 * brick_edge, plane_cells).T.astype(jnp.float32)

    def boundary(values):
        picked = jnp.dot(
            values.astype(jnp.float32).reshape(bricks * z_layers, plane_cells),
            picker,
            precision=lax.Precision.HIGHEST,
        )
        return picked.reshape(bricks, z_layers, 4, brick_edge).transpose(0, 2, 1, 3)

    tissue_faces = boundary(tissue)
    cos_faces = jnp.cos(boundary(fiber_angle)) ** 2
    factor_faces = jnp.concatenate(
        [
            ACROSS + (ALONG - ACROSS) * cos_faces[:, :2],
            ACROSS + (ALONG - ACROSS) * (1.0 - cos_faces[:, 2:]),
        ],
        axis=1,
    )
    fields = jnp.stack(
        [tissue_faces * factor_faces, boundary(potential), boundary(sensitivity)], axis=2
    )
    flattened = fields.reshape(face_count, 3 * face_cells)
    outgoing = jnp.zeros((blocks * capacity, 3 * face_cells), jnp.float32).at[send_slot].set(flattened)
    shifted = [conductance] + [
        lax.ppermute(conductance, "par", [(i, (i + s) % parts) for i in range(parts)])
        for s in range(1, parts)
    ]
    source = (lax.axis_index("par") - jnp.arange(parts, dtype=jnp.int32)) % parts
    extra = jnp.concatenate([jnp.stack(shifted)[source].reshape(-1), brick_cell.astype(jnp.float32)])
    width = capacity * 3 * face_cells
    extra_width = -(-extra.shape[0] // 128) * 128
    extra = jnp.pad(extra, (0, extra_width - extra.shape[0]))
    sending = jnp.concatenate(
        [outgoing.reshape(blocks, width), jnp.broadcast_to(extra[None], (blocks, extra_width))], axis=1
    )
    arrived = lax.all_to_all(sending, "blk", split_axis=0, concat_axis=0, tiled=True)
    received = arrived[:, :width]
    par_cells = own_cells * parts
    cond_all = arrived[:, width : width + par_cells].reshape(-1)
    cell_all = arrived[:, width + par_cells : width + par_cells + bricks].reshape(-1).astype(jnp.int32)
    faces = received.reshape(blocks * capacity, 3 * face_cells)[recv_slot].reshape(
        bricks, 4, 3 * z_layers, brick_edge
    )

    size = lax.axis_size("par")
    up = [(i, i + 1) for i in range(size - 1)]
    down = [(j, i) for i, j in up]
    last = jnp.stack([tissue[:, -1].astype(jnp.float32), potential[:, -1], adjoint[:, -1]], axis=1)
    initial = jnp.stack([tissue[:, 0].astype(jnp.float32), potential[:, 0], adjoint[:, 0]], axis=1)
    halos = jnp.concatenate([lax.ppermute(last, "par", up), lax.ppermute(initial, "par", down)], axis=1)

    theta = cond_all[brick_cell]
    theta_near = cond_all[cell_all[near_slot]]
    scales = jnp.concatenate(
        [theta[:, None], theta_near, jnp.zeros((bricks, 3), jnp.float32)], axis=1
    )
    final, adjoint, parts_out = outer_step(scales, potential, sensitivity, inner, faces, halos)
    brick_part = jnp.sum(parts_out, axis=(1, 2))
    onehot_cells = brick_cell[:, None] == jnp.arange(cell_count, dtype=jnp.int32)[None, :]
    shares = jnp.sum(jnp.where(onehot_cells, brick_part[:, None], 0.0), axis=0)
    grad_share = jnp.sum(
        lax.all_to_all(
            shares.reshape(devices, own_cells), ("blk", "par"), split_axis=0, concat_axis=0, tiled=True
        ),
        axis=0,
    )
    cell_gradient = TIMESTEP * grad_share / (conductance * float(BX) ** 1.5)
    return (final, adjoint, cell_gradient)


def solution(mesh):
    placed = (
        P("blk", "par", None),
        P("blk", "par", None),
        P("blk", "par", None),
        P("blk", "par", None),
        P(("blk", "par")),
        P(),
        P("blk", None),
        P("blk"),
    )
    return jax.shard_map(
        body,
        mesh=mesh,
        in_specs=placed,
        out_specs=(P("blk", "par", None), P("blk", "par", None), P(("blk", "par"))),
        check_vma=False,
    )
```

```python
import jax
import jax.numpy as jnp
from jax import lax
from jax.sharding import PartitionSpec as P
from jax.experimental import pallas as pl
from jax.experimental.pallas import tpu as pltpu

BX = 32
STEPS = 1


TIMESTEP = 0.12
THRESHOLD = 0.2
ACROSS = 0.3
ALONG = 1.0
VERTICAL = 0.6


def extended(x, sides, width):
    for axis, dim in sides:
        size, length = (lax.axis_size(axis), x.shape[dim])
        up = [(i, (i + 1) % size) for i in range(size - 1)]
        down = [(j, i) for i, j in up]
        last = lax.slice_in_dim(x, length - width, length, axis=dim)
        initial = lax.slice_in_dim(x, 0, width, axis=dim)
        before = lax.ppermute(last, axis, up)
        after = lax.ppermute(initial, axis, down)
        x = jnp.concatenate([before, x, after], axis=dim)
    return x


def layers(values, brick_edge):
    return jnp.stack(
        [
            values[..., :brick_edge],
            values[..., -brick_edge:],
            values[..., 0::brick_edge],
            values[..., brick_edge - 1 :: brick_edge],
        ],
        axis=1,
    )


def along_x(values, lower_face, upper_face, brick_edge):
    return (
        jnp.concatenate([lower_face, values[..., :-brick_edge]], -1),
        jnp.concatenate([values[..., brick_edge:], upper_face], -1),
    )


def along_y(values, lower_face, upper_face, brick_edge):
    y_index = jnp.arange(values.shape[-1]) % brick_edge
    zero_pad = jnp.zeros(values.shape[:-1] + (1,), values.dtype)
    shifted_down = jnp.concatenate([zero_pad, values[..., :-1]], -1)
    shifted_up = jnp.concatenate([values[..., 1:], zero_pad], -1)
    return (
        jnp.where(y_index == 0, jnp.repeat(lower_face, brick_edge, axis=-1), shifted_down),
        jnp.where(
            y_index == brick_edge - 1, jnp.repeat(upper_face, brick_edge, axis=-1), shifted_up
        ),
    )


def near_values(values, layer_set, padded, brick_edge):
    x_low, x_high = along_x(values, layer_set[:, 0], layer_set[:, 1], brick_edge)
    y_low, y_high = along_y(values, layer_set[:, 2], layer_set[:, 3], brick_edge)
    return (x_low, x_high, y_low, y_high, padded[:, :-2], padded[:, 2:])


def laplace(conduct, values, beside):
    summed = conduct[0] * (beside[0] - values)
    for facet in range(1, 6):
        summed = summed + conduct[facet] * (beside[facet] - values)
    return summed


def brick_terms(conduct, adjoint, beside_adjoint, earlier, beside_state):
    summed = -conduct[0] * (adjoint - beside_adjoint[0]) * (earlier - beside_state[0])
    for facet in range(1, 6):
        summed = summed - conduct[facet] * (adjoint - beside_adjoint[facet]) * (
            earlier - beside_state[facet]
        )
    return jnp.sum(summed, axis=(1, 2))


def weights(tissue, fiber_angle, brick_scale):
    present = tissue.astype(jnp.float32)
    cos_square = jnp.cos(fiber_angle.astype(jnp.float32)) ** 2
    weight_x = present * brick_scale * (ACROSS + (ALONG - ACROSS) * cos_square)
    weight_y = present * brick_scale * (ACROSS + (ALONG - ACROSS) * (1.0 - cos_square))
    weight_z = present * brick_scale * VERTICAL
    return (weight_x, weight_y, weight_z)


def conductances(weight_x, weight_y, weight_z, weight_near, padded_z, brick_edge):
    x_low, x_high = along_x(weight_x, weight_near[:, 0], weight_near[:, 1], brick_edge)
    y_low, y_high = along_y(weight_y, weight_near[:, 2], weight_near[:, 3], brick_edge)
    return (
        weight_x * x_low,
        weight_x * x_high,
        weight_y * y_low,
        weight_y * y_high,
        weight_z * padded_z[:, :-2],
        weight_z * padded_z[:, 2:],
    )


GROUP = 8


def expanders(edge, cells):
    lane = jnp.arange(cells, dtype=jnp.int32)[None, :]
    k = jnp.arange(edge, dtype=jnp.int32)[:, None]
    return jnp.stack(
        [lane == k, lane == cells - edge + k, lane == edge * k, lane == edge * k + edge - 1]
    )


def cell_kernel(scale_ref, expand_ref, tissue_ref, angle_ref, u_ref, l_ref, face_ref, halo_ref,
                u_out, l_out, part_out):
    g = pl.program_id(0)
    nz, cells = u_ref.shape[1], u_ref.shape[2]
    edge = face_ref.shape[-1]
    lane = lax.broadcasted_iota(jnp.int32, (nz, cells), 1)
    row = lax.broadcasted_iota(jnp.int32, (nz, cells), 0)
    ycoord = lane % edge
    masks = (lane < edge, lane >= cells - edge, ycoord == 0, ycoord == edge - 1)
    shifts = (edge, cells - edge, 1, cells - 1)
    zlo = row == 0
    zhi = row == nz - 1

    def one(i, carry):
        b = g * GROUP + i
        th = scale_ref[b, 0]
        present = tissue_ref[i].astype(jnp.float32)
        c = jnp.cos(angle_ref[i].astype(jnp.float32))
        c2 = c * c
        scaled = present * th
        wx = scaled * (ACROSS + (ALONG - ACROSS) * c2)
        wy = scaled * (ACROSS + (ALONG - ACROSS) * (1.0 - c2))
        wz = scaled * VERTICAL
        u = u_ref[i]
        l = l_ref[i].astype(jnp.float32)
        halo = halo_ref[i]
        conds, ub, lb = [], [], []
        for f in range(4):
            face = face_ref[i, f]
            high = face.astype(jnp.bfloat16)
            rest = face - high.astype(jnp.float32)
            middle = rest.astype(jnp.bfloat16)
            low = (rest - middle.astype(jnp.float32)).astype(jnp.bfloat16)
            ext = jnp.dot(high, expand_ref[f], preferred_element_type=jnp.float32)
            ext = ext + jnp.dot(middle, expand_ref[f], preferred_element_type=jnp.float32)
            ext = ext + jnp.dot(low, expand_ref[f], preferred_element_type=jnp.float32)
            w_self = wx if f < 2 else wy
            w_near = jnp.where(masks[f], scale_ref[b, 1 + f] * ext[:nz], pltpu.roll(w_self, shifts[f], 1))
            conds.append(w_self * w_near)
            ub.append(jnp.where(masks[f], ext[nz:2 * nz], pltpu.roll(u, shifts[f], 1)))
            lb.append(jnp.where(masks[f], ext[2 * nz:3 * nz], pltpu.roll(l, shifts[f], 1)))
        wz_lo = jnp.where(zlo, (halo[0:1] * th) * VERTICAL, pltpu.roll(wz, 1, 0))
        wz_hi = jnp.where(zhi, (halo[3:4] * th) * VERTICAL, pltpu.roll(wz, nz - 1, 0))
        conds += [wz * wz_lo, wz * wz_hi]
        ub += [jnp.where(zlo, halo[1:2], pltpu.roll(u, 1, 0)), jnp.where(zhi, halo[4:5], pltpu.roll(u, nz - 1, 0))]
        lb += [jnp.where(zlo, halo[2:3], pltpu.roll(l, 1, 0)), jnp.where(zhi, halo[5:6], pltpu.roll(l, nz - 1, 0))]
        lap_u = conds[0] * (ub[0] - u)
        lap_l = conds[0] * (lb[0] - l)
        terms = lap_l * (ub[0] - u)
        for k in range(1, 6):
            step_u = ub[k] - u
            step_l = conds[k] * (lb[k] - l)
            lap_u = lap_u + conds[k] * step_u
            lap_l = lap_l + step_l
            terms = terms + step_l * step_u
        ionic = u * (1.0 - u) * (u - THRESHOLD)
        slope = -3.0 * u * u + 2.0 * (1.0 + THRESHOLD) * u - THRESHOLD
        u_out[i] = u + TIMESTEP * (lap_u + ionic)
        l_out[i] = l + TIMESTEP * (lap_l + slope * l)
        col = -jnp.sum(terms, axis=0, keepdims=True)
        acc = col[:, 0:128]
        for t in range(1, cells // 128):
            acc = acc + col[:, t * 128:(t + 1) * 128]
        part_out[i] = acc
        return carry

    lax.fori_loop(0, GROUP, one, 0)


def cell_step(scales, tissue, angle, potential, sensitivity, faces, halos, interpret=False):
    bricks, nz, cells = potential.shape
    edge = faces.shape[-1]
    expand = expanders(edge, cells).astype(jnp.bfloat16)
    blk3 = lambda: pl.BlockSpec((GROUP, nz, cells), lambda g: (g, 0, 0))
    return pl.pallas_call(
        cell_kernel,
        grid=(bricks // GROUP,),
        in_specs=[
            pl.BlockSpec(memory_space=pltpu.SMEM),
            pl.BlockSpec((4, edge, cells), lambda g: (0, 0, 0)),
            blk3(), blk3(), blk3(), blk3(),
            pl.BlockSpec((GROUP, 4, faces.shape[2], edge), lambda g: (g, 0, 0, 0)),
            pl.BlockSpec((GROUP, 6, cells), lambda g: (g, 0, 0)),
        ],
        out_specs=[blk3(), blk3(), pl.BlockSpec((GROUP, 1, 128), lambda g: (g, 0, 0))],
        out_shape=[
            jax.ShapeDtypeStruct((bricks, nz, cells), jnp.float32),
            jax.ShapeDtypeStruct((bricks, nz, cells), jnp.float32),
            jax.ShapeDtypeStruct((bricks, 1, 128), jnp.float32),
        ],
        compiler_params=pltpu.CompilerParams(dimension_semantics=("parallel",)),
        interpret=interpret,
    )(scales, expand, tissue, angle, potential, sensitivity, faces, halos)


def group_sum(values):
    col = jnp.sum(values, axis=0, keepdims=True)
    acc = col[:, 0:128]
    for t in range(1, values.shape[1] // 128):
        acc = acc + col[:, t * 128:(t + 1) * 128]
    return acc


def inner_kernel(tissue_ref, angle_ref, u_ref, l_ref, lu_out, ll_out, gx_out, gy_out, part_out):
    nz, cells = u_ref.shape[1], u_ref.shape[2]
    edge = BX
    lane = lax.broadcasted_iota(jnp.int32, (nz, cells), 1)
    row = lax.broadcasted_iota(jnp.int32, (nz, cells), 0)
    ycoord = lane % edge
    inside = (lane >= edge, lane < cells - edge, ycoord != 0, ycoord != edge - 1, row != 0, row != nz - 1)
    shifts = ((edge, 1), (cells - edge, 1), (1, 1), (cells - 1, 1), (1, 0), (nz - 1, 0))

    def one(i, carry):
        present = tissue_ref[i].astype(jnp.float32)
        c = jnp.cos(angle_ref[i].astype(jnp.float32))
        c2 = c * c
        gx = present * (ACROSS + (ALONG - ACROSS) * c2)
        gy = present * (ACROSS + (ALONG - ACROSS) * (1.0 - c2))
        gz = present * VERTICAL
        u = u_ref[i]
        l = l_ref[i].astype(jnp.float32)
        lap_u = jnp.zeros_like(u)
        lap_l = jnp.zeros_like(u)
        terms = jnp.zeros_like(u)
        for k in range(6):
            g = gx if k < 2 else (gy if k < 4 else gz)
            shift, axis = shifts[k]
            conduct = jnp.where(inside[k], g * pltpu.roll(g, shift, axis), 0.0)
            step_u = pltpu.roll(u, shift, axis) - u
            step_l = conduct * (pltpu.roll(l, shift, axis) - l)
            lap_u = lap_u + conduct * step_u
            lap_l = lap_l + step_l
            terms = terms + step_l * step_u
        lu_out[i] = lap_u
        ll_out[i] = lap_l
        gx_out[i] = gx
        gy_out[i] = gy
        part_out[i] = group_sum(terms)
        return carry

    lax.fori_loop(0, GROUP, one, 0)


def outer_kernel(cond_ref, cell_ref, own_ref, near_ref, expand_ref, u_ref, l_ref, lu_ref, ll_ref, gx_ref, gy_ref, inner_ref, face_ref,
                 halo_ref, u_out, l_out, part_out, ext_ref):
    g = pl.program_id(0)
    nz, cells = u_ref.shape[1], u_ref.shape[2]
    edge = BX
    rows = 8 * nz
    for f in range(4):
        face = face_ref[:, f]
        part = face[:, :2 * nz]
        high = part.astype(jnp.bfloat16).astype(jnp.float32)
        rest = part - high
        middle = rest.astype(jnp.bfloat16).astype(jnp.float32)
        low = (rest - middle).astype(jnp.bfloat16).astype(jnp.float32)
        stacked = jnp.concatenate(
            [high, middle, low, face[:, 2 * nz:3 * nz], jnp.zeros_like(face[:, :nz])], axis=1
        )
        ext_ref[f] = jnp.dot(
            stacked.reshape(GROUP * rows, edge).astype(jnp.bfloat16),
            expand_ref[f],
            preferred_element_type=jnp.float32,
        )
    lane = lax.broadcasted_iota(jnp.int32, (nz, cells), 1)
    row = lax.broadcasted_iota(jnp.int32, (nz, cells), 0)
    ycoord = lane % edge
    masks = (lane < edge, lane >= cells - edge, ycoord == 0, ycoord == edge - 1)

    def one(i, carry):
        b = g * GROUP + i
        th = cond_ref[own_ref[b]]
        u = u_ref[i]
        l = l_ref[i].astype(jnp.float32)
        gx = gx_ref[i]
        gy = gy_ref[i]
        halo = halo_ref[i]
        edge_u, edge_l, edge_t = [], [], []
        for side, r in ((0, 0), (1, nz - 1)):
            own_z = (gx[r:r + 1] != 0.0).astype(jnp.float32) * VERTICAL
            conduct = own_z * (halo[3 * side:3 * side + 1] * VERTICAL)
            step_u = halo[3 * side + 1:3 * side + 2] - u[r:r + 1]
            step_l = conduct * (halo[3 * side + 2:3 * side + 3] - l[r:r + 1])
            edge_u.append(conduct * step_u)
            edge_l.append(step_l)
            edge_t.append(step_l * step_u)
        lap_u = lu_ref[i] + jnp.where(row == 0, edge_u[0], 0.0) + jnp.where(row == nz - 1, edge_u[1], 0.0)
        lap_l = ll_ref[i] + jnp.where(row == 0, edge_l[0], 0.0) + jnp.where(row == nz - 1, edge_l[1], 0.0)
        inner = inner_ref[i] + group_sum(edge_t[0]) + group_sum(edge_t[1])
        face_u = jnp.zeros_like(u)
        face_l = jnp.zeros_like(u)
        face_t = jnp.zeros_like(u)
        for f in range(4):
            ext = ext_ref[f, pl.ds(pl.multiple_of(i * rows, rows), rows), :]
            near_w = (ext[0:nz] + ext[2 * nz:3 * nz]) + ext[4 * nz:5 * nz]
            near_u = (ext[nz:2 * nz] + ext[3 * nz:4 * nz]) + ext[5 * nz:6 * nz]
            near_l = ext[6 * nz:7 * nz]
            g_self = gx if f < 2 else gy
            conduct = jnp.where(masks[f], cond_ref[cell_ref[near_ref[4 * b + f]]] * (g_self * near_w), 0.0)
            step_u = near_u - u
            step_l = conduct * (near_l - l)
            face_u = face_u + conduct * step_u
            face_l = face_l + step_l
            face_t = face_t + step_l * step_u
        square = th * th
        ionic = u * (1.0 - u) * (u - THRESHOLD)
        slope = -3.0 * u * u + 2.0 * (1.0 + THRESHOLD) * u - THRESHOLD
        u_out[i] = u + TIMESTEP * ((square * lap_u + th * face_u) + ionic)
        l_out[i] = l + TIMESTEP * ((square * lap_l + th * face_l) + slope * l)
        part_out[i] = -(square * inner + th * group_sum(face_t))
        return carry

    lax.fori_loop(0, GROUP, one, 0)


def inner_step(tissue, angle, potential, sensitivity, interpret=False):
    bricks, nz, cells = potential.shape
    blk3 = lambda: pl.BlockSpec((GROUP, nz, cells), lambda g: (g, 0, 0))
    full = jax.ShapeDtypeStruct((bricks, nz, cells), jnp.float32)
    return pl.pallas_call(
        inner_kernel,
        grid=(bricks // GROUP,),
        in_specs=[blk3(), blk3(), blk3(), blk3()],
        out_specs=[blk3(), blk3(), blk3(), blk3(), pl.BlockSpec((GROUP, 1, 128), lambda g: (g, 0, 0))],
        out_shape=[full, full, full, full, jax.ShapeDtypeStruct((bricks, 1, 128), jnp.float32)],
        compiler_params=pltpu.CompilerParams(dimension_semantics=("parallel",)),
        interpret=interpret,
    )(tissue, angle, potential, sensitivity)


def outer_step(tables, potential, sensitivity, inner, faces, halos, interpret=False):
    bricks, nz, cells = potential.shape
    edge = faces.shape[-1]
    expand = expanders(edge, cells).astype(jnp.bfloat16)
    blk3 = lambda: pl.BlockSpec((GROUP, nz, cells), lambda g: (g, 0, 0))
    lap_u, lap_l, gx, gy, inner_part = inner
    return pl.pallas_call(
        outer_kernel,
        grid=(bricks // GROUP,),
        in_specs=[pl.BlockSpec(memory_space=pltpu.SMEM) for _ in tables] + [
            pl.BlockSpec((4, edge, cells), lambda g: (0, 0, 0)),
            blk3(), blk3(), blk3(), blk3(), blk3(), blk3(),
            pl.BlockSpec((GROUP, 1, 128), lambda g: (g, 0, 0)),
            pl.BlockSpec((GROUP, 4, faces.shape[2], edge), lambda g: (g, 0, 0, 0)),
            pl.BlockSpec((GROUP, 6, cells), lambda g: (g, 0, 0)),
        ],
        out_specs=[blk3(), blk3(), pl.BlockSpec((GROUP, 1, 128), lambda g: (g, 0, 0))],
        out_shape=[
            jax.ShapeDtypeStruct((bricks, nz, cells), jnp.float32),
            jax.ShapeDtypeStruct((bricks, nz, cells), jnp.float32),
            jax.ShapeDtypeStruct((bricks, 1, 128), jnp.float32),
        ],
        scratch_shapes=[pltpu.VMEM((4, GROUP * 8 * nz, cells), jnp.float32)],
        compiler_params=pltpu.CompilerParams(dimension_semantics=("parallel",)),
        interpret=interpret,
    )(*tables, expand, potential, sensitivity, lap_u, lap_l, gx, gy, inner_part, faces, halos)


def body(
    potential, fiber_angle, tissue, sensitivity, conductance, brick_slot, neighbours, brick_cell
):
    bricks, z_layers, plane_cells = potential.shape
    brick_edge = BX
    blocks = lax.axis_size("blk")
    parts = lax.axis_size("par")
    devices = blocks * parts
    capacity = max(4, 8 * bricks // blocks)
    face_count = 4 * bricks
    face_cells = z_layers * brick_edge
    own_cells = conductance.shape[0]
    cell_count = own_cells * devices
    opposite = jnp.array([1, 0, 3, 2], jnp.int32)

    near_slot = brick_slot[neighbours]
    near_blk = (near_slot // bricks).reshape(-1)
    far_key = (near_slot % bricks * 4 + opposite[None, :]).reshape(-1)
    own_key = jnp.arange(face_count, dtype=jnp.int32)
    matches = near_blk[:, None] == near_blk[None, :]
    send_rank = jnp.sum((matches & (own_key[None, :] < own_key[:, None])).astype(jnp.int32), axis=1)
    recv_rank = jnp.sum((matches & (far_key[None, :] < far_key[:, None])).astype(jnp.int32), axis=1)
    send_slot = near_blk * capacity + send_rank
    recv_slot = near_blk * capacity + recv_rank

    adjoint = sensitivity.astype(jnp.float32)
    inner = inner_step(tissue, fiber_angle, potential, sensitivity)
    picker = expanders(brick_edge, plane_cells).reshape(4 * brick_edge, plane_cells).T.astype(jnp.float32)

    def boundary(values):
        picked = jnp.dot(
            values.astype(jnp.float32).reshape(bricks * z_layers, plane_cells),
            picker,
            precision=lax.Precision.HIGHEST,
        )
        return picked.reshape(bricks, z_layers, 4, brick_edge).transpose(0, 2, 1, 3)

    tissue_faces = boundary(tissue)
    cos_faces = jnp.cos(boundary(fiber_angle)) ** 2
    factor_faces = jnp.concatenate(
        [
            ACROSS + (ALONG - ACROSS) * cos_faces[:, :2],
            ACROSS + (ALONG - ACROSS) * (1.0 - cos_faces[:, 2:]),
        ],
        axis=1,
    )
    fields = jnp.stack(
        [tissue_faces * factor_faces, boundary(potential), boundary(sensitivity)], axis=2
    )
    flattened = fields.reshape(face_count, 3 * face_cells)
    outgoing = jnp.zeros((blocks * capacity, 3 * face_cells), jnp.float32).at[send_slot].set(flattened)
    shifted = [conductance] + [
        lax.ppermute(conductance, "par", [(i, (i + s) % parts) for i in range(parts)])
        for s in range(1, parts)
    ]
    source = (lax.axis_index("par") - jnp.arange(parts, dtype=jnp.int32)) % parts
    extra = jnp.concatenate([jnp.stack(shifted)[source].reshape(-1), brick_cell.astype(jnp.float32)])
    width = capacity * 3 * face_cells
    extra_width = -(-extra.shape[0] // 128) * 128
    extra = jnp.pad(extra, (0, extra_width - extra.shape[0]))
    sending = jnp.concatenate(
        [outgoing.reshape(blocks, width), jnp.broadcast_to(extra[None], (blocks, extra_width))], axis=1
    )
    arrived = lax.all_to_all(sending, "blk", split_axis=0, concat_axis=0, tiled=True)
    received = arrived[:, :width]
    par_cells = own_cells * parts
    cond_all = arrived[:, width : width + par_cells].reshape(-1)
    cell_all = arrived[:, width + par_cells : width + par_cells + bricks].reshape(-1).astype(jnp.int32)
    faces = received.reshape(blocks * capacity, 3 * face_cells)[recv_slot].reshape(
        bricks, 4, 3 * z_layers, brick_edge
    )

    size = lax.axis_size("par")
    up = [(i, i + 1) for i in range(size - 1)]
    down = [(j, i) for i, j in up]
    last = jnp.stack([tissue[:, -1].astype(jnp.float32), potential[:, -1], adjoint[:, -1]], axis=1)
    initial = jnp.stack([tissue[:, 0].astype(jnp.float32), potential[:, 0], adjoint[:, 0]], axis=1)
    halos = jnp.concatenate([lax.ppermute(last, "par", up), lax.ppermute(initial, "par", down)], axis=1)

    tables = (cond_all, cell_all, brick_cell, near_slot.reshape(-1))
    final, adjoint, parts_out = outer_step(tables, potential, sensitivity, inner, faces, halos)
    brick_part = jnp.sum(parts_out, axis=(1, 2))
    onehot_cells = brick_cell[:, None] == jnp.arange(cell_count, dtype=jnp.int32)[None, :]
    shares = jnp.sum(jnp.where(onehot_cells, brick_part[:, None], 0.0), axis=0)
    grad_share = jnp.sum(
        lax.all_to_all(
            shares.reshape(devices, own_cells), ("blk", "par"), split_axis=0, concat_axis=0, tiled=True
        ),
        axis=0,
    )
    cell_gradient = TIMESTEP * grad_share / (conductance * float(BX) ** 1.5)
    return (final, adjoint, cell_gradient)


def solution(mesh):
    placed = (
        P("blk", "par", None),
        P("blk", "par", None),
        P("blk", "par", None),
        P("blk", "par", None),
        P(("blk", "par")),
        P(),
        P("blk", None),
        P("blk"),
    )
    return jax.shard_map(
        body,
        mesh=mesh,
        in_specs=placed,
        out_specs=(P("blk", "par", None), P("blk", "par", None), P(("blk", "par"))),
        check_vma=False,
    )
```

```python
import jax
import jax.numpy as jnp
from jax import lax
from jax.sharding import PartitionSpec as P
from jax.experimental import pallas as pl
from jax.experimental.pallas import tpu as pltpu

BX = 32
STEPS = 1


TIMESTEP = 0.12
THRESHOLD = 0.2
ACROSS = 0.3
ALONG = 1.0
VERTICAL = 0.6


def extended(x, sides, width):
    for axis, dim in sides:
        size, length = (lax.axis_size(axis), x.shape[dim])
        up = [(i, (i + 1) % size) for i in range(size - 1)]
        down = [(j, i) for i, j in up]
        last = lax.slice_in_dim(x, length - width, length, axis=dim)
        initial = lax.slice_in_dim(x, 0, width, axis=dim)
        before = lax.ppermute(last, axis, up)
        after = lax.ppermute(initial, axis, down)
        x = jnp.concatenate([before, x, after], axis=dim)
    return x


def layers(values, brick_edge):
    return jnp.stack(
        [
            values[..., :brick_edge],
            values[..., -brick_edge:],
            values[..., 0::brick_edge],
            values[..., brick_edge - 1 :: brick_edge],
        ],
        axis=1,
    )


def along_x(values, lower_face, upper_face, brick_edge):
    return (
        jnp.concatenate([lower_face, values[..., :-brick_edge]], -1),
        jnp.concatenate([values[..., brick_edge:], upper_face], -1),
    )


def along_y(values, lower_face, upper_face, brick_edge):
    y_index = jnp.arange(values.shape[-1]) % brick_edge
    zero_pad = jnp.zeros(values.shape[:-1] + (1,), values.dtype)
    shifted_down = jnp.concatenate([zero_pad, values[..., :-1]], -1)
    shifted_up = jnp.concatenate([values[..., 1:], zero_pad], -1)
    return (
        jnp.where(y_index == 0, jnp.repeat(lower_face, brick_edge, axis=-1), shifted_down),
        jnp.where(
            y_index == brick_edge - 1, jnp.repeat(upper_face, brick_edge, axis=-1), shifted_up
        ),
    )


def near_values(values, layer_set, padded, brick_edge):
    x_low, x_high = along_x(values, layer_set[:, 0], layer_set[:, 1], brick_edge)
    y_low, y_high = along_y(values, layer_set[:, 2], layer_set[:, 3], brick_edge)
    return (x_low, x_high, y_low, y_high, padded[:, :-2], padded[:, 2:])


def laplace(conduct, values, beside):
    summed = conduct[0] * (beside[0] - values)
    for facet in range(1, 6):
        summed = summed + conduct[facet] * (beside[facet] - values)
    return summed


def brick_terms(conduct, adjoint, beside_adjoint, earlier, beside_state):
    summed = -conduct[0] * (adjoint - beside_adjoint[0]) * (earlier - beside_state[0])
    for facet in range(1, 6):
        summed = summed - conduct[facet] * (adjoint - beside_adjoint[facet]) * (
            earlier - beside_state[facet]
        )
    return jnp.sum(summed, axis=(1, 2))


def weights(tissue, fiber_angle, brick_scale):
    present = tissue.astype(jnp.float32)
    cos_square = jnp.cos(fiber_angle.astype(jnp.float32)) ** 2
    weight_x = present * brick_scale * (ACROSS + (ALONG - ACROSS) * cos_square)
    weight_y = present * brick_scale * (ACROSS + (ALONG - ACROSS) * (1.0 - cos_square))
    weight_z = present * brick_scale * VERTICAL
    return (weight_x, weight_y, weight_z)


def conductances(weight_x, weight_y, weight_z, weight_near, padded_z, brick_edge):
    x_low, x_high = along_x(weight_x, weight_near[:, 0], weight_near[:, 1], brick_edge)
    y_low, y_high = along_y(weight_y, weight_near[:, 2], weight_near[:, 3], brick_edge)
    return (
        weight_x * x_low,
        weight_x * x_high,
        weight_y * y_low,
        weight_y * y_high,
        weight_z * padded_z[:, :-2],
        weight_z * padded_z[:, 2:],
    )


GROUP = 8


def expanders(edge, cells):
    lane = jnp.arange(cells, dtype=jnp.int32)[None, :]
    k = jnp.arange(edge, dtype=jnp.int32)[:, None]
    return jnp.stack(
        [lane == k, lane == cells - edge + k, lane == edge * k, lane == edge * k + edge - 1]
    )


def cell_kernel(scale_ref, expand_ref, tissue_ref, angle_ref, u_ref, l_ref, face_ref, halo_ref,
                u_out, l_out, part_out):
    g = pl.program_id(0)
    nz, cells = u_ref.shape[1], u_ref.shape[2]
    edge = face_ref.shape[-1]
    lane = lax.broadcasted_iota(jnp.int32, (nz, cells), 1)
    row = lax.broadcasted_iota(jnp.int32, (nz, cells), 0)
    ycoord = lane % edge
    masks = (lane < edge, lane >= cells - edge, ycoord == 0, ycoord == edge - 1)
    shifts = (edge, cells - edge, 1, cells - 1)
    zlo = row == 0
    zhi = row == nz - 1

    def one(i, carry):
        b = g * GROUP + i
        th = scale_ref[b, 0]
        present = tissue_ref[i].astype(jnp.float32)
        c = jnp.cos(angle_ref[i].astype(jnp.float32))
        c2 = c * c
        scaled = present * th
        wx = scaled * (ACROSS + (ALONG - ACROSS) * c2)
        wy = scaled * (ACROSS + (ALONG - ACROSS) * (1.0 - c2))
        wz = scaled * VERTICAL
        u = u_ref[i]
        l = l_ref[i].astype(jnp.float32)
        halo = halo_ref[i]
        conds, ub, lb = [], [], []
        for f in range(4):
            face = face_ref[i, f]
            high = face.astype(jnp.bfloat16)
            rest = face - high.astype(jnp.float32)
            middle = rest.astype(jnp.bfloat16)
            low = (rest - middle.astype(jnp.float32)).astype(jnp.bfloat16)
            ext = jnp.dot(high, expand_ref[f], preferred_element_type=jnp.float32)
            ext = ext + jnp.dot(middle, expand_ref[f], preferred_element_type=jnp.float32)
            ext = ext + jnp.dot(low, expand_ref[f], preferred_element_type=jnp.float32)
            w_self = wx if f < 2 else wy
            w_near = jnp.where(masks[f], scale_ref[b, 1 + f] * ext[:nz], pltpu.roll(w_self, shifts[f], 1))
            conds.append(w_self * w_near)
            ub.append(jnp.where(masks[f], ext[nz:2 * nz], pltpu.roll(u, shifts[f], 1)))
            lb.append(jnp.where(masks[f], ext[2 * nz:3 * nz], pltpu.roll(l, shifts[f], 1)))
        wz_lo = jnp.where(zlo, (halo[0:1] * th) * VERTICAL, pltpu.roll(wz, 1, 0))
        wz_hi = jnp.where(zhi, (halo[3:4] * th) * VERTICAL, pltpu.roll(wz, nz - 1, 0))
        conds += [wz * wz_lo, wz * wz_hi]
        ub += [jnp.where(zlo, halo[1:2], pltpu.roll(u, 1, 0)), jnp.where(zhi, halo[4:5], pltpu.roll(u, nz - 1, 0))]
        lb += [jnp.where(zlo, halo[2:3], pltpu.roll(l, 1, 0)), jnp.where(zhi, halo[5:6], pltpu.roll(l, nz - 1, 0))]
        lap_u = conds[0] * (ub[0] - u)
        lap_l = conds[0] * (lb[0] - l)
        terms = lap_l * (ub[0] - u)
        for k in range(1, 6):
            step_u = ub[k] - u
            step_l = conds[k] * (lb[k] - l)
            lap_u = lap_u + conds[k] * step_u
            lap_l = lap_l + step_l
            terms = terms + step_l * step_u
        ionic = u * (1.0 - u) * (u - THRESHOLD)
        slope = -3.0 * u * u + 2.0 * (1.0 + THRESHOLD) * u - THRESHOLD
        u_out[i] = u + TIMESTEP * (lap_u + ionic)
        l_out[i] = l + TIMESTEP * (lap_l + slope * l)
        col = -jnp.sum(terms, axis=0, keepdims=True)
        acc = col[:, 0:128]
        for t in range(1, cells // 128):
            acc = acc + col[:, t * 128:(t + 1) * 128]
        part_out[i] = acc
        return carry

    lax.fori_loop(0, GROUP, one, 0)


def cell_step(scales, tissue, angle, potential, sensitivity, faces, halos, interpret=False):
    bricks, nz, cells = potential.shape
    edge = faces.shape[-1]
    expand = expanders(edge, cells).astype(jnp.bfloat16)
    blk3 = lambda: pl.BlockSpec((GROUP, nz, cells), lambda g: (g, 0, 0))
    return pl.pallas_call(
        cell_kernel,
        grid=(bricks // GROUP,),
        in_specs=[
            pl.BlockSpec(memory_space=pltpu.SMEM),
            pl.BlockSpec((4, edge, cells), lambda g: (0, 0, 0)),
            blk3(), blk3(), blk3(), blk3(),
            pl.BlockSpec((GROUP, 4, faces.shape[2], edge), lambda g: (g, 0, 0, 0)),
            pl.BlockSpec((GROUP, 6, cells), lambda g: (g, 0, 0)),
        ],
        out_specs=[blk3(), blk3(), pl.BlockSpec((GROUP, 1, 128), lambda g: (g, 0, 0))],
        out_shape=[
            jax.ShapeDtypeStruct((bricks, nz, cells), jnp.float32),
            jax.ShapeDtypeStruct((bricks, nz, cells), jnp.float32),
            jax.ShapeDtypeStruct((bricks, 1, 128), jnp.float32),
        ],
        compiler_params=pltpu.CompilerParams(dimension_semantics=("parallel",)),
        interpret=interpret,
    )(scales, expand, tissue, angle, potential, sensitivity, faces, halos)


def group_sum(values):
    col = jnp.sum(values, axis=0, keepdims=True)
    acc = col[:, 0:128]
    for t in range(1, values.shape[1] // 128):
        acc = acc + col[:, t * 128:(t + 1) * 128]
    return acc


def inner_kernel(tissue_ref, angle_ref, u_ref, l_ref, lu_out, ll_out, gx_out, gy_out, part_out):
    nz, cells = u_ref.shape[1], u_ref.shape[2]
    edge = BX
    lane = lax.broadcasted_iota(jnp.int32, (nz, cells), 1)
    row = lax.broadcasted_iota(jnp.int32, (nz, cells), 0)
    ycoord = lane % edge
    inside = (lane >= edge, lane < cells - edge, ycoord != 0, ycoord != edge - 1, row != 0, row != nz - 1)
    shifts = ((edge, 1), (cells - edge, 1), (1, 1), (cells - 1, 1), (1, 0), (nz - 1, 0))

    def one(i, carry):
        present = tissue_ref[i].astype(jnp.float32)
        c = jnp.cos(angle_ref[i].astype(jnp.float32))
        c2 = c * c
        gx = present * (ACROSS + (ALONG - ACROSS) * c2)
        gy = present * (ACROSS + (ALONG - ACROSS) * (1.0 - c2))
        gz = present * VERTICAL
        u = u_ref[i]
        l = l_ref[i].astype(jnp.float32)
        lap_u = jnp.zeros_like(u)
        lap_l = jnp.zeros_like(u)
        terms = jnp.zeros_like(u)
        for k in range(6):
            g = gx if k < 2 else (gy if k < 4 else gz)
            shift, axis = shifts[k]
            conduct = jnp.where(inside[k], g * pltpu.roll(g, shift, axis), 0.0)
            step_u = pltpu.roll(u, shift, axis) - u
            step_l = conduct * (pltpu.roll(l, shift, axis) - l)
            lap_u = lap_u + conduct * step_u
            lap_l = lap_l + step_l
            terms = terms + step_l * step_u
        lu_out[i] = lap_u
        ll_out[i] = lap_l
        gx_out[i] = gx
        gy_out[i] = gy
        part_out[i] = group_sum(terms)
        return carry

    lax.fori_loop(0, GROUP, one, 0)


def outer_kernel(cond_ref, cell_ref, own_ref, near_ref, expand_ref, u_ref, l_ref, lu_ref, ll_ref, gx_ref, gy_ref, inner_ref, face_ref,
                 halo_ref, u_out, l_out, part_out, ext_ref):
    g = pl.program_id(0)
    nz, cells = u_ref.shape[1], u_ref.shape[2]
    edge = BX
    rows = 8 * nz
    for f in range(4):
        face = face_ref[:, f]
        part = face[:, :2 * nz]
        high = part.astype(jnp.bfloat16).astype(jnp.float32)
        rest = part - high
        middle = rest.astype(jnp.bfloat16).astype(jnp.float32)
        low = (rest - middle).astype(jnp.bfloat16).astype(jnp.float32)
        stacked = jnp.concatenate(
            [high, middle, low, face[:, 2 * nz:3 * nz], jnp.zeros_like(face[:, :nz])], axis=1
        )
        ext_ref[f] = jnp.dot(
            stacked.reshape(GROUP * rows, edge).astype(jnp.bfloat16),
            expand_ref[f],
            preferred_element_type=jnp.float32,
        )
    lane = lax.broadcasted_iota(jnp.int32, (nz, cells), 1)
    row = lax.broadcasted_iota(jnp.int32, (nz, cells), 0)
    ycoord = lane % edge
    masks = (lane < edge, lane >= cells - edge, ycoord == 0, ycoord == edge - 1)

    def one(i, carry):
        b = g * GROUP + i
        th = cond_ref[own_ref[b]]
        u = u_ref[i]
        l = l_ref[i].astype(jnp.float32)
        gx = gx_ref[i]
        gy = gy_ref[i]
        halo = halo_ref[i]
        edge_u, edge_l, edge_t = [], [], []
        for side, r in ((0, 0), (1, nz - 1)):
            own_z = (gx[r:r + 1] != 0.0).astype(jnp.float32) * VERTICAL
            conduct = own_z * (halo[3 * side:3 * side + 1] * VERTICAL)
            step_u = halo[3 * side + 1:3 * side + 2] - u[r:r + 1]
            step_l = conduct * (halo[3 * side + 2:3 * side + 3] - l[r:r + 1])
            edge_u.append(conduct * step_u)
            edge_l.append(step_l)
            edge_t.append(step_l * step_u)
        lap_u = lu_ref[i] + jnp.where(row == 0, edge_u[0], 0.0) + jnp.where(row == nz - 1, edge_u[1], 0.0)
        lap_l = ll_ref[i] + jnp.where(row == 0, edge_l[0], 0.0) + jnp.where(row == nz - 1, edge_l[1], 0.0)
        inner = inner_ref[i] + group_sum(edge_t[0]) + group_sum(edge_t[1])
        face_u = jnp.zeros_like(u)
        face_l = jnp.zeros_like(u)
        face_t = jnp.zeros_like(u)
        for f in range(4):
            ext = ext_ref[f, pl.ds(pl.multiple_of(i * rows, rows), rows), :]
            near_w = (ext[0:nz] + ext[2 * nz:3 * nz]) + ext[4 * nz:5 * nz]
            near_u = (ext[nz:2 * nz] + ext[3 * nz:4 * nz]) + ext[5 * nz:6 * nz]
            near_l = ext[6 * nz:7 * nz]
            g_self = gx if f < 2 else gy
            conduct = jnp.where(masks[f], cond_ref[cell_ref[near_ref[4 * b + f]]] * (g_self * near_w), 0.0)
            step_u = near_u - u
            step_l = conduct * (near_l - l)
            face_u = face_u + conduct * step_u
            face_l = face_l + step_l
            face_t = face_t + step_l * step_u
        square = th * th
        ionic = u * (1.0 - u) * (u - THRESHOLD)
        slope = -3.0 * u * u + 2.0 * (1.0 + THRESHOLD) * u - THRESHOLD
        u_out[i] = u + TIMESTEP * ((square * lap_u + th * face_u) + ionic)
        l_out[i] = l + TIMESTEP * ((square * lap_l + th * face_l) + slope * l)
        part_out[i] = -(square * inner + th * group_sum(face_t))
        return carry

    lax.fori_loop(0, GROUP, one, 0)


def inner_step(tissue, angle, potential, sensitivity, interpret=False):
    bricks, nz, cells = potential.shape
    blk3 = lambda: pl.BlockSpec((GROUP, nz, cells), lambda g: (g, 0, 0))
    full = jax.ShapeDtypeStruct((bricks, nz, cells), jnp.float32)
    return pl.pallas_call(
        inner_kernel,
        grid=(bricks // GROUP,),
        in_specs=[blk3(), blk3(), blk3(), blk3()],
        out_specs=[blk3(), blk3(), blk3(), blk3(), pl.BlockSpec((GROUP, 1, 128), lambda g: (g, 0, 0))],
        out_shape=[full, full, full, full, jax.ShapeDtypeStruct((bricks, 1, 128), jnp.float32)],
        compiler_params=pltpu.CompilerParams(dimension_semantics=("parallel",)),
        interpret=interpret,
    )(tissue, angle, potential, sensitivity)


def outer_step(tables, potential, sensitivity, inner, faces, halos, interpret=False):
    bricks, nz, cells = potential.shape
    edge = faces.shape[-1]
    expand = expanders(edge, cells).astype(jnp.bfloat16)
    blk3 = lambda: pl.BlockSpec((GROUP, nz, cells), lambda g: (g, 0, 0))
    lap_u, lap_l, gx, gy, inner_part = inner
    return pl.pallas_call(
        outer_kernel,
        grid=(bricks // GROUP,),
        in_specs=[pl.BlockSpec(memory_space=pltpu.SMEM) for _ in tables] + [
            pl.BlockSpec((4, edge, cells), lambda g: (0, 0, 0)),
            blk3(), blk3(), blk3(), blk3(), blk3(), blk3(),
            pl.BlockSpec((GROUP, 1, 128), lambda g: (g, 0, 0)),
            pl.BlockSpec((GROUP, 4, faces.shape[2], edge), lambda g: (g, 0, 0, 0)),
            pl.BlockSpec((GROUP, 6, cells), lambda g: (g, 0, 0)),
        ],
        out_specs=[blk3(), blk3(), pl.BlockSpec((GROUP, 1, 128), lambda g: (g, 0, 0))],
        out_shape=[
            jax.ShapeDtypeStruct((bricks, nz, cells), jnp.float32),
            jax.ShapeDtypeStruct((bricks, nz, cells), jnp.float32),
            jax.ShapeDtypeStruct((bricks, 1, 128), jnp.float32),
        ],
        scratch_shapes=[pltpu.VMEM((4, GROUP * 8 * nz, cells), jnp.float32)],
        compiler_params=pltpu.CompilerParams(dimension_semantics=("parallel",)),
        interpret=interpret,
    )(*tables, expand, potential, sensitivity, lap_u, lap_l, gx, gy, inner_part, faces, halos)


def body(
    potential, fiber_angle, tissue, sensitivity, conductance, brick_slot, neighbours, brick_cell
):
    bricks, z_layers, plane_cells = potential.shape
    brick_edge = BX
    blocks = lax.axis_size("blk")
    parts = lax.axis_size("par")
    devices = blocks * parts
    capacity = max(4, 8 * bricks // blocks)
    face_count = 4 * bricks
    face_cells = z_layers * brick_edge
    own_cells = conductance.shape[0]
    cell_count = own_cells * devices
    opposite = jnp.array([1, 0, 3, 2], jnp.int32)

    near_slot = brick_slot[neighbours]
    near_blk = (near_slot // bricks).reshape(-1)
    far_key = (near_slot % bricks * 4 + opposite[None, :]).reshape(-1)
    own_key = jnp.arange(face_count, dtype=jnp.int32)
    matches = near_blk[:, None] == near_blk[None, :]
    send_rank = jnp.sum((matches & (own_key[None, :] < own_key[:, None])).astype(jnp.int32), axis=1)
    recv_rank = jnp.sum((matches & (far_key[None, :] < far_key[:, None])).astype(jnp.int32), axis=1)
    send_slot = near_blk * capacity + send_rank
    recv_slot = near_blk * capacity + recv_rank

    adjoint = sensitivity.astype(jnp.float32)
    inner = inner_step(tissue, fiber_angle, potential, sensitivity)
    picker = expanders(brick_edge, plane_cells).reshape(4 * brick_edge, plane_cells).T.astype(jnp.float32)

    def boundary(values):
        picked = jnp.dot(
            values.astype(jnp.float32).reshape(bricks * z_layers, plane_cells),
            picker,
            precision=lax.Precision.HIGHEST,
        )
        return picked.reshape(bricks, z_layers, 4, brick_edge).transpose(0, 2, 1, 3)

    tissue_faces = boundary(tissue)
    cos_faces = jnp.cos(boundary(fiber_angle)) ** 2
    factor_faces = jnp.concatenate(
        [
            ACROSS + (ALONG - ACROSS) * cos_faces[:, :2],
            ACROSS + (ALONG - ACROSS) * (1.0 - cos_faces[:, 2:]),
        ],
        axis=1,
    )
    fields = jnp.stack(
        [tissue_faces * factor_faces, boundary(potential), boundary(sensitivity)], axis=2
    )
    flattened = fields.reshape(face_count, 3 * face_cells)
    outgoing = jnp.zeros((blocks * capacity, 3 * face_cells), jnp.float32).at[send_slot].set(flattened)
    shifted = [conductance] + [
        lax.ppermute(conductance, "par", [(i, (i + s) % parts) for i in range(parts)])
        for s in range(1, parts)
    ]
    source = (lax.axis_index("par") - jnp.arange(parts, dtype=jnp.int32)) % parts
    extra = jnp.concatenate([jnp.stack(shifted)[source].reshape(-1), brick_cell.astype(jnp.float32)])
    width = capacity * 3 * face_cells
    extra_width = -(-extra.shape[0] // 128) * 128
    extra = jnp.pad(extra, (0, extra_width - extra.shape[0]))
    sending = jnp.concatenate(
        [outgoing.reshape(blocks, width), jnp.broadcast_to(extra[None], (blocks, extra_width))], axis=1
    )
    arrived = lax.all_to_all(sending, "blk", split_axis=0, concat_axis=0, tiled=True)
    received = arrived[:, :width]
    par_cells = own_cells * parts
    cond_all = arrived[:, width : width + par_cells].reshape(-1)
    cell_all = arrived[:, width + par_cells : width + par_cells + bricks].reshape(-1).astype(jnp.int32)
    faces = received.reshape(blocks * capacity, 3 * face_cells)[recv_slot].reshape(
        bricks, 4, 3 * z_layers, brick_edge
    )

    size = lax.axis_size("par")
    up = [(i, i + 1) for i in range(size - 1)]
    down = [(j, i) for i, j in up]
    last = jnp.stack([tissue[:, -1].astype(jnp.float32), potential[:, -1], adjoint[:, -1]], axis=1)
    initial = jnp.stack([tissue[:, 0].astype(jnp.float32), potential[:, 0], adjoint[:, 0]], axis=1)
    halos = jnp.concatenate([lax.ppermute(last, "par", up), lax.ppermute(initial, "par", down)], axis=1)

    tables = (cond_all, cell_all, brick_cell, near_slot.reshape(-1))
    final, adjoint, parts_out = outer_step(tables, potential, sensitivity, inner, faces, halos)
    brick_part = jnp.sum(parts_out, axis=(1, 2))
    onehot_cells = brick_cell[:, None] == jnp.arange(cell_count, dtype=jnp.int32)[None, :]
    shares = jnp.sum(jnp.where(onehot_cells, brick_part[:, None], 0.0), axis=0)
    column = jnp.sum(
        lax.all_to_all(
            shares.reshape(blocks, parts * own_cells), "blk", split_axis=0, concat_axis=0, tiled=True
        ),
        axis=0,
    )
    summed = column
    for s in range(1, parts):
        summed = summed + lax.ppermute(column, "par", [(i, (i + s) % parts) for i in range(parts)])
    grad_share = lax.dynamic_slice(summed, (lax.axis_index("par") * own_cells,), (own_cells,))
    cell_gradient = TIMESTEP * grad_share / (conductance * float(BX) ** 1.5)
    return (final, adjoint, cell_gradient)


def solution(mesh):
    placed = (
        P("blk", "par", None),
        P("blk", "par", None),
        P("blk", "par", None),
        P("blk", "par", None),
        P(("blk", "par")),
        P(),
        P("blk", None),
        P("blk"),
    )
    return jax.shard_map(
        body,
        mesh=mesh,
        in_specs=placed,
        out_specs=(P("blk", "par", None), P("blk", "par", None), P(("blk", "par"))),
        check_vma=False,
    )
```

```python
import jax
import jax.numpy as jnp
from jax import lax
from jax.sharding import PartitionSpec as P
from jax.experimental import pallas as pl
from jax.experimental.pallas import tpu as pltpu

BX = 32
STEPS = 1


TIMESTEP = 0.12
THRESHOLD = 0.2
ACROSS = 0.3
ALONG = 1.0
VERTICAL = 0.6


def extended(x, sides, width):
    for axis, dim in sides:
        size, length = (lax.axis_size(axis), x.shape[dim])
        up = [(i, (i + 1) % size) for i in range(size - 1)]
        down = [(j, i) for i, j in up]
        last = lax.slice_in_dim(x, length - width, length, axis=dim)
        initial = lax.slice_in_dim(x, 0, width, axis=dim)
        before = lax.ppermute(last, axis, up)
        after = lax.ppermute(initial, axis, down)
        x = jnp.concatenate([before, x, after], axis=dim)
    return x


def layers(values, brick_edge):
    return jnp.stack(
        [
            values[..., :brick_edge],
            values[..., -brick_edge:],
            values[..., 0::brick_edge],
            values[..., brick_edge - 1 :: brick_edge],
        ],
        axis=1,
    )


def along_x(values, lower_face, upper_face, brick_edge):
    return (
        jnp.concatenate([lower_face, values[..., :-brick_edge]], -1),
        jnp.concatenate([values[..., brick_edge:], upper_face], -1),
    )


def along_y(values, lower_face, upper_face, brick_edge):
    y_index = jnp.arange(values.shape[-1]) % brick_edge
    zero_pad = jnp.zeros(values.shape[:-1] + (1,), values.dtype)
    shifted_down = jnp.concatenate([zero_pad, values[..., :-1]], -1)
    shifted_up = jnp.concatenate([values[..., 1:], zero_pad], -1)
    return (
        jnp.where(y_index == 0, jnp.repeat(lower_face, brick_edge, axis=-1), shifted_down),
        jnp.where(
            y_index == brick_edge - 1, jnp.repeat(upper_face, brick_edge, axis=-1), shifted_up
        ),
    )


def near_values(values, layer_set, padded, brick_edge):
    x_low, x_high = along_x(values, layer_set[:, 0], layer_set[:, 1], brick_edge)
    y_low, y_high = along_y(values, layer_set[:, 2], layer_set[:, 3], brick_edge)
    return (x_low, x_high, y_low, y_high, padded[:, :-2], padded[:, 2:])


def laplace(conduct, values, beside):
    summed = conduct[0] * (beside[0] - values)
    for facet in range(1, 6):
        summed = summed + conduct[facet] * (beside[facet] - values)
    return summed


def brick_terms(conduct, adjoint, beside_adjoint, earlier, beside_state):
    summed = -conduct[0] * (adjoint - beside_adjoint[0]) * (earlier - beside_state[0])
    for facet in range(1, 6):
        summed = summed - conduct[facet] * (adjoint - beside_adjoint[facet]) * (
            earlier - beside_state[facet]
        )
    return jnp.sum(summed, axis=(1, 2))


def weights(tissue, fiber_angle, brick_scale):
    present = tissue.astype(jnp.float32)
    cos_square = jnp.cos(fiber_angle.astype(jnp.float32)) ** 2
    weight_x = present * brick_scale * (ACROSS + (ALONG - ACROSS) * cos_square)
    weight_y = present * brick_scale * (ACROSS + (ALONG - ACROSS) * (1.0 - cos_square))
    weight_z = present * brick_scale * VERTICAL
    return (weight_x, weight_y, weight_z)


def conductances(weight_x, weight_y, weight_z, weight_near, padded_z, brick_edge):
    x_low, x_high = along_x(weight_x, weight_near[:, 0], weight_near[:, 1], brick_edge)
    y_low, y_high = along_y(weight_y, weight_near[:, 2], weight_near[:, 3], brick_edge)
    return (
        weight_x * x_low,
        weight_x * x_high,
        weight_y * y_low,
        weight_y * y_high,
        weight_z * padded_z[:, :-2],
        weight_z * padded_z[:, 2:],
    )


GROUP = 8


def expanders(edge, cells):
    lane = jnp.arange(cells, dtype=jnp.int32)[None, :]
    k = jnp.arange(edge, dtype=jnp.int32)[:, None]
    return jnp.stack(
        [lane == k, lane == cells - edge + k, lane == edge * k, lane == edge * k + edge - 1]
    )


def cell_kernel(scale_ref, expand_ref, tissue_ref, angle_ref, u_ref, l_ref, face_ref, halo_ref,
                u_out, l_out, part_out):
    g = pl.program_id(0)
    nz, cells = u_ref.shape[1], u_ref.shape[2]
    edge = face_ref.shape[-1]
    lane = lax.broadcasted_iota(jnp.int32, (nz, cells), 1)
    row = lax.broadcasted_iota(jnp.int32, (nz, cells), 0)
    ycoord = lane % edge
    masks = (lane < edge, lane >= cells - edge, ycoord == 0, ycoord == edge - 1)
    shifts = (edge, cells - edge, 1, cells - 1)
    zlo = row == 0
    zhi = row == nz - 1

    def one(i, carry):
        b = g * GROUP + i
        th = scale_ref[b, 0]
        present = tissue_ref[i].astype(jnp.float32)
        c = jnp.cos(angle_ref[i].astype(jnp.float32))
        c2 = c * c
        scaled = present * th
        wx = scaled * (ACROSS + (ALONG - ACROSS) * c2)
        wy = scaled * (ACROSS + (ALONG - ACROSS) * (1.0 - c2))
        wz = scaled * VERTICAL
        u = u_ref[i]
        l = l_ref[i].astype(jnp.float32)
        halo = halo_ref[i]
        conds, ub, lb = [], [], []
        for f in range(4):
            face = face_ref[i, f]
            high = face.astype(jnp.bfloat16)
            rest = face - high.astype(jnp.float32)
            middle = rest.astype(jnp.bfloat16)
            low = (rest - middle.astype(jnp.float32)).astype(jnp.bfloat16)
            ext = jnp.dot(high, expand_ref[f], preferred_element_type=jnp.float32)
            ext = ext + jnp.dot(middle, expand_ref[f], preferred_element_type=jnp.float32)
            ext = ext + jnp.dot(low, expand_ref[f], preferred_element_type=jnp.float32)
            w_self = wx if f < 2 else wy
            w_near = jnp.where(masks[f], scale_ref[b, 1 + f] * ext[:nz], pltpu.roll(w_self, shifts[f], 1))
            conds.append(w_self * w_near)
            ub.append(jnp.where(masks[f], ext[nz:2 * nz], pltpu.roll(u, shifts[f], 1)))
            lb.append(jnp.where(masks[f], ext[2 * nz:3 * nz], pltpu.roll(l, shifts[f], 1)))
        wz_lo = jnp.where(zlo, (halo[0:1] * th) * VERTICAL, pltpu.roll(wz, 1, 0))
        wz_hi = jnp.where(zhi, (halo[3:4] * th) * VERTICAL, pltpu.roll(wz, nz - 1, 0))
        conds += [wz * wz_lo, wz * wz_hi]
        ub += [jnp.where(zlo, halo[1:2], pltpu.roll(u, 1, 0)), jnp.where(zhi, halo[4:5], pltpu.roll(u, nz - 1, 0))]
        lb += [jnp.where(zlo, halo[2:3], pltpu.roll(l, 1, 0)), jnp.where(zhi, halo[5:6], pltpu.roll(l, nz - 1, 0))]
        lap_u = conds[0] * (ub[0] - u)
        lap_l = conds[0] * (lb[0] - l)
        terms = lap_l * (ub[0] - u)
        for k in range(1, 6):
            step_u = ub[k] - u
            step_l = conds[k] * (lb[k] - l)
            lap_u = lap_u + conds[k] * step_u
            lap_l = lap_l + step_l
            terms = terms + step_l * step_u
        ionic = u * (1.0 - u) * (u - THRESHOLD)
        slope = -3.0 * u * u + 2.0 * (1.0 + THRESHOLD) * u - THRESHOLD
        u_out[i] = u + TIMESTEP * (lap_u + ionic)
        l_out[i] = l + TIMESTEP * (lap_l + slope * l)
        col = -jnp.sum(terms, axis=0, keepdims=True)
        acc = col[:, 0:128]
        for t in range(1, cells // 128):
            acc = acc + col[:, t * 128:(t + 1) * 128]
        part_out[i] = acc
        return carry

    lax.fori_loop(0, GROUP, one, 0)


def cell_step(scales, tissue, angle, potential, sensitivity, faces, halos, interpret=False):
    bricks, nz, cells = potential.shape
    edge = faces.shape[-1]
    expand = expanders(edge, cells).astype(jnp.bfloat16)
    blk3 = lambda: pl.BlockSpec((GROUP, nz, cells), lambda g: (g, 0, 0))
    return pl.pallas_call(
        cell_kernel,
        grid=(bricks // GROUP,),
        in_specs=[
            pl.BlockSpec(memory_space=pltpu.SMEM),
            pl.BlockSpec((4, edge, cells), lambda g: (0, 0, 0)),
            blk3(), blk3(), blk3(), blk3(),
            pl.BlockSpec((GROUP, 4, faces.shape[2], edge), lambda g: (g, 0, 0, 0)),
            pl.BlockSpec((GROUP, 6, cells), lambda g: (g, 0, 0)),
        ],
        out_specs=[blk3(), blk3(), pl.BlockSpec((GROUP, 1, 128), lambda g: (g, 0, 0))],
        out_shape=[
            jax.ShapeDtypeStruct((bricks, nz, cells), jnp.float32),
            jax.ShapeDtypeStruct((bricks, nz, cells), jnp.float32),
            jax.ShapeDtypeStruct((bricks, 1, 128), jnp.float32),
        ],
        compiler_params=pltpu.CompilerParams(dimension_semantics=("parallel",)),
        interpret=interpret,
    )(scales, expand, tissue, angle, potential, sensitivity, faces, halos)


def group_sum(values):
    col = jnp.sum(values, axis=0, keepdims=True)
    acc = col[:, 0:128]
    for t in range(1, values.shape[1] // 128):
        acc = acc + col[:, t * 128:(t + 1) * 128]
    return acc


def inner_kernel(tissue_ref, angle_ref, u_ref, l_ref, lu_out, ll_out, gx_out, gy_out, part_out):
    nz, cells = u_ref.shape[1], u_ref.shape[2]
    edge = BX
    lane = lax.broadcasted_iota(jnp.int32, (nz, cells), 1)
    row = lax.broadcasted_iota(jnp.int32, (nz, cells), 0)
    ycoord = lane % edge
    inside = (lane >= edge, lane < cells - edge, ycoord != 0, ycoord != edge - 1, row != 0, row != nz - 1)
    shifts = ((edge, 1), (cells - edge, 1), (1, 1), (cells - 1, 1), (1, 0), (nz - 1, 0))

    def one(i, carry):
        present = tissue_ref[i].astype(jnp.float32)
        c = jnp.cos(angle_ref[i].astype(jnp.float32))
        c2 = c * c
        gx = present * (ACROSS + (ALONG - ACROSS) * c2)
        gy = present * (ACROSS + (ALONG - ACROSS) * (1.0 - c2))
        gz = present * VERTICAL
        u = u_ref[i]
        l = l_ref[i].astype(jnp.float32)
        lap_u = jnp.zeros_like(u)
        lap_l = jnp.zeros_like(u)
        terms = jnp.zeros_like(u)
        for k in range(6):
            g = gx if k < 2 else (gy if k < 4 else gz)
            shift, axis = shifts[k]
            conduct = jnp.where(inside[k], g * pltpu.roll(g, shift, axis), 0.0)
            step_u = pltpu.roll(u, shift, axis) - u
            step_l = conduct * (pltpu.roll(l, shift, axis) - l)
            lap_u = lap_u + conduct * step_u
            lap_l = lap_l + step_l
            terms = terms + step_l * step_u
        lu_out[i] = lap_u
        ll_out[i] = lap_l
        gx_out[i] = gx
        gy_out[i] = gy
        part_out[i] = group_sum(terms)
        return carry

    lax.fori_loop(0, GROUP, one, 0)


def outer_kernel(cond_ref, cell_ref, own_ref, near_ref, expand_ref, u_ref, l_ref, lu_ref, ll_ref, gx_ref, gy_ref, inner_ref, face_ref,
                 halo_ref, u_out, l_out, part_out, ext_ref):
    g = pl.program_id(0)
    nz, cells = u_ref.shape[1], u_ref.shape[2]
    edge = BX
    rows = 8 * nz
    layer = nz * edge
    spread = lax.broadcasted_iota(jnp.int32, (nz, layer), 1) // edge == lax.broadcasted_iota(
        jnp.int32, (nz, layer), 0
    )
    for f in range(4):
        flat = face_ref[:, f]
        face = jnp.concatenate(
            [jnp.where(spread[None], flat[:, None, k * layer:(k + 1) * layer], 0.0) for k in range(3)], axis=1
        )
        part = face[:, :2 * nz]
        high = part.astype(jnp.bfloat16).astype(jnp.float32)
        rest = part - high
        middle = rest.astype(jnp.bfloat16).astype(jnp.float32)
        low = (rest - middle).astype(jnp.bfloat16).astype(jnp.float32)
        stacked = jnp.concatenate(
            [high, middle, low, face[:, 2 * nz:3 * nz], jnp.zeros_like(face[:, :nz])], axis=1
        )
        ext_ref[f] = jnp.dot(
            stacked.reshape(GROUP * rows, layer).astype(jnp.bfloat16),
            expand_ref[f],
            preferred_element_type=jnp.float32,
        )
    lane = lax.broadcasted_iota(jnp.int32, (nz, cells), 1)
    row = lax.broadcasted_iota(jnp.int32, (nz, cells), 0)
    ycoord = lane % edge
    masks = (lane < edge, lane >= cells - edge, ycoord == 0, ycoord == edge - 1)

    def one(i, carry):
        b = g * GROUP + i
        th = cond_ref[own_ref[b]]
        u = u_ref[i]
        l = l_ref[i].astype(jnp.float32)
        gx = gx_ref[i]
        gy = gy_ref[i]
        halo = halo_ref[i]
        edge_u, edge_l, edge_t = [], [], []
        for side, r in ((0, 0), (1, nz - 1)):
            own_z = (gx[r:r + 1] != 0.0).astype(jnp.float32) * VERTICAL
            conduct = own_z * (halo[3 * side:3 * side + 1] * VERTICAL)
            step_u = halo[3 * side + 1:3 * side + 2] - u[r:r + 1]
            step_l = conduct * (halo[3 * side + 2:3 * side + 3] - l[r:r + 1])
            edge_u.append(conduct * step_u)
            edge_l.append(step_l)
            edge_t.append(step_l * step_u)
        lap_u = lu_ref[i] + jnp.where(row == 0, edge_u[0], 0.0) + jnp.where(row == nz - 1, edge_u[1], 0.0)
        lap_l = ll_ref[i] + jnp.where(row == 0, edge_l[0], 0.0) + jnp.where(row == nz - 1, edge_l[1], 0.0)
        inner = inner_ref[i] + group_sum(edge_t[0]) + group_sum(edge_t[1])
        face_u = jnp.zeros_like(u)
        face_l = jnp.zeros_like(u)
        face_t = jnp.zeros_like(u)
        for f in range(4):
            ext = ext_ref[f, pl.ds(pl.multiple_of(i * rows, rows), rows), :]
            near_w = (ext[0:nz] + ext[2 * nz:3 * nz]) + ext[4 * nz:5 * nz]
            near_u = (ext[nz:2 * nz] + ext[3 * nz:4 * nz]) + ext[5 * nz:6 * nz]
            near_l = ext[6 * nz:7 * nz]
            g_self = gx if f < 2 else gy
            conduct = jnp.where(masks[f], cond_ref[cell_ref[near_ref[4 * b + f]]] * (g_self * near_w), 0.0)
            step_u = near_u - u
            step_l = conduct * (near_l - l)
            face_u = face_u + conduct * step_u
            face_l = face_l + step_l
            face_t = face_t + step_l * step_u
        square = th * th
        ionic = u * (1.0 - u) * (u - THRESHOLD)
        slope = -3.0 * u * u + 2.0 * (1.0 + THRESHOLD) * u - THRESHOLD
        u_out[i] = u + TIMESTEP * ((square * lap_u + th * face_u) + ionic)
        l_out[i] = l + TIMESTEP * ((square * lap_l + th * face_l) + slope * l)
        part_out[i] = -(square * inner + th * group_sum(face_t))
        return carry

    lax.fori_loop(0, GROUP, one, 0)


def inner_step(tissue, angle, potential, sensitivity, interpret=False):
    bricks, nz, cells = potential.shape
    blk3 = lambda: pl.BlockSpec((GROUP, nz, cells), lambda g: (g, 0, 0))
    full = jax.ShapeDtypeStruct((bricks, nz, cells), jnp.float32)
    return pl.pallas_call(
        inner_kernel,
        grid=(bricks // GROUP,),
        in_specs=[blk3(), blk3(), blk3(), blk3()],
        out_specs=[blk3(), blk3(), blk3(), blk3(), pl.BlockSpec((GROUP, 1, 128), lambda g: (g, 0, 0))],
        out_shape=[full, full, full, full, jax.ShapeDtypeStruct((bricks, 1, 128), jnp.float32)],
        compiler_params=pltpu.CompilerParams(dimension_semantics=("parallel",)),
        interpret=interpret,
    )(tissue, angle, potential, sensitivity)


def outer_step(tables, potential, sensitivity, inner, faces, halos, interpret=False):
    bricks, nz, cells = potential.shape
    edge = faces.shape[-1]
    edge = BX
    expand = jnp.tile(expanders(edge, cells), (1, nz, 1)).astype(jnp.bfloat16)
    blk3 = lambda: pl.BlockSpec((GROUP, nz, cells), lambda g: (g, 0, 0))
    lap_u, lap_l, gx, gy, inner_part = inner
    return pl.pallas_call(
        outer_kernel,
        grid=(bricks // GROUP,),
        in_specs=[pl.BlockSpec(memory_space=pltpu.SMEM) for _ in tables] + [
            pl.BlockSpec((4, nz * edge, cells), lambda g: (0, 0, 0)),
            blk3(), blk3(), blk3(), blk3(), blk3(), blk3(),
            pl.BlockSpec((GROUP, 1, 128), lambda g: (g, 0, 0)),
            pl.BlockSpec((GROUP, 4, faces.shape[2]), lambda g: (g, 0, 0)),
            pl.BlockSpec((GROUP, 6, cells), lambda g: (g, 0, 0)),
        ],
        out_specs=[blk3(), blk3(), pl.BlockSpec((GROUP, 1, 128), lambda g: (g, 0, 0))],
        out_shape=[
            jax.ShapeDtypeStruct((bricks, nz, cells), jnp.float32),
            jax.ShapeDtypeStruct((bricks, nz, cells), jnp.float32),
            jax.ShapeDtypeStruct((bricks, 1, 128), jnp.float32),
        ],
        scratch_shapes=[pltpu.VMEM((4, GROUP * 8 * nz, cells), jnp.float32)],
        compiler_params=pltpu.CompilerParams(dimension_semantics=("parallel",)),
        interpret=interpret,
    )(*tables, expand, potential, sensitivity, lap_u, lap_l, gx, gy, inner_part, faces, halos)


def body(
    potential, fiber_angle, tissue, sensitivity, conductance, brick_slot, neighbours, brick_cell
):
    bricks, z_layers, plane_cells = potential.shape
    brick_edge = BX
    blocks = lax.axis_size("blk")
    parts = lax.axis_size("par")
    devices = blocks * parts
    capacity = max(4, 8 * bricks // blocks)
    face_count = 4 * bricks
    face_cells = z_layers * brick_edge
    own_cells = conductance.shape[0]
    cell_count = own_cells * devices
    opposite = jnp.array([1, 0, 3, 2], jnp.int32)

    near_slot = brick_slot[neighbours]
    near_blk = (near_slot // bricks).reshape(-1)
    far_key = (near_slot % bricks * 4 + opposite[None, :]).reshape(-1)
    own_key = jnp.arange(face_count, dtype=jnp.int32)
    matches = near_blk[:, None] == near_blk[None, :]
    send_rank = jnp.sum((matches & (own_key[None, :] < own_key[:, None])).astype(jnp.int32), axis=1)
    recv_rank = jnp.sum((matches & (far_key[None, :] < far_key[:, None])).astype(jnp.int32), axis=1)
    send_slot = near_blk * capacity + send_rank
    recv_slot = near_blk * capacity + recv_rank

    adjoint = sensitivity.astype(jnp.float32)
    inner = inner_step(tissue, fiber_angle, potential, sensitivity)
    picker = expanders(brick_edge, plane_cells).reshape(4 * brick_edge, plane_cells).T.astype(jnp.float32)

    def boundary(values):
        picked = jnp.dot(
            values.astype(jnp.float32).reshape(bricks * z_layers, plane_cells),
            picker,
            precision=lax.Precision.HIGHEST,
        )
        return picked.reshape(bricks, z_layers, 4, brick_edge).transpose(0, 2, 1, 3)

    tissue_faces = boundary(tissue)
    cos_faces = jnp.cos(boundary(fiber_angle)) ** 2
    factor_faces = jnp.concatenate(
        [
            ACROSS + (ALONG - ACROSS) * cos_faces[:, :2],
            ACROSS + (ALONG - ACROSS) * (1.0 - cos_faces[:, 2:]),
        ],
        axis=1,
    )
    fields = jnp.stack(
        [tissue_faces * factor_faces, boundary(potential), boundary(sensitivity)], axis=2
    )
    flattened = fields.reshape(face_count, 3 * face_cells)
    outgoing = jnp.zeros((blocks * capacity, 3 * face_cells), jnp.float32).at[send_slot].set(flattened)
    shifted = [conductance] + [
        lax.ppermute(conductance, "par", [(i, (i + s) % parts) for i in range(parts)])
        for s in range(1, parts)
    ]
    source = (lax.axis_index("par") - jnp.arange(parts, dtype=jnp.int32)) % parts
    extra = jnp.concatenate([jnp.stack(shifted)[source].reshape(-1), brick_cell.astype(jnp.float32)])
    width = capacity * 3 * face_cells
    extra_width = -(-extra.shape[0] // 128) * 128
    extra = jnp.pad(extra, (0, extra_width - extra.shape[0]))
    sending = jnp.concatenate(
        [outgoing.reshape(blocks, width), jnp.broadcast_to(extra[None], (blocks, extra_width))], axis=1
    )
    arrived = lax.all_to_all(sending, "blk", split_axis=0, concat_axis=0, tiled=True)
    received = arrived[:, :width]
    par_cells = own_cells * parts
    cond_all = arrived[:, width : width + par_cells].reshape(-1)
    cell_all = arrived[:, width + par_cells : width + par_cells + bricks].reshape(-1).astype(jnp.int32)
    faces = received.reshape(blocks * capacity, 3 * face_cells)[recv_slot].reshape(
        bricks, 4, 3 * face_cells
    )

    size = lax.axis_size("par")
    up = [(i, i + 1) for i in range(size - 1)]
    down = [(j, i) for i, j in up]
    last = jnp.stack([tissue[:, -1].astype(jnp.float32), potential[:, -1], adjoint[:, -1]], axis=1)
    initial = jnp.stack([tissue[:, 0].astype(jnp.float32), potential[:, 0], adjoint[:, 0]], axis=1)
    halos = jnp.concatenate([lax.ppermute(last, "par", up), lax.ppermute(initial, "par", down)], axis=1)

    tables = (cond_all, cell_all, brick_cell, near_slot.reshape(-1))
    final, adjoint, parts_out = outer_step(tables, potential, sensitivity, inner, faces, halos)
    brick_part = jnp.sum(parts_out, axis=(1, 2))
    onehot_cells = brick_cell[:, None] == jnp.arange(cell_count, dtype=jnp.int32)[None, :]
    shares = jnp.sum(jnp.where(onehot_cells, brick_part[:, None], 0.0), axis=0)
    grad_share = jnp.sum(
        lax.all_to_all(
            shares.reshape(devices, own_cells), ("blk", "par"), split_axis=0, concat_axis=0, tiled=True
        ),
        axis=0,
    )
    cell_gradient = TIMESTEP * grad_share / (conductance * float(BX) ** 1.5)
    return (final, adjoint, cell_gradient)


def solution(mesh):
    placed = (
        P("blk", "par", None),
        P("blk", "par", None),
        P("blk", "par", None),
        P("blk", "par", None),
        P(("blk", "par")),
        P(),
        P("blk", None),
        P("blk"),
    )
    return jax.shard_map(
        body,
        mesh=mesh,
        in_specs=placed,
        out_specs=(P("blk", "par", None), P("blk", "par", None), P(("blk", "par"))),
        check_vma=False,
    )
```

```python
import jax
import jax.numpy as jnp
from jax import lax
from jax.sharding import PartitionSpec as P
from jax.experimental import pallas as pl
from jax.experimental.pallas import tpu as pltpu

BX = 32
STEPS = 1


TIMESTEP = 0.12
THRESHOLD = 0.2
ACROSS = 0.3
ALONG = 1.0
VERTICAL = 0.6


def extended(x, sides, width):
    for axis, dim in sides:
        size, length = (lax.axis_size(axis), x.shape[dim])
        up = [(i, (i + 1) % size) for i in range(size - 1)]
        down = [(j, i) for i, j in up]
        last = lax.slice_in_dim(x, length - width, length, axis=dim)
        initial = lax.slice_in_dim(x, 0, width, axis=dim)
        before = lax.ppermute(last, axis, up)
        after = lax.ppermute(initial, axis, down)
        x = jnp.concatenate([before, x, after], axis=dim)
    return x


def layers(values, brick_edge):
    return jnp.stack(
        [
            values[..., :brick_edge],
            values[..., -brick_edge:],
            values[..., 0::brick_edge],
            values[..., brick_edge - 1 :: brick_edge],
        ],
        axis=1,
    )


def along_x(values, lower_face, upper_face, brick_edge):
    return (
        jnp.concatenate([lower_face, values[..., :-brick_edge]], -1),
        jnp.concatenate([values[..., brick_edge:], upper_face], -1),
    )


def along_y(values, lower_face, upper_face, brick_edge):
    y_index = jnp.arange(values.shape[-1]) % brick_edge
    zero_pad = jnp.zeros(values.shape[:-1] + (1,), values.dtype)
    shifted_down = jnp.concatenate([zero_pad, values[..., :-1]], -1)
    shifted_up = jnp.concatenate([values[..., 1:], zero_pad], -1)
    return (
        jnp.where(y_index == 0, jnp.repeat(lower_face, brick_edge, axis=-1), shifted_down),
        jnp.where(
            y_index == brick_edge - 1, jnp.repeat(upper_face, brick_edge, axis=-1), shifted_up
        ),
    )


def near_values(values, layer_set, padded, brick_edge):
    x_low, x_high = along_x(values, layer_set[:, 0], layer_set[:, 1], brick_edge)
    y_low, y_high = along_y(values, layer_set[:, 2], layer_set[:, 3], brick_edge)
    return (x_low, x_high, y_low, y_high, padded[:, :-2], padded[:, 2:])


def laplace(conduct, values, beside):
    summed = conduct[0] * (beside[0] - values)
    for facet in range(1, 6):
        summed = summed + conduct[facet] * (beside[facet] - values)
    return summed


def brick_terms(conduct, adjoint, beside_adjoint, earlier, beside_state):
    summed = -conduct[0] * (adjoint - beside_adjoint[0]) * (earlier - beside_state[0])
    for facet in range(1, 6):
        summed = summed - conduct[facet] * (adjoint - beside_adjoint[facet]) * (
            earlier - beside_state[facet]
        )
    return jnp.sum(summed, axis=(1, 2))


def weights(tissue, fiber_angle, brick_scale):
    present = tissue.astype(jnp.float32)
    cos_square = jnp.cos(fiber_angle.astype(jnp.float32)) ** 2
    weight_x = present * brick_scale * (ACROSS + (ALONG - ACROSS) * cos_square)
    weight_y = present * brick_scale * (ACROSS + (ALONG - ACROSS) * (1.0 - cos_square))
    weight_z = present * brick_scale * VERTICAL
    return (weight_x, weight_y, weight_z)


def conductances(weight_x, weight_y, weight_z, weight_near, padded_z, brick_edge):
    x_low, x_high = along_x(weight_x, weight_near[:, 0], weight_near[:, 1], brick_edge)
    y_low, y_high = along_y(weight_y, weight_near[:, 2], weight_near[:, 3], brick_edge)
    return (
        weight_x * x_low,
        weight_x * x_high,
        weight_y * y_low,
        weight_y * y_high,
        weight_z * padded_z[:, :-2],
        weight_z * padded_z[:, 2:],
    )


GROUP = 8


def expanders(edge, cells):
    lane = jnp.arange(cells, dtype=jnp.int32)[None, :]
    k = jnp.arange(edge, dtype=jnp.int32)[:, None]
    return jnp.stack(
        [lane == k, lane == cells - edge + k, lane == edge * k, lane == edge * k + edge - 1]
    )


def cell_kernel(scale_ref, expand_ref, tissue_ref, angle_ref, u_ref, l_ref, face_ref, halo_ref,
                u_out, l_out, part_out):
    g = pl.program_id(0)
    nz, cells = u_ref.shape[1], u_ref.shape[2]
    edge = face_ref.shape[-1]
    lane = lax.broadcasted_iota(jnp.int32, (nz, cells), 1)
    row = lax.broadcasted_iota(jnp.int32, (nz, cells), 0)
    ycoord = lane % edge
    masks = (lane < edge, lane >= cells - edge, ycoord == 0, ycoord == edge - 1)
    shifts = (edge, cells - edge, 1, cells - 1)
    zlo = row == 0
    zhi = row == nz - 1

    def one(i, carry):
        b = g * GROUP + i
        th = scale_ref[b, 0]
        present = tissue_ref[i].astype(jnp.float32)
        c = jnp.cos(angle_ref[i].astype(jnp.float32))
        c2 = c * c
        scaled = present * th
        wx = scaled * (ACROSS + (ALONG - ACROSS) * c2)
        wy = scaled * (ACROSS + (ALONG - ACROSS) * (1.0 - c2))
        wz = scaled * VERTICAL
        u = u_ref[i]
        l = l_ref[i].astype(jnp.float32)
        halo = halo_ref[i]
        conds, ub, lb = [], [], []
        for f in range(4):
            face = face_ref[i, f]
            high = face.astype(jnp.bfloat16)
            rest = face - high.astype(jnp.float32)
            middle = rest.astype(jnp.bfloat16)
            low = (rest - middle.astype(jnp.float32)).astype(jnp.bfloat16)
            ext = jnp.dot(high, expand_ref[f], preferred_element_type=jnp.float32)
            ext = ext + jnp.dot(middle, expand_ref[f], preferred_element_type=jnp.float32)
            ext = ext + jnp.dot(low, expand_ref[f], preferred_element_type=jnp.float32)
            w_self = wx if f < 2 else wy
            w_near = jnp.where(masks[f], scale_ref[b, 1 + f] * ext[:nz], pltpu.roll(w_self, shifts[f], 1))
            conds.append(w_self * w_near)
            ub.append(jnp.where(masks[f], ext[nz:2 * nz], pltpu.roll(u, shifts[f], 1)))
            lb.append(jnp.where(masks[f], ext[2 * nz:3 * nz], pltpu.roll(l, shifts[f], 1)))
        wz_lo = jnp.where(zlo, (halo[0:1] * th) * VERTICAL, pltpu.roll(wz, 1, 0))
        wz_hi = jnp.where(zhi, (halo[3:4] * th) * VERTICAL, pltpu.roll(wz, nz - 1, 0))
        conds += [wz * wz_lo, wz * wz_hi]
        ub += [jnp.where(zlo, halo[1:2], pltpu.roll(u, 1, 0)), jnp.where(zhi, halo[4:5], pltpu.roll(u, nz - 1, 0))]
        lb += [jnp.where(zlo, halo[2:3], pltpu.roll(l, 1, 0)), jnp.where(zhi, halo[5:6], pltpu.roll(l, nz - 1, 0))]
        lap_u = conds[0] * (ub[0] - u)
        lap_l = conds[0] * (lb[0] - l)
        terms = lap_l * (ub[0] - u)
        for k in range(1, 6):
            step_u = ub[k] - u
            step_l = conds[k] * (lb[k] - l)
            lap_u = lap_u + conds[k] * step_u
            lap_l = lap_l + step_l
            terms = terms + step_l * step_u
        ionic = u * (1.0 - u) * (u - THRESHOLD)
        slope = -3.0 * u * u + 2.0 * (1.0 + THRESHOLD) * u - THRESHOLD
        u_out[i] = u + TIMESTEP * (lap_u + ionic)
        l_out[i] = l + TIMESTEP * (lap_l + slope * l)
        col = -jnp.sum(terms, axis=0, keepdims=True)
        acc = col[:, 0:128]
        for t in range(1, cells // 128):
            acc = acc + col[:, t * 128:(t + 1) * 128]
        part_out[i] = acc
        return carry

    lax.fori_loop(0, GROUP, one, 0)


def cell_step(scales, tissue, angle, potential, sensitivity, faces, halos, interpret=False):
    bricks, nz, cells = potential.shape
    edge = faces.shape[-1]
    expand = expanders(edge, cells).astype(jnp.bfloat16)
    blk3 = lambda: pl.BlockSpec((GROUP, nz, cells), lambda g: (g, 0, 0))
    return pl.pallas_call(
        cell_kernel,
        grid=(bricks // GROUP,),
        in_specs=[
            pl.BlockSpec(memory_space=pltpu.SMEM),
            pl.BlockSpec((4, edge, cells), lambda g: (0, 0, 0)),
            blk3(), blk3(), blk3(), blk3(),
            pl.BlockSpec((GROUP, 4, faces.shape[2], edge), lambda g: (g, 0, 0, 0)),
            pl.BlockSpec((GROUP, 6, cells), lambda g: (g, 0, 0)),
        ],
        out_specs=[blk3(), blk3(), pl.BlockSpec((GROUP, 1, 128), lambda g: (g, 0, 0))],
        out_shape=[
            jax.ShapeDtypeStruct((bricks, nz, cells), jnp.float32),
            jax.ShapeDtypeStruct((bricks, nz, cells), jnp.float32),
            jax.ShapeDtypeStruct((bricks, 1, 128), jnp.float32),
        ],
        compiler_params=pltpu.CompilerParams(dimension_semantics=("parallel",)),
        interpret=interpret,
    )(scales, expand, tissue, angle, potential, sensitivity, faces, halos)


def group_sum(values):
    col = jnp.sum(values, axis=0, keepdims=True)
    acc = col[:, 0:128]
    for t in range(1, values.shape[1] // 128):
        acc = acc + col[:, t * 128:(t + 1) * 128]
    return acc


def inner_kernel(tissue_ref, angle_ref, u_ref, l_ref, lu_out, ll_out, gx_out, gy_out, part_out):
    nz, cells = u_ref.shape[1], u_ref.shape[2]
    edge = BX
    lane = lax.broadcasted_iota(jnp.int32, (nz, cells), 1)
    row = lax.broadcasted_iota(jnp.int32, (nz, cells), 0)
    ycoord = lane % edge
    inside = (lane >= edge, lane < cells - edge, ycoord != 0, ycoord != edge - 1, row != 0, row != nz - 1)
    shifts = ((edge, 1), (cells - edge, 1), (1, 1), (cells - 1, 1), (1, 0), (nz - 1, 0))

    def one(i, carry):
        present = tissue_ref[i].astype(jnp.float32)
        c = jnp.cos(angle_ref[i].astype(jnp.float32))
        c2 = c * c
        gx = present * (ACROSS + (ALONG - ACROSS) * c2)
        gy = present * (ACROSS + (ALONG - ACROSS) * (1.0 - c2))
        gz = present * VERTICAL
        u = u_ref[i]
        l = l_ref[i].astype(jnp.float32)
        lap_u = jnp.zeros_like(u)
        lap_l = jnp.zeros_like(u)
        terms = jnp.zeros_like(u)
        for k in range(6):
            g = gx if k < 2 else (gy if k < 4 else gz)
            shift, axis = shifts[k]
            conduct = jnp.where(inside[k], g * pltpu.roll(g, shift, axis), 0.0)
            step_u = pltpu.roll(u, shift, axis) - u
            step_l = conduct * (pltpu.roll(l, shift, axis) - l)
            lap_u = lap_u + conduct * step_u
            lap_l = lap_l + step_l
            terms = terms + step_l * step_u
        lu_out[i] = lap_u
        ll_out[i] = lap_l
        gx_out[i] = gx
        gy_out[i] = gy
        part_out[i] = group_sum(terms)
        return carry

    lax.fori_loop(0, GROUP, one, 0)


def outer_kernel(cond_ref, cell_ref, own_ref, near_ref, expand_ref, u_ref, l_ref, lu_ref, ll_ref, gx_ref, gy_ref, inner_ref, face_ref,
                 halo_ref, u_out, l_out, part_out, ext_ref):
    g = pl.program_id(0)
    nz, cells = u_ref.shape[1], u_ref.shape[2]
    edge = BX
    rows = 8 * nz
    for f in range(4):
        face = face_ref[:, f]
        part = face[:, :2 * nz]
        high = part.astype(jnp.bfloat16).astype(jnp.float32)
        rest = part - high
        middle = rest.astype(jnp.bfloat16).astype(jnp.float32)
        low = (rest - middle).astype(jnp.bfloat16).astype(jnp.float32)
        stacked = jnp.concatenate(
            [high, middle, low, face[:, 2 * nz:3 * nz], jnp.zeros_like(face[:, :nz])], axis=1
        )
        ext_ref[f] = jnp.dot(
            stacked.reshape(GROUP * rows, edge).astype(jnp.bfloat16),
            expand_ref[f],
            preferred_element_type=jnp.float32,
        )
    lane = lax.broadcasted_iota(jnp.int32, (nz, cells), 1)
    row = lax.broadcasted_iota(jnp.int32, (nz, cells), 0)
    ycoord = lane % edge
    masks = (lane < edge, lane >= cells - edge, ycoord == 0, ycoord == edge - 1)

    chunk = 256
    lane = lax.broadcasted_iota(jnp.int32, (nz, chunk), 1)
    row = lax.broadcasted_iota(jnp.int32, (nz, chunk), 0)
    ycoord = lane % edge

    def one(i, carry):
        b = g * GROUP + i
        th = cond_ref[own_ref[b]]
        near_th = [cond_ref[cell_ref[near_ref[4 * b + f]]] for f in range(4)]
        square = th * th
        base = pl.multiple_of(i * rows, rows)
        total = -square * inner_ref[i]
        for c in range(cells // chunk):
            cols = slice(c * chunk, (c + 1) * chunk)
            at = lane + c * chunk
            masks = (at < edge, at >= cells - edge, ycoord == 0, ycoord == edge - 1)
            u = u_ref[i, :, cols]
            l = l_ref[i, :, cols].astype(jnp.float32)
            gx = gx_ref[i, :, cols]
            gy = gy_ref[i, :, cols]
            halo = halo_ref[i, :, cols]
            edge_u, edge_l, edge_t = [], [], []
            for side, r in ((0, 0), (1, nz - 1)):
                own_z = (gx[r:r + 1] != 0.0).astype(jnp.float32) * VERTICAL
                conduct = own_z * (halo[3 * side:3 * side + 1] * VERTICAL)
                step_u = halo[3 * side + 1:3 * side + 2] - u[r:r + 1]
                step_l = conduct * (halo[3 * side + 2:3 * side + 3] - l[r:r + 1])
                edge_u.append(conduct * step_u)
                edge_l.append(step_l)
                edge_t.append(step_l * step_u)
            lap_u = lu_ref[i, :, cols] + jnp.where(row == 0, edge_u[0], 0.0) + jnp.where(row == nz - 1, edge_u[1], 0.0)
            lap_l = ll_ref[i, :, cols] + jnp.where(row == 0, edge_l[0], 0.0) + jnp.where(row == nz - 1, edge_l[1], 0.0)
            face_u = jnp.zeros_like(u)
            face_l = jnp.zeros_like(u)
            face_t = jnp.zeros_like(u)
            for f in range(4):
                piece = lambda k: ext_ref[f, pl.ds(base + k * nz, nz), cols]
                near_w = (piece(0) + piece(2)) + piece(4)
                near_u = (piece(1) + piece(3)) + piece(5)
                near_l = piece(6)
                g_self = gx if f < 2 else gy
                conduct = jnp.where(masks[f], near_th[f] * (g_self * near_w), 0.0)
                step_u = near_u - u
                step_l = conduct * (near_l - l)
                face_u = face_u + conduct * step_u
                face_l = face_l + step_l
                face_t = face_t + step_l * step_u
            ionic = u * (1.0 - u) * (u - THRESHOLD)
            slope = -3.0 * u * u + 2.0 * (1.0 + THRESHOLD) * u - THRESHOLD
            u_out[i, :, cols] = u + TIMESTEP * ((square * lap_u + th * face_u) + ionic)
            l_out[i, :, cols] = l + TIMESTEP * ((square * lap_l + th * face_l) + slope * l)
            total = total - (square * (group_sum(edge_t[0]) + group_sum(edge_t[1])) + th * group_sum(face_t))
        part_out[i] = total
        return carry

    lax.fori_loop(0, GROUP, one, 0)


def inner_step(tissue, angle, potential, sensitivity, interpret=False):
    bricks, nz, cells = potential.shape
    blk3 = lambda: pl.BlockSpec((GROUP, nz, cells), lambda g: (g, 0, 0))
    full = jax.ShapeDtypeStruct((bricks, nz, cells), jnp.float32)
    return pl.pallas_call(
        inner_kernel,
        grid=(bricks // GROUP,),
        in_specs=[blk3(), blk3(), blk3(), blk3()],
        out_specs=[blk3(), blk3(), blk3(), blk3(), pl.BlockSpec((GROUP, 1, 128), lambda g: (g, 0, 0))],
        out_shape=[full, full, full, full, jax.ShapeDtypeStruct((bricks, 1, 128), jnp.float32)],
        compiler_params=pltpu.CompilerParams(dimension_semantics=("parallel",)),
        interpret=interpret,
    )(tissue, angle, potential, sensitivity)


def outer_step(tables, potential, sensitivity, inner, faces, halos, interpret=False):
    bricks, nz, cells = potential.shape
    edge = faces.shape[-1]
    expand = expanders(edge, cells).astype(jnp.bfloat16)
    blk3 = lambda: pl.BlockSpec((GROUP, nz, cells), lambda g: (g, 0, 0))
    lap_u, lap_l, gx, gy, inner_part = inner
    return pl.pallas_call(
        outer_kernel,
        grid=(bricks // GROUP,),
        in_specs=[pl.BlockSpec(memory_space=pltpu.SMEM) for _ in tables] + [
            pl.BlockSpec((4, edge, cells), lambda g: (0, 0, 0)),
            blk3(), blk3(), blk3(), blk3(), blk3(), blk3(),
            pl.BlockSpec((GROUP, 1, 128), lambda g: (g, 0, 0)),
            pl.BlockSpec((GROUP, 4, faces.shape[2], edge), lambda g: (g, 0, 0, 0)),
            pl.BlockSpec((GROUP, 6, cells), lambda g: (g, 0, 0)),
        ],
        out_specs=[blk3(), blk3(), pl.BlockSpec((GROUP, 1, 128), lambda g: (g, 0, 0))],
        out_shape=[
            jax.ShapeDtypeStruct((bricks, nz, cells), jnp.float32),
            jax.ShapeDtypeStruct((bricks, nz, cells), jnp.float32),
            jax.ShapeDtypeStruct((bricks, 1, 128), jnp.float32),
        ],
        scratch_shapes=[pltpu.VMEM((4, GROUP * 8 * nz, cells), jnp.float32)],
        compiler_params=pltpu.CompilerParams(dimension_semantics=("parallel",)),
        interpret=interpret,
    )(*tables, expand, potential, sensitivity, lap_u, lap_l, gx, gy, inner_part, faces, halos)


def body(
    potential, fiber_angle, tissue, sensitivity, conductance, brick_slot, neighbours, brick_cell
):
    bricks, z_layers, plane_cells = potential.shape
    brick_edge = BX
    blocks = lax.axis_size("blk")
    parts = lax.axis_size("par")
    devices = blocks * parts
    capacity = max(4, 8 * bricks // blocks)
    face_count = 4 * bricks
    face_cells = z_layers * brick_edge
    own_cells = conductance.shape[0]
    cell_count = own_cells * devices
    opposite = jnp.array([1, 0, 3, 2], jnp.int32)

    near_slot = brick_slot[neighbours]
    near_blk = (near_slot // bricks).reshape(-1)
    far_key = (near_slot % bricks * 4 + opposite[None, :]).reshape(-1)
    own_key = jnp.arange(face_count, dtype=jnp.int32)
    matches = near_blk[:, None] == near_blk[None, :]
    send_rank = jnp.sum((matches & (own_key[None, :] < own_key[:, None])).astype(jnp.int32), axis=1)
    recv_rank = jnp.sum((matches & (far_key[None, :] < far_key[:, None])).astype(jnp.int32), axis=1)
    send_slot = near_blk * capacity + send_rank
    recv_slot = near_blk * capacity + recv_rank

    adjoint = sensitivity.astype(jnp.float32)
    inner = inner_step(tissue, fiber_angle, potential, sensitivity)
    picker = expanders(brick_edge, plane_cells).reshape(4 * brick_edge, plane_cells).T.astype(jnp.float32)

    def boundary(values):
        picked = jnp.dot(
            values.astype(jnp.float32).reshape(bricks * z_layers, plane_cells),
            picker,
            precision=lax.Precision.HIGHEST,
        )
        return picked.reshape(bricks, z_layers, 4, brick_edge).transpose(0, 2, 1, 3)

    tissue_faces = boundary(tissue)
    cos_faces = jnp.cos(boundary(fiber_angle)) ** 2
    factor_faces = jnp.concatenate(
        [
            ACROSS + (ALONG - ACROSS) * cos_faces[:, :2],
            ACROSS + (ALONG - ACROSS) * (1.0 - cos_faces[:, 2:]),
        ],
        axis=1,
    )
    fields = jnp.stack(
        [tissue_faces * factor_faces, boundary(potential), boundary(sensitivity)], axis=2
    )
    flattened = fields.reshape(face_count, 3 * face_cells)
    outgoing = jnp.zeros((blocks * capacity, 3 * face_cells), jnp.float32).at[send_slot].set(flattened)
    shifted = [conductance] + [
        lax.ppermute(conductance, "par", [(i, (i + s) % parts) for i in range(parts)])
        for s in range(1, parts)
    ]
    source = (lax.axis_index("par") - jnp.arange(parts, dtype=jnp.int32)) % parts
    extra = jnp.concatenate([jnp.stack(shifted)[source].reshape(-1), brick_cell.astype(jnp.float32)])
    width = capacity * 3 * face_cells
    extra_width = -(-extra.shape[0] // 128) * 128
    extra = jnp.pad(extra, (0, extra_width - extra.shape[0]))
    sending = jnp.concatenate(
        [outgoing.reshape(blocks, width), jnp.broadcast_to(extra[None], (blocks, extra_width))], axis=1
    )
    arrived = lax.all_to_all(sending, "blk", split_axis=0, concat_axis=0, tiled=True)
    received = arrived[:, :width]
    par_cells = own_cells * parts
    cond_all = arrived[:, width : width + par_cells].reshape(-1)
    cell_all = arrived[:, width + par_cells : width + par_cells + bricks].reshape(-1).astype(jnp.int32)
    faces = received.reshape(blocks * capacity, 3 * face_cells)[recv_slot].reshape(
        bricks, 4, 3 * z_layers, brick_edge
    )

    size = lax.axis_size("par")
    up = [(i, i + 1) for i in range(size - 1)]
    down = [(j, i) for i, j in up]
    last = jnp.stack([tissue[:, -1].astype(jnp.float32), potential[:, -1], adjoint[:, -1]], axis=1)
    initial = jnp.stack([tissue[:, 0].astype(jnp.float32), potential[:, 0], adjoint[:, 0]], axis=1)
    halos = jnp.concatenate([lax.ppermute(last, "par", up), lax.ppermute(initial, "par", down)], axis=1)

    tables = (cond_all, cell_all, brick_cell, near_slot.reshape(-1))
    final, adjoint, parts_out = outer_step(tables, potential, sensitivity, inner, faces, halos)
    brick_part = jnp.sum(parts_out, axis=(1, 2))
    onehot_cells = brick_cell[:, None] == jnp.arange(cell_count, dtype=jnp.int32)[None, :]
    shares = jnp.sum(jnp.where(onehot_cells, brick_part[:, None], 0.0), axis=0)
    grad_share = jnp.sum(
        lax.all_to_all(
            shares.reshape(devices, own_cells), ("blk", "par"), split_axis=0, concat_axis=0, tiled=True
        ),
        axis=0,
    )
    cell_gradient = TIMESTEP * grad_share / (conductance * float(BX) ** 1.5)
    return (final, adjoint, cell_gradient)


def solution(mesh):
    placed = (
        P("blk", "par", None),
        P("blk", "par", None),
        P("blk", "par", None),
        P("blk", "par", None),
        P(("blk", "par")),
        P(),
        P("blk", None),
        P("blk"),
    )
    return jax.shard_map(
        body,
        mesh=mesh,
        in_specs=placed,
        out_specs=(P("blk", "par", None), P("blk", "par", None), P(("blk", "par"))),
        check_vma=False,
    )
```

```python
import jax
import jax.numpy as jnp
from jax import lax
from jax.sharding import PartitionSpec as P
from jax.experimental import pallas as pl
from jax.experimental.pallas import tpu as pltpu

BX = 32
STEPS = 1


TIMESTEP = 0.12
THRESHOLD = 0.2
ACROSS = 0.3
ALONG = 1.0
VERTICAL = 0.6


def extended(x, sides, width):
    for axis, dim in sides:
        size, length = (lax.axis_size(axis), x.shape[dim])
        up = [(i, (i + 1) % size) for i in range(size - 1)]
        down = [(j, i) for i, j in up]
        last = lax.slice_in_dim(x, length - width, length, axis=dim)
        initial = lax.slice_in_dim(x, 0, width, axis=dim)
        before = lax.ppermute(last, axis, up)
        after = lax.ppermute(initial, axis, down)
        x = jnp.concatenate([before, x, after], axis=dim)
    return x


def layers(values, brick_edge):
    return jnp.stack(
        [
            values[..., :brick_edge],
            values[..., -brick_edge:],
            values[..., 0::brick_edge],
            values[..., brick_edge - 1 :: brick_edge],
        ],
        axis=1,
    )


def along_x(values, lower_face, upper_face, brick_edge):
    return (
        jnp.concatenate([lower_face, values[..., :-brick_edge]], -1),
        jnp.concatenate([values[..., brick_edge:], upper_face], -1),
    )


def along_y(values, lower_face, upper_face, brick_edge):
    y_index = jnp.arange(values.shape[-1]) % brick_edge
    zero_pad = jnp.zeros(values.shape[:-1] + (1,), values.dtype)
    shifted_down = jnp.concatenate([zero_pad, values[..., :-1]], -1)
    shifted_up = jnp.concatenate([values[..., 1:], zero_pad], -1)
    return (
        jnp.where(y_index == 0, jnp.repeat(lower_face, brick_edge, axis=-1), shifted_down),
        jnp.where(
            y_index == brick_edge - 1, jnp.repeat(upper_face, brick_edge, axis=-1), shifted_up
        ),
    )


def near_values(values, layer_set, padded, brick_edge):
    x_low, x_high = along_x(values, layer_set[:, 0], layer_set[:, 1], brick_edge)
    y_low, y_high = along_y(values, layer_set[:, 2], layer_set[:, 3], brick_edge)
    return (x_low, x_high, y_low, y_high, padded[:, :-2], padded[:, 2:])


def laplace(conduct, values, beside):
    summed = conduct[0] * (beside[0] - values)
    for facet in range(1, 6):
        summed = summed + conduct[facet] * (beside[facet] - values)
    return summed


def brick_terms(conduct, adjoint, beside_adjoint, earlier, beside_state):
    summed = -conduct[0] * (adjoint - beside_adjoint[0]) * (earlier - beside_state[0])
    for facet in range(1, 6):
        summed = summed - conduct[facet] * (adjoint - beside_adjoint[facet]) * (
            earlier - beside_state[facet]
        )
    return jnp.sum(summed, axis=(1, 2))


def weights(tissue, fiber_angle, brick_scale):
    present = tissue.astype(jnp.float32)
    cos_square = jnp.cos(fiber_angle.astype(jnp.float32)) ** 2
    weight_x = present * brick_scale * (ACROSS + (ALONG - ACROSS) * cos_square)
    weight_y = present * brick_scale * (ACROSS + (ALONG - ACROSS) * (1.0 - cos_square))
    weight_z = present * brick_scale * VERTICAL
    return (weight_x, weight_y, weight_z)


def conductances(weight_x, weight_y, weight_z, weight_near, padded_z, brick_edge):
    x_low, x_high = along_x(weight_x, weight_near[:, 0], weight_near[:, 1], brick_edge)
    y_low, y_high = along_y(weight_y, weight_near[:, 2], weight_near[:, 3], brick_edge)
    return (
        weight_x * x_low,
        weight_x * x_high,
        weight_y * y_low,
        weight_y * y_high,
        weight_z * padded_z[:, :-2],
        weight_z * padded_z[:, 2:],
    )


GROUP = 8


def expanders(edge, cells):
    lane = jnp.arange(cells, dtype=jnp.int32)[None, :]
    k = jnp.arange(edge, dtype=jnp.int32)[:, None]
    return jnp.stack(
        [lane == k, lane == cells - edge + k, lane == edge * k, lane == edge * k + edge - 1]
    )


def cell_kernel(scale_ref, expand_ref, tissue_ref, angle_ref, u_ref, l_ref, face_ref, halo_ref,
                u_out, l_out, part_out):
    g = pl.program_id(0)
    nz, cells = u_ref.shape[1], u_ref.shape[2]
    edge = face_ref.shape[-1]
    lane = lax.broadcasted_iota(jnp.int32, (nz, cells), 1)
    row = lax.broadcasted_iota(jnp.int32, (nz, cells), 0)
    ycoord = lane % edge
    masks = (lane < edge, lane >= cells - edge, ycoord == 0, ycoord == edge - 1)
    shifts = (edge, cells - edge, 1, cells - 1)
    zlo = row == 0
    zhi = row == nz - 1

    def one(i, carry):
        b = g * GROUP + i
        th = scale_ref[b, 0]
        present = tissue_ref[i].astype(jnp.float32)
        c = jnp.cos(angle_ref[i].astype(jnp.float32))
        c2 = c * c
        scaled = present * th
        wx = scaled * (ACROSS + (ALONG - ACROSS) * c2)
        wy = scaled * (ACROSS + (ALONG - ACROSS) * (1.0 - c2))
        wz = scaled * VERTICAL
        u = u_ref[i]
        l = l_ref[i].astype(jnp.float32)
        halo = halo_ref[i]
        conds, ub, lb = [], [], []
        for f in range(4):
            face = face_ref[i, f]
            high = face.astype(jnp.bfloat16)
            rest = face - high.astype(jnp.float32)
            middle = rest.astype(jnp.bfloat16)
            low = (rest - middle.astype(jnp.float32)).astype(jnp.bfloat16)
            ext = jnp.dot(high, expand_ref[f], preferred_element_type=jnp.float32)
            ext = ext + jnp.dot(middle, expand_ref[f], preferred_element_type=jnp.float32)
            ext = ext + jnp.dot(low, expand_ref[f], preferred_element_type=jnp.float32)
            w_self = wx if f < 2 else wy
            w_near = jnp.where(masks[f], scale_ref[b, 1 + f] * ext[:nz], pltpu.roll(w_self, shifts[f], 1))
            conds.append(w_self * w_near)
            ub.append(jnp.where(masks[f], ext[nz:2 * nz], pltpu.roll(u, shifts[f], 1)))
            lb.append(jnp.where(masks[f], ext[2 * nz:3 * nz], pltpu.roll(l, shifts[f], 1)))
        wz_lo = jnp.where(zlo, (halo[0:1] * th) * VERTICAL, pltpu.roll(wz, 1, 0))
        wz_hi = jnp.where(zhi, (halo[3:4] * th) * VERTICAL, pltpu.roll(wz, nz - 1, 0))
        conds += [wz * wz_lo, wz * wz_hi]
        ub += [jnp.where(zlo, halo[1:2], pltpu.roll(u, 1, 0)), jnp.where(zhi, halo[4:5], pltpu.roll(u, nz - 1, 0))]
        lb += [jnp.where(zlo, halo[2:3], pltpu.roll(l, 1, 0)), jnp.where(zhi, halo[5:6], pltpu.roll(l, nz - 1, 0))]
        lap_u = conds[0] * (ub[0] - u)
        lap_l = conds[0] * (lb[0] - l)
        terms = lap_l * (ub[0] - u)
        for k in range(1, 6):
            step_u = ub[k] - u
            step_l = conds[k] * (lb[k] - l)
            lap_u = lap_u + conds[k] * step_u
            lap_l = lap_l + step_l
            terms = terms + step_l * step_u
        ionic = u * (1.0 - u) * (u - THRESHOLD)
        slope = -3.0 * u * u + 2.0 * (1.0 + THRESHOLD) * u - THRESHOLD
        u_out[i] = u + TIMESTEP * (lap_u + ionic)
        l_out[i] = l + TIMESTEP * (lap_l + slope * l)
        col = -jnp.sum(terms, axis=0, keepdims=True)
        acc = col[:, 0:128]
        for t in range(1, cells // 128):
            acc = acc + col[:, t * 128:(t + 1) * 128]
        part_out[i] = acc
        return carry

    lax.fori_loop(0, GROUP, one, 0)


def cell_step(scales, tissue, angle, potential, sensitivity, faces, halos, interpret=False):
    bricks, nz, cells = potential.shape
    edge = faces.shape[-1]
    expand = expanders(edge, cells).astype(jnp.bfloat16)
    blk3 = lambda: pl.BlockSpec((GROUP, nz, cells), lambda g: (g, 0, 0))
    return pl.pallas_call(
        cell_kernel,
        grid=(bricks // GROUP,),
        in_specs=[
            pl.BlockSpec(memory_space=pltpu.SMEM),
            pl.BlockSpec((4, edge, cells), lambda g: (0, 0, 0)),
            blk3(), blk3(), blk3(), blk3(),
            pl.BlockSpec((GROUP, 4, faces.shape[2], edge), lambda g: (g, 0, 0, 0)),
            pl.BlockSpec((GROUP, 6, cells), lambda g: (g, 0, 0)),
        ],
        out_specs=[blk3(), blk3(), pl.BlockSpec((GROUP, 1, 128), lambda g: (g, 0, 0))],
        out_shape=[
            jax.ShapeDtypeStruct((bricks, nz, cells), jnp.float32),
            jax.ShapeDtypeStruct((bricks, nz, cells), jnp.float32),
            jax.ShapeDtypeStruct((bricks, 1, 128), jnp.float32),
        ],
        compiler_params=pltpu.CompilerParams(dimension_semantics=("parallel",)),
        interpret=interpret,
    )(scales, expand, tissue, angle, potential, sensitivity, faces, halos)


def group_sum(values):
    col = jnp.sum(values, axis=0, keepdims=True)
    acc = col[:, 0:128]
    for t in range(1, values.shape[1] // 128):
        acc = acc + col[:, t * 128:(t + 1) * 128]
    return acc


def inner_kernel(tissue_ref, angle_ref, u_ref, l_ref, lu_out, ll_out, gx_out, part_out):
    nz, cells = u_ref.shape[1], u_ref.shape[2]
    edge = BX
    lane = lax.broadcasted_iota(jnp.int32, (nz, cells), 1)
    row = lax.broadcasted_iota(jnp.int32, (nz, cells), 0)
    ycoord = lane % edge
    inside = (lane >= edge, lane < cells - edge, ycoord != 0, ycoord != edge - 1, row != 0, row != nz - 1)
    shifts = ((edge, 1), (cells - edge, 1), (1, 1), (cells - 1, 1), (1, 0), (nz - 1, 0))

    def one(i, carry):
        present = tissue_ref[i].astype(jnp.float32)
        c = jnp.cos(angle_ref[i].astype(jnp.float32))
        c2 = c * c
        gx = present * (ACROSS + (ALONG - ACROSS) * c2)
        gy = present * (ACROSS + (ALONG - ACROSS) * (1.0 - c2))
        gz = present * VERTICAL
        u = u_ref[i]
        l = l_ref[i].astype(jnp.float32)
        lap_u = jnp.zeros_like(u)
        lap_l = jnp.zeros_like(u)
        terms = jnp.zeros_like(u)
        for k in range(6):
            g = gx if k < 2 else (gy if k < 4 else gz)
            shift, axis = shifts[k]
            conduct = jnp.where(inside[k], g * pltpu.roll(g, shift, axis), 0.0)
            step_u = pltpu.roll(u, shift, axis) - u
            step_l = conduct * (pltpu.roll(l, shift, axis) - l)
            lap_u = lap_u + conduct * step_u
            lap_l = lap_l + step_l
            terms = terms + step_l * step_u
        lu_out[i] = lap_u
        ll_out[i] = lap_l
        gx_out[i] = gx
        part_out[i] = group_sum(terms)
        return carry

    lax.fori_loop(0, GROUP, one, 0)


def outer_kernel(cond_ref, cell_ref, own_ref, near_ref, expand_ref, u_ref, l_ref, lu_ref, ll_ref, gx_ref, inner_ref, face_ref,
                 halo_ref, u_out, l_out, part_out, ext_ref):
    g = pl.program_id(0)
    nz, cells = u_ref.shape[1], u_ref.shape[2]
    edge = BX
    rows = 8 * nz
    for f in range(4):
        face = face_ref[:, f]
        part = face[:, :2 * nz]
        high = part.astype(jnp.bfloat16).astype(jnp.float32)
        rest = part - high
        middle = rest.astype(jnp.bfloat16).astype(jnp.float32)
        low = (rest - middle).astype(jnp.bfloat16).astype(jnp.float32)
        stacked = jnp.concatenate(
            [high, middle, low, face[:, 2 * nz:3 * nz], jnp.zeros_like(face[:, :nz])], axis=1
        )
        ext_ref[f] = jnp.dot(
            stacked.reshape(GROUP * rows, edge).astype(jnp.bfloat16),
            expand_ref[f],
            preferred_element_type=jnp.float32,
        )
    lane = lax.broadcasted_iota(jnp.int32, (nz, cells), 1)
    row = lax.broadcasted_iota(jnp.int32, (nz, cells), 0)
    ycoord = lane % edge
    masks = (lane < edge, lane >= cells - edge, ycoord == 0, ycoord == edge - 1)

    chunk = 256
    lane = lax.broadcasted_iota(jnp.int32, (nz, chunk), 1)
    row = lax.broadcasted_iota(jnp.int32, (nz, chunk), 0)
    ycoord = lane % edge

    def one(i, carry):
        b = g * GROUP + i
        th = cond_ref[own_ref[b]]
        near_th = [cond_ref[cell_ref[near_ref[4 * b + f]]] for f in range(4)]
        square = th * th
        base = pl.multiple_of(i * rows, rows)
        total = -square * inner_ref[i]
        for c in range(cells // chunk):
            cols = slice(c * chunk, (c + 1) * chunk)
            at = lane + c * chunk
            masks = (at < edge, at >= cells - edge, ycoord == 0, ycoord == edge - 1)
            u = u_ref[i, :, cols]
            l = l_ref[i, :, cols].astype(jnp.float32)
            gx = gx_ref[i, :, cols]
            gy = jnp.where(gx != 0.0, (ALONG + ACROSS) - gx, 0.0)
            halo = halo_ref[i, :, cols]
            edge_u, edge_l, edge_t = [], [], []
            for side, r in ((0, 0), (1, nz - 1)):
                own_z = (gx[r:r + 1] != 0.0).astype(jnp.float32) * VERTICAL
                conduct = own_z * (halo[3 * side:3 * side + 1] * VERTICAL)
                step_u = halo[3 * side + 1:3 * side + 2] - u[r:r + 1]
                step_l = conduct * (halo[3 * side + 2:3 * side + 3] - l[r:r + 1])
                edge_u.append(conduct * step_u)
                edge_l.append(step_l)
                edge_t.append(step_l * step_u)
            lap_u = lu_ref[i, :, cols] + jnp.where(row == 0, edge_u[0], 0.0) + jnp.where(row == nz - 1, edge_u[1], 0.0)
            lap_l = ll_ref[i, :, cols] + jnp.where(row == 0, edge_l[0], 0.0) + jnp.where(row == nz - 1, edge_l[1], 0.0)
            face_u = jnp.zeros_like(u)
            face_l = jnp.zeros_like(u)
            face_t = jnp.zeros_like(u)
            for f in range(4):
                piece = lambda k: ext_ref[f, pl.ds(base + k * nz, nz), cols]
                near_w = (piece(0) + piece(2)) + piece(4)
                near_u = (piece(1) + piece(3)) + piece(5)
                near_l = piece(6)
                g_self = gx if f < 2 else gy
                conduct = jnp.where(masks[f], near_th[f] * (g_self * near_w), 0.0)
                step_u = near_u - u
                step_l = conduct * (near_l - l)
                face_u = face_u + conduct * step_u
                face_l = face_l + step_l
                face_t = face_t + step_l * step_u
            ionic = u * (1.0 - u) * (u - THRESHOLD)
            slope = -3.0 * u * u + 2.0 * (1.0 + THRESHOLD) * u - THRESHOLD
            u_out[i, :, cols] = u + TIMESTEP * ((square * lap_u + th * face_u) + ionic)
            l_out[i, :, cols] = l + TIMESTEP * ((square * lap_l + th * face_l) + slope * l)
            total = total - (square * (group_sum(edge_t[0]) + group_sum(edge_t[1])) + th * group_sum(face_t))
        part_out[i] = total
        return carry

    lax.fori_loop(0, GROUP, one, 0)


def inner_step(tissue, angle, potential, sensitivity, interpret=False):
    bricks, nz, cells = potential.shape
    blk3 = lambda: pl.BlockSpec((GROUP, nz, cells), lambda g: (g, 0, 0))
    full = jax.ShapeDtypeStruct((bricks, nz, cells), jnp.float32)
    return pl.pallas_call(
        inner_kernel,
        grid=(bricks // GROUP,),
        in_specs=[blk3(), blk3(), blk3(), blk3()],
        out_specs=[blk3(), blk3(), blk3(), pl.BlockSpec((GROUP, 1, 128), lambda g: (g, 0, 0))],
        out_shape=[full, full, full, jax.ShapeDtypeStruct((bricks, 1, 128), jnp.float32)],
        compiler_params=pltpu.CompilerParams(dimension_semantics=("parallel",)),
        interpret=interpret,
    )(tissue, angle, potential, sensitivity)


def outer_step(tables, potential, sensitivity, inner, faces, halos, interpret=False):
    bricks, nz, cells = potential.shape
    edge = faces.shape[-1]
    expand = expanders(edge, cells).astype(jnp.bfloat16)
    blk3 = lambda: pl.BlockSpec((GROUP, nz, cells), lambda g: (g, 0, 0))
    lap_u, lap_l, gx, inner_part = inner
    return pl.pallas_call(
        outer_kernel,
        grid=(bricks // GROUP,),
        in_specs=[pl.BlockSpec(memory_space=pltpu.SMEM) for _ in tables] + [
            pl.BlockSpec((4, edge, cells), lambda g: (0, 0, 0)),
            blk3(), blk3(), blk3(), blk3(), blk3(),
            pl.BlockSpec((GROUP, 1, 128), lambda g: (g, 0, 0)),
            pl.BlockSpec((GROUP, 4, faces.shape[2], edge), lambda g: (g, 0, 0, 0)),
            pl.BlockSpec((GROUP, 6, cells), lambda g: (g, 0, 0)),
        ],
        out_specs=[blk3(), blk3(), pl.BlockSpec((GROUP, 1, 128), lambda g: (g, 0, 0))],
        out_shape=[
            jax.ShapeDtypeStruct((bricks, nz, cells), jnp.float32),
            jax.ShapeDtypeStruct((bricks, nz, cells), jnp.float32),
            jax.ShapeDtypeStruct((bricks, 1, 128), jnp.float32),
        ],
        scratch_shapes=[pltpu.VMEM((4, GROUP * 8 * nz, cells), jnp.float32)],
        compiler_params=pltpu.CompilerParams(dimension_semantics=("parallel",)),
        interpret=interpret,
    )(*tables, expand, potential, sensitivity, lap_u, lap_l, gx, inner_part, faces, halos)


def body(
    potential, fiber_angle, tissue, sensitivity, conductance, brick_slot, neighbours, brick_cell
):
    bricks, z_layers, plane_cells = potential.shape
    brick_edge = BX
    blocks = lax.axis_size("blk")
    parts = lax.axis_size("par")
    devices = blocks * parts
    capacity = max(4, 8 * bricks // blocks)
    face_count = 4 * bricks
    face_cells = z_layers * brick_edge
    own_cells = conductance.shape[0]
    cell_count = own_cells * devices
    opposite = jnp.array([1, 0, 3, 2], jnp.int32)

    near_slot = brick_slot[neighbours]
    near_blk = (near_slot // bricks).reshape(-1)
    far_key = (near_slot % bricks * 4 + opposite[None, :]).reshape(-1)
    own_key = jnp.arange(face_count, dtype=jnp.int32)
    matches = near_blk[:, None] == near_blk[None, :]
    send_rank = jnp.sum((matches & (own_key[None, :] < own_key[:, None])).astype(jnp.int32), axis=1)
    recv_rank = jnp.sum((matches & (far_key[None, :] < far_key[:, None])).astype(jnp.int32), axis=1)
    send_slot = near_blk * capacity + send_rank
    recv_slot = near_blk * capacity + recv_rank

    adjoint = sensitivity.astype(jnp.float32)
    inner = inner_step(tissue, fiber_angle, potential, sensitivity)
    picker = expanders(brick_edge, plane_cells).reshape(4 * brick_edge, plane_cells).T.astype(jnp.float32)

    def boundary(values):
        picked = jnp.dot(
            values.astype(jnp.float32).reshape(bricks * z_layers, plane_cells),
            picker,
            precision=lax.Precision.HIGHEST,
        )
        return picked.reshape(bricks, z_layers, 4, brick_edge).transpose(0, 2, 1, 3)

    tissue_faces = boundary(tissue)
    cos_faces = jnp.cos(boundary(fiber_angle)) ** 2
    factor_faces = jnp.concatenate(
        [
            ACROSS + (ALONG - ACROSS) * cos_faces[:, :2],
            ACROSS + (ALONG - ACROSS) * (1.0 - cos_faces[:, 2:]),
        ],
        axis=1,
    )
    fields = jnp.stack(
        [tissue_faces * factor_faces, boundary(potential), boundary(sensitivity)], axis=2
    )
    flattened = fields.reshape(face_count, 3 * face_cells)
    outgoing = jnp.zeros((blocks * capacity, 3 * face_cells), jnp.float32).at[send_slot].set(flattened)
    shifted = [conductance] + [
        lax.ppermute(conductance, "par", [(i, (i + s) % parts) for i in range(parts)])
        for s in range(1, parts)
    ]
    source = (lax.axis_index("par") - jnp.arange(parts, dtype=jnp.int32)) % parts
    extra = jnp.concatenate([jnp.stack(shifted)[source].reshape(-1), brick_cell.astype(jnp.float32)])
    width = capacity * 3 * face_cells
    extra_width = -(-extra.shape[0] // 128) * 128
    extra = jnp.pad(extra, (0, extra_width - extra.shape[0]))
    sending = jnp.concatenate(
        [outgoing.reshape(blocks, width), jnp.broadcast_to(extra[None], (blocks, extra_width))], axis=1
    )
    arrived = lax.all_to_all(sending, "blk", split_axis=0, concat_axis=0, tiled=True)
    received = arrived[:, :width]
    par_cells = own_cells * parts
    cond_all = arrived[:, width : width + par_cells].reshape(-1)
    cell_all = arrived[:, width + par_cells : width + par_cells + bricks].reshape(-1).astype(jnp.int32)
    faces = received.reshape(blocks * capacity, 3 * face_cells)[recv_slot].reshape(
        bricks, 4, 3 * z_layers, brick_edge
    )

    size = lax.axis_size("par")
    up = [(i, i + 1) for i in range(size - 1)]
    down = [(j, i) for i, j in up]
    last = jnp.stack([tissue[:, -1].astype(jnp.float32), potential[:, -1], adjoint[:, -1]], axis=1)
    initial = jnp.stack([tissue[:, 0].astype(jnp.float32), potential[:, 0], adjoint[:, 0]], axis=1)
    halos = jnp.concatenate([lax.ppermute(last, "par", up), lax.ppermute(initial, "par", down)], axis=1)

    tables = (cond_all, cell_all, brick_cell, near_slot.reshape(-1))
    final, adjoint, parts_out = outer_step(tables, potential, sensitivity, inner, faces, halos)
    brick_part = jnp.sum(parts_out, axis=(1, 2))
    onehot_cells = brick_cell[:, None] == jnp.arange(cell_count, dtype=jnp.int32)[None, :]
    shares = jnp.sum(jnp.where(onehot_cells, brick_part[:, None], 0.0), axis=0)
    grad_share = jnp.sum(
        lax.all_to_all(
            shares.reshape(devices, own_cells), ("blk", "par"), split_axis=0, concat_axis=0, tiled=True
        ),
        axis=0,
    )
    cell_gradient = TIMESTEP * grad_share / (conductance * float(BX) ** 1.5)
    return (final, adjoint, cell_gradient)


def solution(mesh):
    placed = (
        P("blk", "par", None),
        P("blk", "par", None),
        P("blk", "par", None),
        P("blk", "par", None),
        P(("blk", "par")),
        P(),
        P("blk", None),
        P("blk"),
    )
    return jax.shard_map(
        body,
        mesh=mesh,
        in_specs=placed,
        out_specs=(P("blk", "par", None), P("blk", "par", None), P(("blk", "par"))),
        check_vma=False,
    )
```

```python
import jax
import jax.numpy as jnp
from jax import lax
from jax.sharding import PartitionSpec as P
from jax.experimental import pallas as pl
from jax.experimental.pallas import tpu as pltpu

BX = 32
STEPS = 1


TIMESTEP = 0.12
THRESHOLD = 0.2
ACROSS = 0.3
ALONG = 1.0
VERTICAL = 0.6


def extended(x, sides, width):
    for axis, dim in sides:
        size, length = (lax.axis_size(axis), x.shape[dim])
        up = [(i, (i + 1) % size) for i in range(size - 1)]
        down = [(j, i) for i, j in up]
        last = lax.slice_in_dim(x, length - width, length, axis=dim)
        initial = lax.slice_in_dim(x, 0, width, axis=dim)
        before = lax.ppermute(last, axis, up)
        after = lax.ppermute(initial, axis, down)
        x = jnp.concatenate([before, x, after], axis=dim)
    return x


def layers(values, brick_edge):
    return jnp.stack(
        [
            values[..., :brick_edge],
            values[..., -brick_edge:],
            values[..., 0::brick_edge],
            values[..., brick_edge - 1 :: brick_edge],
        ],
        axis=1,
    )


def along_x(values, lower_face, upper_face, brick_edge):
    return (
        jnp.concatenate([lower_face, values[..., :-brick_edge]], -1),
        jnp.concatenate([values[..., brick_edge:], upper_face], -1),
    )


def along_y(values, lower_face, upper_face, brick_edge):
    y_index = jnp.arange(values.shape[-1]) % brick_edge
    zero_pad = jnp.zeros(values.shape[:-1] + (1,), values.dtype)
    shifted_down = jnp.concatenate([zero_pad, values[..., :-1]], -1)
    shifted_up = jnp.concatenate([values[..., 1:], zero_pad], -1)
    return (
        jnp.where(y_index == 0, jnp.repeat(lower_face, brick_edge, axis=-1), shifted_down),
        jnp.where(
            y_index == brick_edge - 1, jnp.repeat(upper_face, brick_edge, axis=-1), shifted_up
        ),
    )


def near_values(values, layer_set, padded, brick_edge):
    x_low, x_high = along_x(values, layer_set[:, 0], layer_set[:, 1], brick_edge)
    y_low, y_high = along_y(values, layer_set[:, 2], layer_set[:, 3], brick_edge)
    return (x_low, x_high, y_low, y_high, padded[:, :-2], padded[:, 2:])


def laplace(conduct, values, beside):
    summed = conduct[0] * (beside[0] - values)
    for facet in range(1, 6):
        summed = summed + conduct[facet] * (beside[facet] - values)
    return summed


def brick_terms(conduct, adjoint, beside_adjoint, earlier, beside_state):
    summed = -conduct[0] * (adjoint - beside_adjoint[0]) * (earlier - beside_state[0])
    for facet in range(1, 6):
        summed = summed - conduct[facet] * (adjoint - beside_adjoint[facet]) * (
            earlier - beside_state[facet]
        )
    return jnp.sum(summed, axis=(1, 2))


def weights(tissue, fiber_angle, brick_scale):
    present = tissue.astype(jnp.float32)
    cos_square = jnp.cos(fiber_angle.astype(jnp.float32)) ** 2
    weight_x = present * brick_scale * (ACROSS + (ALONG - ACROSS) * cos_square)
    weight_y = present * brick_scale * (ACROSS + (ALONG - ACROSS) * (1.0 - cos_square))
    weight_z = present * brick_scale * VERTICAL
    return (weight_x, weight_y, weight_z)


def conductances(weight_x, weight_y, weight_z, weight_near, padded_z, brick_edge):
    x_low, x_high = along_x(weight_x, weight_near[:, 0], weight_near[:, 1], brick_edge)
    y_low, y_high = along_y(weight_y, weight_near[:, 2], weight_near[:, 3], brick_edge)
    return (
        weight_x * x_low,
        weight_x * x_high,
        weight_y * y_low,
        weight_y * y_high,
        weight_z * padded_z[:, :-2],
        weight_z * padded_z[:, 2:],
    )


GROUP = 8


def expanders(edge, cells):
    lane = jnp.arange(cells, dtype=jnp.int32)[None, :]
    k = jnp.arange(edge, dtype=jnp.int32)[:, None]
    return jnp.stack(
        [lane == k, lane == cells - edge + k, lane == edge * k, lane == edge * k + edge - 1]
    )


def cell_kernel(scale_ref, expand_ref, tissue_ref, angle_ref, u_ref, l_ref, face_ref, halo_ref,
                u_out, l_out, part_out):
    g = pl.program_id(0)
    nz, cells = u_ref.shape[1], u_ref.shape[2]
    edge = face_ref.shape[-1]
    lane = lax.broadcasted_iota(jnp.int32, (nz, cells), 1)
    row = lax.broadcasted_iota(jnp.int32, (nz, cells), 0)
    ycoord = lane % edge
    masks = (lane < edge, lane >= cells - edge, ycoord == 0, ycoord == edge - 1)
    shifts = (edge, cells - edge, 1, cells - 1)
    zlo = row == 0
    zhi = row == nz - 1

    def one(i, carry):
        b = g * GROUP + i
        th = scale_ref[b, 0]
        present = tissue_ref[i].astype(jnp.float32)
        c = jnp.cos(angle_ref[i].astype(jnp.float32))
        c2 = c * c
        scaled = present * th
        wx = scaled * (ACROSS + (ALONG - ACROSS) * c2)
        wy = scaled * (ACROSS + (ALONG - ACROSS) * (1.0 - c2))
        wz = scaled * VERTICAL
        u = u_ref[i]
        l = l_ref[i].astype(jnp.float32)
        halo = halo_ref[i]
        conds, ub, lb = [], [], []
        for f in range(4):
            face = face_ref[i, f]
            high = face.astype(jnp.bfloat16)
            rest = face - high.astype(jnp.float32)
            middle = rest.astype(jnp.bfloat16)
            low = (rest - middle.astype(jnp.float32)).astype(jnp.bfloat16)
            ext = jnp.dot(high, expand_ref[f], preferred_element_type=jnp.float32)
            ext = ext + jnp.dot(middle, expand_ref[f], preferred_element_type=jnp.float32)
            ext = ext + jnp.dot(low, expand_ref[f], preferred_element_type=jnp.float32)
            w_self = wx if f < 2 else wy
            w_near = jnp.where(masks[f], scale_ref[b, 1 + f] * ext[:nz], pltpu.roll(w_self, shifts[f], 1))
            conds.append(w_self * w_near)
            ub.append(jnp.where(masks[f], ext[nz:2 * nz], pltpu.roll(u, shifts[f], 1)))
            lb.append(jnp.where(masks[f], ext[2 * nz:3 * nz], pltpu.roll(l, shifts[f], 1)))
        wz_lo = jnp.where(zlo, (halo[0:1] * th) * VERTICAL, pltpu.roll(wz, 1, 0))
        wz_hi = jnp.where(zhi, (halo[3:4] * th) * VERTICAL, pltpu.roll(wz, nz - 1, 0))
        conds += [wz * wz_lo, wz * wz_hi]
        ub += [jnp.where(zlo, halo[1:2], pltpu.roll(u, 1, 0)), jnp.where(zhi, halo[4:5], pltpu.roll(u, nz - 1, 0))]
        lb += [jnp.where(zlo, halo[2:3], pltpu.roll(l, 1, 0)), jnp.where(zhi, halo[5:6], pltpu.roll(l, nz - 1, 0))]
        lap_u = conds[0] * (ub[0] - u)
        lap_l = conds[0] * (lb[0] - l)
        terms = lap_l * (ub[0] - u)
        for k in range(1, 6):
            step_u = ub[k] - u
            step_l = conds[k] * (lb[k] - l)
            lap_u = lap_u + conds[k] * step_u
            lap_l = lap_l + step_l
            terms = terms + step_l * step_u
        ionic = u * (1.0 - u) * (u - THRESHOLD)
        slope = -3.0 * u * u + 2.0 * (1.0 + THRESHOLD) * u - THRESHOLD
        u_out[i] = u + TIMESTEP * (lap_u + ionic)
        l_out[i] = l + TIMESTEP * (lap_l + slope * l)
        col = -jnp.sum(terms, axis=0, keepdims=True)
        acc = col[:, 0:128]
        for t in range(1, cells // 128):
            acc = acc + col[:, t * 128:(t + 1) * 128]
        part_out[i] = acc
        return carry

    lax.fori_loop(0, GROUP, one, 0)


def cell_step(scales, tissue, angle, potential, sensitivity, faces, halos, interpret=False):
    bricks, nz, cells = potential.shape
    edge = faces.shape[-1]
    expand = expanders(edge, cells).astype(jnp.bfloat16)
    blk3 = lambda: pl.BlockSpec((GROUP, nz, cells), lambda g: (g, 0, 0))
    return pl.pallas_call(
        cell_kernel,
        grid=(bricks // GROUP,),
        in_specs=[
            pl.BlockSpec(memory_space=pltpu.SMEM),
            pl.BlockSpec((4, edge, cells), lambda g: (0, 0, 0)),
            blk3(), blk3(), blk3(), blk3(),
            pl.BlockSpec((GROUP, 4, faces.shape[2], edge), lambda g: (g, 0, 0, 0)),
            pl.BlockSpec((GROUP, 6, cells), lambda g: (g, 0, 0)),
        ],
        out_specs=[blk3(), blk3(), pl.BlockSpec((GROUP, 1, 128), lambda g: (g, 0, 0))],
        out_shape=[
            jax.ShapeDtypeStruct((bricks, nz, cells), jnp.float32),
            jax.ShapeDtypeStruct((bricks, nz, cells), jnp.float32),
            jax.ShapeDtypeStruct((bricks, 1, 128), jnp.float32),
        ],
        compiler_params=pltpu.CompilerParams(dimension_semantics=("parallel",)),
        interpret=interpret,
    )(scales, expand, tissue, angle, potential, sensitivity, faces, halos)


def group_sum(values):
    col = jnp.sum(values, axis=0, keepdims=True)
    acc = col[:, 0:128]
    for t in range(1, values.shape[1] // 128):
        acc = acc + col[:, t * 128:(t + 1) * 128]
    return acc


def inner_kernel(tissue_ref, angle_ref, u_ref, l_ref, lu_out, ll_out, gx_out, part_out):
    nz, cells = u_ref.shape[1], u_ref.shape[2]
    edge = BX
    lane = lax.broadcasted_iota(jnp.int32, (nz, cells), 1)
    row = lax.broadcasted_iota(jnp.int32, (nz, cells), 0)
    ycoord = lane % edge
    inside = (lane >= edge, lane < cells - edge, ycoord != 0, ycoord != edge - 1, row != 0, row != nz - 1)
    shifts = ((edge, 1), (cells - edge, 1), (1, 1), (cells - 1, 1), (1, 0), (nz - 1, 0))

    def one(i, carry):
        present = tissue_ref[i].astype(jnp.float32)
        c = jnp.cos(angle_ref[i].astype(jnp.float32))
        c2 = c * c
        gx = present * (ACROSS + (ALONG - ACROSS) * c2)
        gy = present * (ACROSS + (ALONG - ACROSS) * (1.0 - c2))
        gz = present * VERTICAL
        u = u_ref[i]
        l = l_ref[i].astype(jnp.float32)
        lap_u = jnp.zeros_like(u)
        lap_l = jnp.zeros_like(u)
        terms = jnp.zeros_like(u)
        for k in range(6):
            g = gx if k < 2 else (gy if k < 4 else gz)
            shift, axis = shifts[k]
            conduct = jnp.where(inside[k], g * pltpu.roll(g, shift, axis), 0.0)
            step_u = pltpu.roll(u, shift, axis) - u
            step_l = conduct * (pltpu.roll(l, shift, axis) - l)
            lap_u = lap_u + conduct * step_u
            lap_l = lap_l + step_l
            terms = terms + step_l * step_u
        lu_out[i] = lap_u
        ll_out[i] = lap_l
        gx_out[i] = gx
        part_out[i] = group_sum(terms)
        return carry

    lax.fori_loop(0, GROUP, one, 0)


def outer_kernel(table_ref, own_ref, near_ref, expand_ref, u_ref, l_ref, lu_ref, ll_ref, gx_ref, inner_ref, face_ref,
                 halo_ref, u_out, l_out, part_out, ext_ref):
    g = pl.program_id(0)
    nz, cells = u_ref.shape[1], u_ref.shape[2]
    edge = BX
    rows = 8 * nz
    for f in range(4):
        face = face_ref[:, f]
        part = face[:, :2 * nz]
        high = part.astype(jnp.bfloat16).astype(jnp.float32)
        rest = part - high
        middle = rest.astype(jnp.bfloat16).astype(jnp.float32)
        low = (rest - middle).astype(jnp.bfloat16).astype(jnp.float32)
        stacked = jnp.concatenate(
            [high, middle, low, face[:, 2 * nz:3 * nz], jnp.zeros_like(face[:, :nz])], axis=1
        )
        ext_ref[f] = jnp.dot(
            stacked.reshape(GROUP * rows, edge).astype(jnp.bfloat16),
            expand_ref[f],
            preferred_element_type=jnp.float32,
        )
    lane = lax.broadcasted_iota(jnp.int32, (nz, cells), 1)
    row = lax.broadcasted_iota(jnp.int32, (nz, cells), 0)
    ycoord = lane % edge
    masks = (lane < edge, lane >= cells - edge, ycoord == 0, ycoord == edge - 1)

    chunk = 256
    lane = lax.broadcasted_iota(jnp.int32, (nz, chunk), 1)
    row = lax.broadcasted_iota(jnp.int32, (nz, chunk), 0)
    ycoord = lane % edge

    def one(i, carry):
        b = g * GROUP + i
        width = table_ref.shape[1] - own_ref.shape[0]

        def cond_of(q):
            return table_ref[q // width, q % width]

        def cell_of(s):
            return table_ref[s // own_ref.shape[0], width + s % own_ref.shape[0]].astype(jnp.int32)

        th = cond_of(own_ref[b])
        near_th = [cond_of(cell_of(near_ref[4 * b + f])) for f in range(4)]
        square = th * th
        base = pl.multiple_of(i * rows, rows)
        total = -square * inner_ref[i]
        for c in range(cells // chunk):
            cols = slice(c * chunk, (c + 1) * chunk)
            at = lane + c * chunk
            masks = (at < edge, at >= cells - edge, ycoord == 0, ycoord == edge - 1)
            u = u_ref[i, :, cols]
            l = l_ref[i, :, cols].astype(jnp.float32)
            gx = gx_ref[i, :, cols]
            gy = jnp.where(gx != 0.0, (ALONG + ACROSS) - gx, 0.0)
            halo = halo_ref[i, :, cols]
            edge_u, edge_l, edge_t = [], [], []
            for side, r in ((0, 0), (1, nz - 1)):
                own_z = (gx[r:r + 1] != 0.0).astype(jnp.float32) * VERTICAL
                conduct = own_z * (halo[3 * side:3 * side + 1] * VERTICAL)
                step_u = halo[3 * side + 1:3 * side + 2] - u[r:r + 1]
                step_l = conduct * (halo[3 * side + 2:3 * side + 3] - l[r:r + 1])
                edge_u.append(conduct * step_u)
                edge_l.append(step_l)
                edge_t.append(step_l * step_u)
            lap_u = lu_ref[i, :, cols] + jnp.where(row == 0, edge_u[0], 0.0) + jnp.where(row == nz - 1, edge_u[1], 0.0)
            lap_l = ll_ref[i, :, cols] + jnp.where(row == 0, edge_l[0], 0.0) + jnp.where(row == nz - 1, edge_l[1], 0.0)
            face_u = jnp.zeros_like(u)
            face_l = jnp.zeros_like(u)
            face_t = jnp.zeros_like(u)
            for f in range(4):
                piece = lambda k: ext_ref[f, pl.ds(base + k * nz, nz), cols]
                near_w = (piece(0) + piece(2)) + piece(4)
                near_u = (piece(1) + piece(3)) + piece(5)
                near_l = piece(6)
                g_self = gx if f < 2 else gy
                conduct = jnp.where(masks[f], near_th[f] * (g_self * near_w), 0.0)
                step_u = near_u - u
                step_l = conduct * (near_l - l)
                face_u = face_u + conduct * step_u
                face_l = face_l + step_l
                face_t = face_t + step_l * step_u
            ionic = u * (1.0 - u) * (u - THRESHOLD)
            slope = -3.0 * u * u + 2.0 * (1.0 + THRESHOLD) * u - THRESHOLD
            u_out[i, :, cols] = u + TIMESTEP * ((square * lap_u + th * face_u) + ionic)
            l_out[i, :, cols] = l + TIMESTEP * ((square * lap_l + th * face_l) + slope * l)
            total = total - (square * (group_sum(edge_t[0]) + group_sum(edge_t[1])) + th * group_sum(face_t))
        part_out[i] = total
        return carry

    lax.fori_loop(0, GROUP, one, 0)


def inner_step(tissue, angle, potential, sensitivity, interpret=False):
    bricks, nz, cells = potential.shape
    blk3 = lambda: pl.BlockSpec((GROUP, nz, cells), lambda g: (g, 0, 0))
    full = jax.ShapeDtypeStruct((bricks, nz, cells), jnp.float32)
    return pl.pallas_call(
        inner_kernel,
        grid=(bricks // GROUP,),
        in_specs=[blk3(), blk3(), blk3(), blk3()],
        out_specs=[blk3(), blk3(), blk3(), pl.BlockSpec((GROUP, 1, 128), lambda g: (g, 0, 0))],
        out_shape=[full, full, full, jax.ShapeDtypeStruct((bricks, 1, 128), jnp.float32)],
        compiler_params=pltpu.CompilerParams(dimension_semantics=("parallel",)),
        interpret=interpret,
    )(tissue, angle, potential, sensitivity)


def outer_step(tables, potential, sensitivity, inner, faces, halos, interpret=False):
    bricks, nz, cells = potential.shape
    edge = faces.shape[-1]
    expand = expanders(edge, cells).astype(jnp.bfloat16)
    blk3 = lambda: pl.BlockSpec((GROUP, nz, cells), lambda g: (g, 0, 0))
    lap_u, lap_l, gx, inner_part = inner
    return pl.pallas_call(
        outer_kernel,
        grid=(bricks // GROUP,),
        in_specs=[pl.BlockSpec(memory_space=pltpu.SMEM) for _ in tables] + [
            pl.BlockSpec((4, edge, cells), lambda g: (0, 0, 0)),
            blk3(), blk3(), blk3(), blk3(), blk3(),
            pl.BlockSpec((GROUP, 1, 128), lambda g: (g, 0, 0)),
            pl.BlockSpec((GROUP, 4, faces.shape[2], edge), lambda g: (g, 0, 0, 0)),
            pl.BlockSpec((GROUP, 6, cells), lambda g: (g, 0, 0)),
        ],
        out_specs=[blk3(), blk3(), pl.BlockSpec((GROUP, 1, 128), lambda g: (g, 0, 0))],
        out_shape=[
            jax.ShapeDtypeStruct((bricks, nz, cells), jnp.float32),
            jax.ShapeDtypeStruct((bricks, nz, cells), jnp.float32),
            jax.ShapeDtypeStruct((bricks, 1, 128), jnp.float32),
        ],
        scratch_shapes=[pltpu.VMEM((4, GROUP * 8 * nz, cells), jnp.float32)],
        compiler_params=pltpu.CompilerParams(dimension_semantics=("parallel",)),
        interpret=interpret,
    )(*tables, expand, potential, sensitivity, lap_u, lap_l, gx, inner_part, faces, halos)


def body(
    potential, fiber_angle, tissue, sensitivity, conductance, brick_slot, neighbours, brick_cell
):
    bricks, z_layers, plane_cells = potential.shape
    brick_edge = BX
    blocks = lax.axis_size("blk")
    parts = lax.axis_size("par")
    devices = blocks * parts
    capacity = max(4, 8 * bricks // blocks)
    face_count = 4 * bricks
    face_cells = z_layers * brick_edge
    own_cells = conductance.shape[0]
    cell_count = own_cells * devices
    opposite = jnp.array([1, 0, 3, 2], jnp.int32)

    near_slot = brick_slot[neighbours]
    near_blk = (near_slot // bricks).reshape(-1)
    far_key = (near_slot % bricks * 4 + opposite[None, :]).reshape(-1)
    own_key = jnp.arange(face_count, dtype=jnp.int32)
    matches = near_blk[:, None] == near_blk[None, :]
    send_rank = jnp.sum((matches & (own_key[None, :] < own_key[:, None])).astype(jnp.int32), axis=1)
    recv_rank = jnp.sum((matches & (far_key[None, :] < far_key[:, None])).astype(jnp.int32), axis=1)
    send_slot = near_blk * capacity + send_rank
    recv_slot = near_blk * capacity + recv_rank

    adjoint = sensitivity.astype(jnp.float32)
    inner = inner_step(tissue, fiber_angle, potential, sensitivity)
    picker = expanders(brick_edge, plane_cells).reshape(4 * brick_edge, plane_cells).T.astype(jnp.float32)

    def boundary(values):
        picked = jnp.dot(
            values.astype(jnp.float32).reshape(bricks * z_layers, plane_cells),
            picker,
            precision=lax.Precision.HIGHEST,
        )
        return picked.reshape(bricks, z_layers, 4, brick_edge).transpose(0, 2, 1, 3)

    tissue_faces = boundary(tissue)
    cos_faces = jnp.cos(boundary(fiber_angle)) ** 2
    factor_faces = jnp.concatenate(
        [
            ACROSS + (ALONG - ACROSS) * cos_faces[:, :2],
            ACROSS + (ALONG - ACROSS) * (1.0 - cos_faces[:, 2:]),
        ],
        axis=1,
    )
    fields = jnp.stack(
        [tissue_faces * factor_faces, boundary(potential), boundary(sensitivity)], axis=2
    )
    flattened = fields.reshape(face_count, 3 * face_cells)
    outgoing = jnp.zeros((blocks * capacity, 3 * face_cells), jnp.float32).at[send_slot].set(flattened)
    shifted = [conductance] + [
        lax.ppermute(conductance, "par", [(i, (i + s) % parts) for i in range(parts)])
        for s in range(1, parts)
    ]
    source = (lax.axis_index("par") - jnp.arange(parts, dtype=jnp.int32)) % parts
    extra = jnp.concatenate([jnp.stack(shifted)[source].reshape(-1), brick_cell.astype(jnp.float32)])
    width = capacity * 3 * face_cells
    extra_width = -(-extra.shape[0] // 128) * 128
    extra = jnp.pad(extra, (0, extra_width - extra.shape[0]))
    sending = jnp.concatenate(
        [outgoing.reshape(blocks, width), jnp.broadcast_to(extra[None], (blocks, extra_width))], axis=1
    )
    arrived = lax.all_to_all(sending, "blk", split_axis=0, concat_axis=0, tiled=True)
    received = arrived[:, :width]
    par_cells = own_cells * parts
    cond_all = arrived[:, width : width + par_cells].reshape(-1)
    cell_all = arrived[:, width + par_cells : width + par_cells + bricks].reshape(-1).astype(jnp.int32)
    faces = received.reshape(blocks * capacity, 3 * face_cells)[recv_slot].reshape(
        bricks, 4, 3 * z_layers, brick_edge
    )

    size = lax.axis_size("par")
    up = [(i, i + 1) for i in range(size - 1)]
    down = [(j, i) for i, j in up]
    last = jnp.stack([tissue[:, -1].astype(jnp.float32), potential[:, -1], adjoint[:, -1]], axis=1)
    initial = jnp.stack([tissue[:, 0].astype(jnp.float32), potential[:, 0], adjoint[:, 0]], axis=1)
    halos = jnp.concatenate([lax.ppermute(last, "par", up), lax.ppermute(initial, "par", down)], axis=1)

    tables = (arrived[:, width : width + par_cells + bricks], brick_cell, near_slot.reshape(-1))
    final, adjoint, parts_out = outer_step(tables, potential, sensitivity, inner, faces, halos)
    brick_part = jnp.sum(parts_out, axis=(1, 2))
    onehot_cells = brick_cell[:, None] == jnp.arange(cell_count, dtype=jnp.int32)[None, :]
    shares = jnp.sum(jnp.where(onehot_cells, brick_part[:, None], 0.0), axis=0)
    grad_share = jnp.sum(
        lax.all_to_all(
            shares.reshape(devices, own_cells), ("blk", "par"), split_axis=0, concat_axis=0, tiled=True
        ),
        axis=0,
    )
    cell_gradient = TIMESTEP * grad_share / (conductance * float(BX) ** 1.5)
    return (final, adjoint, cell_gradient)


def solution(mesh):
    placed = (
        P("blk", "par", None),
        P("blk", "par", None),
        P("blk", "par", None),
        P("blk", "par", None),
        P(("blk", "par")),
        P(),
        P("blk", None),
        P("blk"),
    )
    return jax.shard_map(
        body,
        mesh=mesh,
        in_specs=placed,
        out_specs=(P("blk", "par", None), P("blk", "par", None), P(("blk", "par"))),
        check_vma=False,
    )
```

```python
import jax
import jax.numpy as jnp
from jax import lax
from jax.sharding import PartitionSpec as P
from jax.experimental import pallas as pl
from jax.experimental.pallas import tpu as pltpu

BX = 32
STEPS = 1


TIMESTEP = 0.12
THRESHOLD = 0.2
ACROSS = 0.3
ALONG = 1.0
VERTICAL = 0.6


def extended(x, sides, width):
    for axis, dim in sides:
        size, length = (lax.axis_size(axis), x.shape[dim])
        up = [(i, (i + 1) % size) for i in range(size - 1)]
        down = [(j, i) for i, j in up]
        last = lax.slice_in_dim(x, length - width, length, axis=dim)
        initial = lax.slice_in_dim(x, 0, width, axis=dim)
        before = lax.ppermute(last, axis, up)
        after = lax.ppermute(initial, axis, down)
        x = jnp.concatenate([before, x, after], axis=dim)
    return x


def layers(values, brick_edge):
    return jnp.stack(
        [
            values[..., :brick_edge],
            values[..., -brick_edge:],
            values[..., 0::brick_edge],
            values[..., brick_edge - 1 :: brick_edge],
        ],
        axis=1,
    )


def along_x(values, lower_face, upper_face, brick_edge):
    return (
        jnp.concatenate([lower_face, values[..., :-brick_edge]], -1),
        jnp.concatenate([values[..., brick_edge:], upper_face], -1),
    )


def along_y(values, lower_face, upper_face, brick_edge):
    y_index = jnp.arange(values.shape[-1]) % brick_edge
    zero_pad = jnp.zeros(values.shape[:-1] + (1,), values.dtype)
    shifted_down = jnp.concatenate([zero_pad, values[..., :-1]], -1)
    shifted_up = jnp.concatenate([values[..., 1:], zero_pad], -1)
    return (
        jnp.where(y_index == 0, jnp.repeat(lower_face, brick_edge, axis=-1), shifted_down),
        jnp.where(
            y_index == brick_edge - 1, jnp.repeat(upper_face, brick_edge, axis=-1), shifted_up
        ),
    )


def near_values(values, layer_set, padded, brick_edge):
    x_low, x_high = along_x(values, layer_set[:, 0], layer_set[:, 1], brick_edge)
    y_low, y_high = along_y(values, layer_set[:, 2], layer_set[:, 3], brick_edge)
    return (x_low, x_high, y_low, y_high, padded[:, :-2], padded[:, 2:])


def laplace(conduct, values, beside):
    summed = conduct[0] * (beside[0] - values)
    for facet in range(1, 6):
        summed = summed + conduct[facet] * (beside[facet] - values)
    return summed


def brick_terms(conduct, adjoint, beside_adjoint, earlier, beside_state):
    summed = -conduct[0] * (adjoint - beside_adjoint[0]) * (earlier - beside_state[0])
    for facet in range(1, 6):
        summed = summed - conduct[facet] * (adjoint - beside_adjoint[facet]) * (
            earlier - beside_state[facet]
        )
    return jnp.sum(summed, axis=(1, 2))


def weights(tissue, fiber_angle, brick_scale):
    present = tissue.astype(jnp.float32)
    cos_square = jnp.cos(fiber_angle.astype(jnp.float32)) ** 2
    weight_x = present * brick_scale * (ACROSS + (ALONG - ACROSS) * cos_square)
    weight_y = present * brick_scale * (ACROSS + (ALONG - ACROSS) * (1.0 - cos_square))
    weight_z = present * brick_scale * VERTICAL
    return (weight_x, weight_y, weight_z)


def conductances(weight_x, weight_y, weight_z, weight_near, padded_z, brick_edge):
    x_low, x_high = along_x(weight_x, weight_near[:, 0], weight_near[:, 1], brick_edge)
    y_low, y_high = along_y(weight_y, weight_near[:, 2], weight_near[:, 3], brick_edge)
    return (
        weight_x * x_low,
        weight_x * x_high,
        weight_y * y_low,
        weight_y * y_high,
        weight_z * padded_z[:, :-2],
        weight_z * padded_z[:, 2:],
    )


GROUP = 8
OUTER = 4


def expanders(edge, cells):
    lane = jnp.arange(cells, dtype=jnp.int32)[None, :]
    k = jnp.arange(edge, dtype=jnp.int32)[:, None]
    return jnp.stack(
        [lane == k, lane == cells - edge + k, lane == edge * k, lane == edge * k + edge - 1]
    )


def cell_kernel(scale_ref, expand_ref, tissue_ref, angle_ref, u_ref, l_ref, face_ref, halo_ref,
                u_out, l_out, part_out):
    g = pl.program_id(0)
    nz, cells = u_ref.shape[1], u_ref.shape[2]
    edge = face_ref.shape[-1]
    lane = lax.broadcasted_iota(jnp.int32, (nz, cells), 1)
    row = lax.broadcasted_iota(jnp.int32, (nz, cells), 0)
    ycoord = lane % edge
    masks = (lane < edge, lane >= cells - edge, ycoord == 0, ycoord == edge - 1)
    shifts = (edge, cells - edge, 1, cells - 1)
    zlo = row == 0
    zhi = row == nz - 1

    def one(i, carry):
        b = g * GROUP + i
        th = scale_ref[b, 0]
        present = tissue_ref[i].astype(jnp.float32)
        c = jnp.cos(angle_ref[i].astype(jnp.float32))
        c2 = c * c
        scaled = present * th
        wx = scaled * (ACROSS + (ALONG - ACROSS) * c2)
        wy = scaled * (ACROSS + (ALONG - ACROSS) * (1.0 - c2))
        wz = scaled * VERTICAL
        u = u_ref[i]
        l = l_ref[i].astype(jnp.float32)
        halo = halo_ref[i]
        conds, ub, lb = [], [], []
        for f in range(4):
            face = face_ref[i, f]
            high = face.astype(jnp.bfloat16)
            rest = face - high.astype(jnp.float32)
            middle = rest.astype(jnp.bfloat16)
            low = (rest - middle.astype(jnp.float32)).astype(jnp.bfloat16)
            ext = jnp.dot(high, expand_ref[f], preferred_element_type=jnp.float32)
            ext = ext + jnp.dot(middle, expand_ref[f], preferred_element_type=jnp.float32)
            ext = ext + jnp.dot(low, expand_ref[f], preferred_element_type=jnp.float32)
            w_self = wx if f < 2 else wy
            w_near = jnp.where(masks[f], scale_ref[b, 1 + f] * ext[:nz], pltpu.roll(w_self, shifts[f], 1))
            conds.append(w_self * w_near)
            ub.append(jnp.where(masks[f], ext[nz:2 * nz], pltpu.roll(u, shifts[f], 1)))
            lb.append(jnp.where(masks[f], ext[2 * nz:3 * nz], pltpu.roll(l, shifts[f], 1)))
        wz_lo = jnp.where(zlo, (halo[0:1] * th) * VERTICAL, pltpu.roll(wz, 1, 0))
        wz_hi = jnp.where(zhi, (halo[3:4] * th) * VERTICAL, pltpu.roll(wz, nz - 1, 0))
        conds += [wz * wz_lo, wz * wz_hi]
        ub += [jnp.where(zlo, halo[1:2], pltpu.roll(u, 1, 0)), jnp.where(zhi, halo[4:5], pltpu.roll(u, nz - 1, 0))]
        lb += [jnp.where(zlo, halo[2:3], pltpu.roll(l, 1, 0)), jnp.where(zhi, halo[5:6], pltpu.roll(l, nz - 1, 0))]
        lap_u = conds[0] * (ub[0] - u)
        lap_l = conds[0] * (lb[0] - l)
        terms = lap_l * (ub[0] - u)
        for k in range(1, 6):
            step_u = ub[k] - u
            step_l = conds[k] * (lb[k] - l)
            lap_u = lap_u + conds[k] * step_u
            lap_l = lap_l + step_l
            terms = terms + step_l * step_u
        ionic = u * (1.0 - u) * (u - THRESHOLD)
        slope = -3.0 * u * u + 2.0 * (1.0 + THRESHOLD) * u - THRESHOLD
        u_out[i] = u + TIMESTEP * (lap_u + ionic)
        l_out[i] = l + TIMESTEP * (lap_l + slope * l)
        col = -jnp.sum(terms, axis=0, keepdims=True)
        acc = col[:, 0:128]
        for t in range(1, cells // 128):
            acc = acc + col[:, t * 128:(t + 1) * 128]
        part_out[i] = acc
        return carry

    lax.fori_loop(0, GROUP, one, 0)


def cell_step(scales, tissue, angle, potential, sensitivity, faces, halos, interpret=False):
    bricks, nz, cells = potential.shape
    edge = faces.shape[-1]
    expand = expanders(edge, cells).astype(jnp.bfloat16)
    blk3 = lambda: pl.BlockSpec((GROUP, nz, cells), lambda g: (g, 0, 0))
    return pl.pallas_call(
        cell_kernel,
        grid=(bricks // GROUP,),
        in_specs=[
            pl.BlockSpec(memory_space=pltpu.SMEM),
            pl.BlockSpec((4, edge, cells), lambda g: (0, 0, 0)),
            blk3(), blk3(), blk3(), blk3(),
            pl.BlockSpec((GROUP, 4, faces.shape[2], edge), lambda g: (g, 0, 0, 0)),
            pl.BlockSpec((GROUP, 6, cells), lambda g: (g, 0, 0)),
        ],
        out_specs=[blk3(), blk3(), pl.BlockSpec((GROUP, 1, 128), lambda g: (g, 0, 0))],
        out_shape=[
            jax.ShapeDtypeStruct((bricks, nz, cells), jnp.float32),
            jax.ShapeDtypeStruct((bricks, nz, cells), jnp.float32),
            jax.ShapeDtypeStruct((bricks, 1, 128), jnp.float32),
        ],
        compiler_params=pltpu.CompilerParams(dimension_semantics=("parallel",)),
        interpret=interpret,
    )(scales, expand, tissue, angle, potential, sensitivity, faces, halos)


def group_sum(values):
    col = jnp.sum(values, axis=0, keepdims=True)
    acc = col[:, 0:128]
    for t in range(1, values.shape[1] // 128):
        acc = acc + col[:, t * 128:(t + 1) * 128]
    return acc


def inner_kernel(tissue_ref, angle_ref, u_ref, l_ref, lu_out, ll_out, gx_out, part_out):
    nz, cells = u_ref.shape[1], u_ref.shape[2]
    edge = BX
    lane = lax.broadcasted_iota(jnp.int32, (nz, cells), 1)
    row = lax.broadcasted_iota(jnp.int32, (nz, cells), 0)
    ycoord = lane % edge
    inside = (lane >= edge, lane < cells - edge, ycoord != 0, ycoord != edge - 1, row != 0, row != nz - 1)
    shifts = ((edge, 1), (cells - edge, 1), (1, 1), (cells - 1, 1), (1, 0), (nz - 1, 0))

    def one(i, carry):
        present = tissue_ref[i].astype(jnp.float32)
        c = jnp.cos(angle_ref[i].astype(jnp.float32))
        c2 = c * c
        gx = present * (ACROSS + (ALONG - ACROSS) * c2)
        gy = present * (ACROSS + (ALONG - ACROSS) * (1.0 - c2))
        gz = present * VERTICAL
        u = u_ref[i]
        l = l_ref[i].astype(jnp.float32)
        lap_u = jnp.zeros_like(u)
        lap_l = jnp.zeros_like(u)
        terms = jnp.zeros_like(u)
        for k in range(6):
            g = gx if k < 2 else (gy if k < 4 else gz)
            shift, axis = shifts[k]
            conduct = jnp.where(inside[k], g * pltpu.roll(g, shift, axis), 0.0)
            step_u = pltpu.roll(u, shift, axis) - u
            step_l = conduct * (pltpu.roll(l, shift, axis) - l)
            lap_u = lap_u + conduct * step_u
            lap_l = lap_l + step_l
            terms = terms + step_l * step_u
        lu_out[i] = lap_u
        ll_out[i] = lap_l
        gx_out[i] = gx
        part_out[i] = group_sum(terms)
        return carry

    lax.fori_loop(0, GROUP, one, 0)


def outer_kernel(cond_ref, cell_ref, own_ref, near_ref, expand_ref, u_ref, l_ref, lu_ref, ll_ref, gx_ref, inner_ref, face_ref,
                 halo_ref, u_out, l_out, part_out, ext_ref):
    g = pl.program_id(0)
    nz, cells = u_ref.shape[1], u_ref.shape[2]
    edge = BX
    rows = 8 * nz
    for f in range(4):
        face = face_ref[:, f]
        part = face[:, :2 * nz]
        high = part.astype(jnp.bfloat16).astype(jnp.float32)
        rest = part - high
        middle = rest.astype(jnp.bfloat16).astype(jnp.float32)
        low = (rest - middle).astype(jnp.bfloat16).astype(jnp.float32)
        stacked = jnp.concatenate(
            [high, middle, low, face[:, 2 * nz:3 * nz], jnp.zeros_like(face[:, :nz])], axis=1
        )
        ext_ref[f] = jnp.dot(
            stacked.reshape(OUTER * rows, edge).astype(jnp.bfloat16),
            expand_ref[f],
            preferred_element_type=jnp.float32,
        )
    lane = lax.broadcasted_iota(jnp.int32, (nz, cells), 1)
    row = lax.broadcasted_iota(jnp.int32, (nz, cells), 0)
    ycoord = lane % edge
    masks = (lane < edge, lane >= cells - edge, ycoord == 0, ycoord == edge - 1)

    chunk = 256
    lane = lax.broadcasted_iota(jnp.int32, (nz, chunk), 1)
    row = lax.broadcasted_iota(jnp.int32, (nz, chunk), 0)
    ycoord = lane % edge

    def one(i, carry):
        b = g * OUTER + i
        th = cond_ref[own_ref[b]]
        near_th = [cond_ref[cell_ref[near_ref[4 * b + f]]] for f in range(4)]
        square = th * th
        base = pl.multiple_of(i * rows, rows)
        total = -square * inner_ref[i]
        for c in range(cells // chunk):
            cols = slice(c * chunk, (c + 1) * chunk)
            at = lane + c * chunk
            masks = (at < edge, at >= cells - edge, ycoord == 0, ycoord == edge - 1)
            u = u_ref[i, :, cols]
            l = l_ref[i, :, cols].astype(jnp.float32)
            gx = gx_ref[i, :, cols]
            gy = jnp.where(gx != 0.0, (ALONG + ACROSS) - gx, 0.0)
            halo = halo_ref[i, :, cols]
            edge_u, edge_l, edge_t = [], [], []
            for side, r in ((0, 0), (1, nz - 1)):
                own_z = (gx[r:r + 1] != 0.0).astype(jnp.float32) * VERTICAL
                conduct = own_z * (halo[3 * side:3 * side + 1] * VERTICAL)
                step_u = halo[3 * side + 1:3 * side + 2] - u[r:r + 1]
                step_l = conduct * (halo[3 * side + 2:3 * side + 3] - l[r:r + 1])
                edge_u.append(conduct * step_u)
                edge_l.append(step_l)
                edge_t.append(step_l * step_u)
            lap_u = lu_ref[i, :, cols] + jnp.where(row == 0, edge_u[0], 0.0) + jnp.where(row == nz - 1, edge_u[1], 0.0)
            lap_l = ll_ref[i, :, cols] + jnp.where(row == 0, edge_l[0], 0.0) + jnp.where(row == nz - 1, edge_l[1], 0.0)
            face_u = jnp.zeros_like(u)
            face_l = jnp.zeros_like(u)
            face_t = jnp.zeros_like(u)
            for f in range(4):
                piece = lambda k: ext_ref[f, pl.ds(base + k * nz, nz), cols]
                near_w = (piece(0) + piece(2)) + piece(4)
                near_u = (piece(1) + piece(3)) + piece(5)
                near_l = piece(6)
                g_self = gx if f < 2 else gy
                conduct = jnp.where(masks[f], near_th[f] * (g_self * near_w), 0.0)
                step_u = near_u - u
                step_l = conduct * (near_l - l)
                face_u = face_u + conduct * step_u
                face_l = face_l + step_l
                face_t = face_t + step_l * step_u
            ionic = u * (1.0 - u) * (u - THRESHOLD)
            slope = -3.0 * u * u + 2.0 * (1.0 + THRESHOLD) * u - THRESHOLD
            u_out[i, :, cols] = u + TIMESTEP * ((square * lap_u + th * face_u) + ionic)
            l_out[i, :, cols] = l + TIMESTEP * ((square * lap_l + th * face_l) + slope * l)
            total = total - (square * (group_sum(edge_t[0]) + group_sum(edge_t[1])) + th * group_sum(face_t))
        part_out[i] = total
        return carry

    lax.fori_loop(0, OUTER, one, 0)


def inner_step(tissue, angle, potential, sensitivity, interpret=False):
    bricks, nz, cells = potential.shape
    blk3 = lambda: pl.BlockSpec((GROUP, nz, cells), lambda g: (g, 0, 0))
    full = jax.ShapeDtypeStruct((bricks, nz, cells), jnp.float32)
    return pl.pallas_call(
        inner_kernel,
        grid=(bricks // GROUP,),
        in_specs=[blk3(), blk3(), blk3(), blk3()],
        out_specs=[blk3(), blk3(), blk3(), pl.BlockSpec((GROUP, 1, 128), lambda g: (g, 0, 0))],
        out_shape=[full, full, full, jax.ShapeDtypeStruct((bricks, 1, 128), jnp.float32)],
        compiler_params=pltpu.CompilerParams(dimension_semantics=("parallel",)),
        interpret=interpret,
    )(tissue, angle, potential, sensitivity)


def outer_step(tables, potential, sensitivity, inner, faces, halos, interpret=False):
    bricks, nz, cells = potential.shape
    edge = faces.shape[-1]
    expand = expanders(edge, cells).astype(jnp.bfloat16)
    blk3 = lambda: pl.BlockSpec((OUTER, nz, cells), lambda g: (g, 0, 0))
    lap_u, lap_l, gx, inner_part = inner
    return pl.pallas_call(
        outer_kernel,
        grid=(bricks // OUTER,),
        in_specs=[pl.BlockSpec(memory_space=pltpu.SMEM) for _ in tables] + [
            pl.BlockSpec((4, edge, cells), lambda g: (0, 0, 0)),
            blk3(), blk3(), blk3(), blk3(), blk3(),
            pl.BlockSpec((OUTER, 1, 128), lambda g: (g, 0, 0)),
            pl.BlockSpec((OUTER, 4, faces.shape[2], edge), lambda g: (g, 0, 0, 0)),
            pl.BlockSpec((OUTER, 6, cells), lambda g: (g, 0, 0)),
        ],
        out_specs=[blk3(), blk3(), pl.BlockSpec((OUTER, 1, 128), lambda g: (g, 0, 0))],
        out_shape=[
            jax.ShapeDtypeStruct((bricks, nz, cells), jnp.float32),
            jax.ShapeDtypeStruct((bricks, nz, cells), jnp.float32),
            jax.ShapeDtypeStruct((bricks, 1, 128), jnp.float32),
        ],
        scratch_shapes=[pltpu.VMEM((4, OUTER * 8 * nz, cells), jnp.float32)],
        compiler_params=pltpu.CompilerParams(dimension_semantics=("parallel",)),
        interpret=interpret,
    )(*tables, expand, potential, sensitivity, lap_u, lap_l, gx, inner_part, faces, halos)


def body(
    potential, fiber_angle, tissue, sensitivity, conductance, brick_slot, neighbours, brick_cell
):
    bricks, z_layers, plane_cells = potential.shape
    brick_edge = BX
    blocks = lax.axis_size("blk")
    parts = lax.axis_size("par")
    devices = blocks * parts
    capacity = max(4, 8 * bricks // blocks)
    face_count = 4 * bricks
    face_cells = z_layers * brick_edge
    own_cells = conductance.shape[0]
    cell_count = own_cells * devices
    opposite = jnp.array([1, 0, 3, 2], jnp.int32)

    near_slot = brick_slot[neighbours]
    near_blk = (near_slot // bricks).reshape(-1)
    far_key = (near_slot % bricks * 4 + opposite[None, :]).reshape(-1)
    own_key = jnp.arange(face_count, dtype=jnp.int32)
    matches = near_blk[:, None] == near_blk[None, :]
    send_rank = jnp.sum((matches & (own_key[None, :] < own_key[:, None])).astype(jnp.int32), axis=1)
    recv_rank = jnp.sum((matches & (far_key[None, :] < far_key[:, None])).astype(jnp.int32), axis=1)
    send_slot = near_blk * capacity + send_rank
    recv_slot = near_blk * capacity + recv_rank

    adjoint = sensitivity.astype(jnp.float32)
    inner = inner_step(tissue, fiber_angle, potential, sensitivity)
    picker = expanders(brick_edge, plane_cells).reshape(4 * brick_edge, plane_cells).T.astype(jnp.float32)

    def boundary(values):
        picked = jnp.dot(
            values.astype(jnp.float32).reshape(bricks * z_layers, plane_cells),
            picker,
            precision=lax.Precision.HIGHEST,
        )
        return picked.reshape(bricks, z_layers, 4, brick_edge).transpose(0, 2, 1, 3)

    tissue_faces = boundary(tissue)
    cos_faces = jnp.cos(boundary(fiber_angle)) ** 2
    factor_faces = jnp.concatenate(
        [
            ACROSS + (ALONG - ACROSS) * cos_faces[:, :2],
            ACROSS + (ALONG - ACROSS) * (1.0 - cos_faces[:, 2:]),
        ],
        axis=1,
    )
    fields = jnp.stack(
        [tissue_faces * factor_faces, boundary(potential), boundary(sensitivity)], axis=2
    )
    flattened = fields.reshape(face_count, 3 * face_cells)
    outgoing = jnp.zeros((blocks * capacity, 3 * face_cells), jnp.float32).at[send_slot].set(flattened)
    shifted = [conductance] + [
        lax.ppermute(conductance, "par", [(i, (i + s) % parts) for i in range(parts)])
        for s in range(1, parts)
    ]
    source = (lax.axis_index("par") - jnp.arange(parts, dtype=jnp.int32)) % parts
    extra = jnp.concatenate([jnp.stack(shifted)[source].reshape(-1), brick_cell.astype(jnp.float32)])
    width = capacity * 3 * face_cells
    extra_width = -(-extra.shape[0] // 128) * 128
    extra = jnp.pad(extra, (0, extra_width - extra.shape[0]))
    sending = jnp.concatenate(
        [outgoing.reshape(blocks, width), jnp.broadcast_to(extra[None], (blocks, extra_width))], axis=1
    )
    arrived = lax.all_to_all(sending, "blk", split_axis=0, concat_axis=0, tiled=True)
    received = arrived[:, :width]
    par_cells = own_cells * parts
    cond_all = arrived[:, width : width + par_cells].reshape(-1)
    cell_all = arrived[:, width + par_cells : width + par_cells + bricks].reshape(-1).astype(jnp.int32)
    faces = received.reshape(blocks * capacity, 3 * face_cells)[recv_slot].reshape(
        bricks, 4, 3 * z_layers, brick_edge
    )

    size = lax.axis_size("par")
    up = [(i, i + 1) for i in range(size - 1)]
    down = [(j, i) for i, j in up]
    last = jnp.stack([tissue[:, -1].astype(jnp.float32), potential[:, -1], adjoint[:, -1]], axis=1)
    initial = jnp.stack([tissue[:, 0].astype(jnp.float32), potential[:, 0], adjoint[:, 0]], axis=1)
    halos = jnp.concatenate([lax.ppermute(last, "par", up), lax.ppermute(initial, "par", down)], axis=1)

    tables = (cond_all, cell_all, brick_cell, near_slot.reshape(-1))
    final, adjoint, parts_out = outer_step(tables, potential, sensitivity, inner, faces, halos)
    brick_part = jnp.sum(parts_out, axis=(1, 2))
    onehot_cells = brick_cell[:, None] == jnp.arange(cell_count, dtype=jnp.int32)[None, :]
    shares = jnp.sum(jnp.where(onehot_cells, brick_part[:, None], 0.0), axis=0)
    grad_share = jnp.sum(
        lax.all_to_all(
            shares.reshape(devices, own_cells), ("blk", "par"), split_axis=0, concat_axis=0, tiled=True
        ),
        axis=0,
    )
    cell_gradient = TIMESTEP * grad_share / (conductance * float(BX) ** 1.5)
    return (final, adjoint, cell_gradient)


def solution(mesh):
    placed = (
        P("blk", "par", None),
        P("blk", "par", None),
        P("blk", "par", None),
        P("blk", "par", None),
        P(("blk", "par")),
        P(),
        P("blk", None),
        P("blk"),
    )
    return jax.shard_map(
        body,
        mesh=mesh,
        in_specs=placed,
        out_specs=(P("blk", "par", None), P("blk", "par", None), P(("blk", "par"))),
        check_vma=False,
    )
```

```python
import jax
import jax.numpy as jnp
from jax import lax
from jax.sharding import PartitionSpec as P
from jax.experimental import pallas as pl
from jax.experimental.pallas import tpu as pltpu

BX = 32
STEPS = 1


TIMESTEP = 0.12
THRESHOLD = 0.2
ACROSS = 0.3
ALONG = 1.0
VERTICAL = 0.6


def extended(x, sides, width):
    for axis, dim in sides:
        size, length = (lax.axis_size(axis), x.shape[dim])
        up = [(i, (i + 1) % size) for i in range(size - 1)]
        down = [(j, i) for i, j in up]
        last = lax.slice_in_dim(x, length - width, length, axis=dim)
        initial = lax.slice_in_dim(x, 0, width, axis=dim)
        before = lax.ppermute(last, axis, up)
        after = lax.ppermute(initial, axis, down)
        x = jnp.concatenate([before, x, after], axis=dim)
    return x


def layers(values, brick_edge):
    return jnp.stack(
        [
            values[..., :brick_edge],
            values[..., -brick_edge:],
            values[..., 0::brick_edge],
            values[..., brick_edge - 1 :: brick_edge],
        ],
        axis=1,
    )


def along_x(values, lower_face, upper_face, brick_edge):
    return (
        jnp.concatenate([lower_face, values[..., :-brick_edge]], -1),
        jnp.concatenate([values[..., brick_edge:], upper_face], -1),
    )


def along_y(values, lower_face, upper_face, brick_edge):
    y_index = jnp.arange(values.shape[-1]) % brick_edge
    zero_pad = jnp.zeros(values.shape[:-1] + (1,), values.dtype)
    shifted_down = jnp.concatenate([zero_pad, values[..., :-1]], -1)
    shifted_up = jnp.concatenate([values[..., 1:], zero_pad], -1)
    return (
        jnp.where(y_index == 0, jnp.repeat(lower_face, brick_edge, axis=-1), shifted_down),
        jnp.where(
            y_index == brick_edge - 1, jnp.repeat(upper_face, brick_edge, axis=-1), shifted_up
        ),
    )


def near_values(values, layer_set, padded, brick_edge):
    x_low, x_high = along_x(values, layer_set[:, 0], layer_set[:, 1], brick_edge)
    y_low, y_high = along_y(values, layer_set[:, 2], layer_set[:, 3], brick_edge)
    return (x_low, x_high, y_low, y_high, padded[:, :-2], padded[:, 2:])


def laplace(conduct, values, beside):
    summed = conduct[0] * (beside[0] - values)
    for facet in range(1, 6):
        summed = summed + conduct[facet] * (beside[facet] - values)
    return summed


def brick_terms(conduct, adjoint, beside_adjoint, earlier, beside_state):
    summed = -conduct[0] * (adjoint - beside_adjoint[0]) * (earlier - beside_state[0])
    for facet in range(1, 6):
        summed = summed - conduct[facet] * (adjoint - beside_adjoint[facet]) * (
            earlier - beside_state[facet]
        )
    return jnp.sum(summed, axis=(1, 2))


def weights(tissue, fiber_angle, brick_scale):
    present = tissue.astype(jnp.float32)
    cos_square = jnp.cos(fiber_angle.astype(jnp.float32)) ** 2
    weight_x = present * brick_scale * (ACROSS + (ALONG - ACROSS) * cos_square)
    weight_y = present * brick_scale * (ACROSS + (ALONG - ACROSS) * (1.0 - cos_square))
    weight_z = present * brick_scale * VERTICAL
    return (weight_x, weight_y, weight_z)


def conductances(weight_x, weight_y, weight_z, weight_near, padded_z, brick_edge):
    x_low, x_high = along_x(weight_x, weight_near[:, 0], weight_near[:, 1], brick_edge)
    y_low, y_high = along_y(weight_y, weight_near[:, 2], weight_near[:, 3], brick_edge)
    return (
        weight_x * x_low,
        weight_x * x_high,
        weight_y * y_low,
        weight_y * y_high,
        weight_z * padded_z[:, :-2],
        weight_z * padded_z[:, 2:],
    )


GROUP = 8
OUTER = 16


def expanders(edge, cells):
    lane = jnp.arange(cells, dtype=jnp.int32)[None, :]
    k = jnp.arange(edge, dtype=jnp.int32)[:, None]
    return jnp.stack(
        [lane == k, lane == cells - edge + k, lane == edge * k, lane == edge * k + edge - 1]
    )


def cell_kernel(scale_ref, expand_ref, tissue_ref, angle_ref, u_ref, l_ref, face_ref, halo_ref,
                u_out, l_out, part_out):
    g = pl.program_id(0)
    nz, cells = u_ref.shape[1], u_ref.shape[2]
    edge = face_ref.shape[-1]
    lane = lax.broadcasted_iota(jnp.int32, (nz, cells), 1)
    row = lax.broadcasted_iota(jnp.int32, (nz, cells), 0)
    ycoord = lane % edge
    masks = (lane < edge, lane >= cells - edge, ycoord == 0, ycoord == edge - 1)
    shifts = (edge, cells - edge, 1, cells - 1)
    zlo = row == 0
    zhi = row == nz - 1

    def one(i, carry):
        b = g * GROUP + i
        th = scale_ref[b, 0]
        present = tissue_ref[i].astype(jnp.float32)
        c = jnp.cos(angle_ref[i].astype(jnp.float32))
        c2 = c * c
        scaled = present * th
        wx = scaled * (ACROSS + (ALONG - ACROSS) * c2)
        wy = scaled * (ACROSS + (ALONG - ACROSS) * (1.0 - c2))
        wz = scaled * VERTICAL
        u = u_ref[i]
        l = l_ref[i].astype(jnp.float32)
        halo = halo_ref[i]
        conds, ub, lb = [], [], []
        for f in range(4):
            face = face_ref[i, f]
            high = face.astype(jnp.bfloat16)
            rest = face - high.astype(jnp.float32)
            middle = rest.astype(jnp.bfloat16)
            low = (rest - middle.astype(jnp.float32)).astype(jnp.bfloat16)
            ext = jnp.dot(high, expand_ref[f], preferred_element_type=jnp.float32)
            ext = ext + jnp.dot(middle, expand_ref[f], preferred_element_type=jnp.float32)
            ext = ext + jnp.dot(low, expand_ref[f], preferred_element_type=jnp.float32)
            w_self = wx if f < 2 else wy
            w_near = jnp.where(masks[f], scale_ref[b, 1 + f] * ext[:nz], pltpu.roll(w_self, shifts[f], 1))
            conds.append(w_self * w_near)
            ub.append(jnp.where(masks[f], ext[nz:2 * nz], pltpu.roll(u, shifts[f], 1)))
            lb.append(jnp.where(masks[f], ext[2 * nz:3 * nz], pltpu.roll(l, shifts[f], 1)))
        wz_lo = jnp.where(zlo, (halo[0:1] * th) * VERTICAL, pltpu.roll(wz, 1, 0))
        wz_hi = jnp.where(zhi, (halo[3:4] * th) * VERTICAL, pltpu.roll(wz, nz - 1, 0))
        conds += [wz * wz_lo, wz * wz_hi]
        ub += [jnp.where(zlo, halo[1:2], pltpu.roll(u, 1, 0)), jnp.where(zhi, halo[4:5], pltpu.roll(u, nz - 1, 0))]
        lb += [jnp.where(zlo, halo[2:3], pltpu.roll(l, 1, 0)), jnp.where(zhi, halo[5:6], pltpu.roll(l, nz - 1, 0))]
        lap_u = conds[0] * (ub[0] - u)
        lap_l = conds[0] * (lb[0] - l)
        terms = lap_l * (ub[0] - u)
        for k in range(1, 6):
            step_u = ub[k] - u
            step_l = conds[k] * (lb[k] - l)
            lap_u = lap_u + conds[k] * step_u
            lap_l = lap_l + step_l
            terms = terms + step_l * step_u
        ionic = u * (1.0 - u) * (u - THRESHOLD)
        slope = -3.0 * u * u + 2.0 * (1.0 + THRESHOLD) * u - THRESHOLD
        u_out[i] = u + TIMESTEP * (lap_u + ionic)
        l_out[i] = l + TIMESTEP * (lap_l + slope * l)
        col = -jnp.sum(terms, axis=0, keepdims=True)
        acc = col[:, 0:128]
        for t in range(1, cells // 128):
            acc = acc + col[:, t * 128:(t + 1) * 128]
        part_out[i] = acc
        return carry

    lax.fori_loop(0, GROUP, one, 0)


def cell_step(scales, tissue, angle, potential, sensitivity, faces, halos, interpret=False):
    bricks, nz, cells = potential.shape
    edge = faces.shape[-1]
    expand = expanders(edge, cells).astype(jnp.bfloat16)
    blk3 = lambda: pl.BlockSpec((GROUP, nz, cells), lambda g: (g, 0, 0))
    return pl.pallas_call(
        cell_kernel,
        grid=(bricks // GROUP,),
        in_specs=[
            pl.BlockSpec(memory_space=pltpu.SMEM),
            pl.BlockSpec((4, edge, cells), lambda g: (0, 0, 0)),
            blk3(), blk3(), blk3(), blk3(),
            pl.BlockSpec((GROUP, 4, faces.shape[2], edge), lambda g: (g, 0, 0, 0)),
            pl.BlockSpec((GROUP, 6, cells), lambda g: (g, 0, 0)),
        ],
        out_specs=[blk3(), blk3(), pl.BlockSpec((GROUP, 1, 128), lambda g: (g, 0, 0))],
        out_shape=[
            jax.ShapeDtypeStruct((bricks, nz, cells), jnp.float32),
            jax.ShapeDtypeStruct((bricks, nz, cells), jnp.float32),
            jax.ShapeDtypeStruct((bricks, 1, 128), jnp.float32),
        ],
        compiler_params=pltpu.CompilerParams(dimension_semantics=("parallel",)),
        interpret=interpret,
    )(scales, expand, tissue, angle, potential, sensitivity, faces, halos)


def group_sum(values):
    col = jnp.sum(values, axis=0, keepdims=True)
    acc = col[:, 0:128]
    for t in range(1, values.shape[1] // 128):
        acc = acc + col[:, t * 128:(t + 1) * 128]
    return acc


def inner_kernel(tissue_ref, angle_ref, u_ref, l_ref, lu_out, ll_out, gx_out, part_out):
    nz, cells = u_ref.shape[1], u_ref.shape[2]
    edge = BX
    lane = lax.broadcasted_iota(jnp.int32, (nz, cells), 1)
    row = lax.broadcasted_iota(jnp.int32, (nz, cells), 0)
    ycoord = lane % edge
    inside = (lane >= edge, lane < cells - edge, ycoord != 0, ycoord != edge - 1, row != 0, row != nz - 1)
    shifts = ((edge, 1), (cells - edge, 1), (1, 1), (cells - 1, 1), (1, 0), (nz - 1, 0))

    def one(i, carry):
        present = tissue_ref[i].astype(jnp.float32)
        c = jnp.cos(angle_ref[i].astype(jnp.float32))
        c2 = c * c
        gx = present * (ACROSS + (ALONG - ACROSS) * c2)
        gy = present * (ACROSS + (ALONG - ACROSS) * (1.0 - c2))
        gz = present * VERTICAL
        u = u_ref[i]
        l = l_ref[i].astype(jnp.float32)
        lap_u = jnp.zeros_like(u)
        lap_l = jnp.zeros_like(u)
        terms = jnp.zeros_like(u)
        for k in range(6):
            g = gx if k < 2 else (gy if k < 4 else gz)
            shift, axis = shifts[k]
            conduct = jnp.where(inside[k], g * pltpu.roll(g, shift, axis), 0.0)
            step_u = pltpu.roll(u, shift, axis) - u
            step_l = conduct * (pltpu.roll(l, shift, axis) - l)
            lap_u = lap_u + conduct * step_u
            lap_l = lap_l + step_l
            terms = terms + step_l * step_u
        lu_out[i] = lap_u
        ll_out[i] = lap_l
        gx_out[i] = gx
        part_out[i] = group_sum(terms)
        return carry

    lax.fori_loop(0, GROUP, one, 0)


def outer_kernel(cond_ref, cell_ref, own_ref, near_ref, expand_ref, u_ref, l_ref, lu_ref, ll_ref, gx_ref, inner_ref, face_ref,
                 halo_ref, u_out, l_out, part_out, ext_ref):
    g = pl.program_id(0)
    nz, cells = u_ref.shape[1], u_ref.shape[2]
    edge = BX
    rows = 8 * nz
    for f in range(4):
        face = face_ref[:, f]
        part = face[:, :2 * nz]
        high = part.astype(jnp.bfloat16).astype(jnp.float32)
        rest = part - high
        middle = rest.astype(jnp.bfloat16).astype(jnp.float32)
        low = (rest - middle).astype(jnp.bfloat16).astype(jnp.float32)
        stacked = jnp.concatenate(
            [high, middle, low, face[:, 2 * nz:3 * nz], jnp.zeros_like(face[:, :nz])], axis=1
        )
        ext_ref[f] = jnp.dot(
            stacked.reshape(OUTER * rows, edge).astype(jnp.bfloat16),
            expand_ref[f],
            preferred_element_type=jnp.float32,
        )
    lane = lax.broadcasted_iota(jnp.int32, (nz, cells), 1)
    row = lax.broadcasted_iota(jnp.int32, (nz, cells), 0)
    ycoord = lane % edge
    masks = (lane < edge, lane >= cells - edge, ycoord == 0, ycoord == edge - 1)

    chunk = 256
    lane = lax.broadcasted_iota(jnp.int32, (nz, chunk), 1)
    row = lax.broadcasted_iota(jnp.int32, (nz, chunk), 0)
    ycoord = lane % edge

    def one(i, carry):
        b = g * OUTER + i
        th = cond_ref[own_ref[b]]
        near_th = [cond_ref[cell_ref[near_ref[4 * b + f]]] for f in range(4)]
        square = th * th
        base = pl.multiple_of(i * rows, rows)
        total = -square * inner_ref[i]
        for c in range(cells // chunk):
            cols = slice(c * chunk, (c + 1) * chunk)
            at = lane + c * chunk
            masks = (at < edge, at >= cells - edge, ycoord == 0, ycoord == edge - 1)
            u = u_ref[i, :, cols]
            l = l_ref[i, :, cols].astype(jnp.float32)
            gx = gx_ref[i, :, cols]
            gy = jnp.where(gx != 0.0, (ALONG + ACROSS) - gx, 0.0)
            halo = halo_ref[i, :, cols]
            edge_u, edge_l, edge_t = [], [], []
            for side, r in ((0, 0), (1, nz - 1)):
                own_z = (gx[r:r + 1] != 0.0).astype(jnp.float32) * VERTICAL
                conduct = own_z * (halo[3 * side:3 * side + 1] * VERTICAL)
                step_u = halo[3 * side + 1:3 * side + 2] - u[r:r + 1]
                step_l = conduct * (halo[3 * side + 2:3 * side + 3] - l[r:r + 1])
                edge_u.append(conduct * step_u)
                edge_l.append(step_l)
                edge_t.append(step_l * step_u)
            lap_u = lu_ref[i, :, cols] + jnp.where(row == 0, edge_u[0], 0.0) + jnp.where(row == nz - 1, edge_u[1], 0.0)
            lap_l = ll_ref[i, :, cols] + jnp.where(row == 0, edge_l[0], 0.0) + jnp.where(row == nz - 1, edge_l[1], 0.0)
            face_u = jnp.zeros_like(u)
            face_l = jnp.zeros_like(u)
            face_t = jnp.zeros_like(u)
            for f in range(4):
                piece = lambda k: ext_ref[f, pl.ds(base + k * nz, nz), cols]
                near_w = (piece(0) + piece(2)) + piece(4)
                near_u = (piece(1) + piece(3)) + piece(5)
                near_l = piece(6)
                g_self = gx if f < 2 else gy
                conduct = jnp.where(masks[f], near_th[f] * (g_self * near_w), 0.0)
                step_u = near_u - u
                step_l = conduct * (near_l - l)
                face_u = face_u + conduct * step_u
                face_l = face_l + step_l
                face_t = face_t + step_l * step_u
            ionic = u * (1.0 - u) * (u - THRESHOLD)
            slope = -3.0 * u * u + 2.0 * (1.0 + THRESHOLD) * u - THRESHOLD
            u_out[i, :, cols] = u + TIMESTEP * ((square * lap_u + th * face_u) + ionic)
            l_out[i, :, cols] = l + TIMESTEP * ((square * lap_l + th * face_l) + slope * l)
            total = total - (square * (group_sum(edge_t[0]) + group_sum(edge_t[1])) + th * group_sum(face_t))
        part_out[i] = total
        return carry

    lax.fori_loop(0, OUTER, one, 0)


def inner_step(tissue, angle, potential, sensitivity, interpret=False):
    bricks, nz, cells = potential.shape
    blk3 = lambda: pl.BlockSpec((GROUP, nz, cells), lambda g: (g, 0, 0))
    full = jax.ShapeDtypeStruct((bricks, nz, cells), jnp.float32)
    return pl.pallas_call(
        inner_kernel,
        grid=(bricks // GROUP,),
        in_specs=[blk3(), blk3(), blk3(), blk3()],
        out_specs=[blk3(), blk3(), blk3(), pl.BlockSpec((GROUP, 1, 128), lambda g: (g, 0, 0))],
        out_shape=[full, full, full, jax.ShapeDtypeStruct((bricks, 1, 128), jnp.float32)],
        compiler_params=pltpu.CompilerParams(dimension_semantics=("parallel",)),
        interpret=interpret,
    )(tissue, angle, potential, sensitivity)


def outer_step(tables, potential, sensitivity, inner, faces, halos, interpret=False):
    bricks, nz, cells = potential.shape
    edge = faces.shape[-1]
    expand = expanders(edge, cells).astype(jnp.bfloat16)
    blk3 = lambda: pl.BlockSpec((OUTER, nz, cells), lambda g: (g, 0, 0))
    lap_u, lap_l, gx, inner_part = inner
    return pl.pallas_call(
        outer_kernel,
        grid=(bricks // OUTER,),
        in_specs=[pl.BlockSpec(memory_space=pltpu.SMEM) for _ in tables] + [
            pl.BlockSpec((4, edge, cells), lambda g: (0, 0, 0)),
            blk3(), blk3(), blk3(), blk3(), blk3(),
            pl.BlockSpec((OUTER, 1, 128), lambda g: (g, 0, 0)),
            pl.BlockSpec((OUTER, 4, faces.shape[2], edge), lambda g: (g, 0, 0, 0)),
            pl.BlockSpec((OUTER, 6, cells), lambda g: (g, 0, 0)),
        ],
        out_specs=[blk3(), blk3(), pl.BlockSpec((OUTER, 1, 128), lambda g: (g, 0, 0))],
        out_shape=[
            jax.ShapeDtypeStruct((bricks, nz, cells), jnp.float32),
            jax.ShapeDtypeStruct((bricks, nz, cells), jnp.float32),
            jax.ShapeDtypeStruct((bricks, 1, 128), jnp.float32),
        ],
        scratch_shapes=[pltpu.VMEM((4, OUTER * 8 * nz, cells), jnp.float32)],
        compiler_params=pltpu.CompilerParams(dimension_semantics=("parallel",)),
        interpret=interpret,
    )(*tables, expand, potential, sensitivity, lap_u, lap_l, gx, inner_part, faces, halos)


def body(
    potential, fiber_angle, tissue, sensitivity, conductance, brick_slot, neighbours, brick_cell
):
    bricks, z_layers, plane_cells = potential.shape
    brick_edge = BX
    blocks = lax.axis_size("blk")
    parts = lax.axis_size("par")
    devices = blocks * parts
    capacity = max(4, 8 * bricks // blocks)
    face_count = 4 * bricks
    face_cells = z_layers * brick_edge
    own_cells = conductance.shape[0]
    cell_count = own_cells * devices
    opposite = jnp.array([1, 0, 3, 2], jnp.int32)

    near_slot = brick_slot[neighbours]
    near_blk = (near_slot // bricks).reshape(-1)
    far_key = (near_slot % bricks * 4 + opposite[None, :]).reshape(-1)
    own_key = jnp.arange(face_count, dtype=jnp.int32)
    matches = near_blk[:, None] == near_blk[None, :]
    send_rank = jnp.sum((matches & (own_key[None, :] < own_key[:, None])).astype(jnp.int32), axis=1)
    recv_rank = jnp.sum((matches & (far_key[None, :] < far_key[:, None])).astype(jnp.int32), axis=1)
    send_slot = near_blk * capacity + send_rank
    recv_slot = near_blk * capacity + recv_rank

    adjoint = sensitivity.astype(jnp.float32)
    inner = inner_step(tissue, fiber_angle, potential, sensitivity)
    picker = expanders(brick_edge, plane_cells).reshape(4 * brick_edge, plane_cells).T.astype(jnp.float32)

    def boundary(values):
        picked = jnp.dot(
            values.astype(jnp.float32).reshape(bricks * z_layers, plane_cells),
            picker,
            precision=lax.Precision.HIGHEST,
        )
        return picked.reshape(bricks, z_layers, 4, brick_edge).transpose(0, 2, 1, 3)

    tissue_faces = boundary(tissue)
    cos_faces = jnp.cos(boundary(fiber_angle)) ** 2
    factor_faces = jnp.concatenate(
        [
            ACROSS + (ALONG - ACROSS) * cos_faces[:, :2],
            ACROSS + (ALONG - ACROSS) * (1.0 - cos_faces[:, 2:]),
        ],
        axis=1,
    )
    fields = jnp.stack(
        [tissue_faces * factor_faces, boundary(potential), boundary(sensitivity)], axis=2
    )
    flattened = fields.reshape(face_count, 3 * face_cells)
    outgoing = jnp.zeros((blocks * capacity, 3 * face_cells), jnp.float32).at[send_slot].set(flattened)
    shifted = [conductance] + [
        lax.ppermute(conductance, "par", [(i, (i + s) % parts) for i in range(parts)])
        for s in range(1, parts)
    ]
    source = (lax.axis_index("par") - jnp.arange(parts, dtype=jnp.int32)) % parts
    extra = jnp.concatenate([jnp.stack(shifted)[source].reshape(-1), brick_cell.astype(jnp.float32)])
    width = capacity * 3 * face_cells
    extra_width = -(-extra.shape[0] // 128) * 128
    extra = jnp.pad(extra, (0, extra_width - extra.shape[0]))
    sending = jnp.concatenate(
        [outgoing.reshape(blocks, width), jnp.broadcast_to(extra[None], (blocks, extra_width))], axis=1
    )
    arrived = lax.all_to_all(sending, "blk", split_axis=0, concat_axis=0, tiled=True)
    received = arrived[:, :width]
    par_cells = own_cells * parts
    cond_all = arrived[:, width : width + par_cells].reshape(-1)
    cell_all = arrived[:, width + par_cells : width + par_cells + bricks].reshape(-1).astype(jnp.int32)
    faces = received.reshape(blocks * capacity, 3 * face_cells)[recv_slot].reshape(
        bricks, 4, 3 * z_layers, brick_edge
    )

    size = lax.axis_size("par")
    up = [(i, i + 1) for i in range(size - 1)]
    down = [(j, i) for i, j in up]
    last = jnp.stack([tissue[:, -1].astype(jnp.float32), potential[:, -1], adjoint[:, -1]], axis=1)
    initial = jnp.stack([tissue[:, 0].astype(jnp.float32), potential[:, 0], adjoint[:, 0]], axis=1)
    halos = jnp.concatenate([lax.ppermute(last, "par", up), lax.ppermute(initial, "par", down)], axis=1)

    tables = (cond_all, cell_all, brick_cell, near_slot.reshape(-1))
    final, adjoint, parts_out = outer_step(tables, potential, sensitivity, inner, faces, halos)
    brick_part = jnp.sum(parts_out, axis=(1, 2))
    onehot_cells = brick_cell[:, None] == jnp.arange(cell_count, dtype=jnp.int32)[None, :]
    shares = jnp.sum(jnp.where(onehot_cells, brick_part[:, None], 0.0), axis=0)
    grad_share = jnp.sum(
        lax.all_to_all(
            shares.reshape(devices, own_cells), ("blk", "par"), split_axis=0, concat_axis=0, tiled=True
        ),
        axis=0,
    )
    cell_gradient = TIMESTEP * grad_share / (conductance * float(BX) ** 1.5)
    return (final, adjoint, cell_gradient)


def solution(mesh):
    placed = (
        P("blk", "par", None),
        P("blk", "par", None),
        P("blk", "par", None),
        P("blk", "par", None),
        P(("blk", "par")),
        P(),
        P("blk", None),
        P("blk"),
    )
    return jax.shard_map(
        body,
        mesh=mesh,
        in_specs=placed,
        out_specs=(P("blk", "par", None), P("blk", "par", None), P(("blk", "par"))),
        check_vma=False,
    )
```
